32 devices in a mesh: blk: 8 (over z, x), gz: 4 (over y, core).
Axes of the slice: x: 2, y: 2, z: 4, core: 2. Of those that a mesh axis runs over, the one named last changes fastest.
Arguments:
- fixed: bfloat16 [8, 32, 32, 128], P('blk', 'gz'), may hold values from -6 to 6
- moving: bfloat16 [8, 32, 32, 128], P('blk', 'gz'), may hold values from -6 to 6
- block_place: int32 [8], P('blk'), may hold values from 0 to 7, each once
- tissue: int32 [8], P('blk'), may hold values 0 or 1
Outputs:
- velocity: float32 [3, 2, 2, 64], replicated
- cc_map: float32 [8, 32, 32, 128], P('blk', 'gz')
The draws below stay inside these ranges and needn't reach their ends.
Inputs may be any that keep to these rules, and one draw needn't show every extreme that they name: `block_place`: each block position from 0 to 7 is named by exactly one block.
All inputs are finite; a program needn't handle non-finite values. No bound on the sum of `tissue` on one device may be relied on, other than what follows from the above.
Results may differ from the reference program's by a relative error of at most 0.0004.
Values may be sent and summed in bfloat16 or wider, within the bound.
No kernel may reach another device: no remote copies, remote signals or barrier semaphores. Data moves between devices by JAX's collectives and lax.ppermute only.
A program may use at most 64 MiB of HBM per device.

```python
import math
import jax
import jax.numpy as jnp
from jax import lax

BX = 32
BY = 128
SCALE = 16
GY = 8
ITERS = 2
BLOCKS = 8
GX = 1
NZ = 32
CZD = 2
CX = 2
CY = 8


def with_ends(result, own_key, smallest, high):
    shape = result.shape
    spot = [jax.random.randint(jax.random.fold_in(own_key, axis), (), 0, shape[axis]) for axis in range(len(shape))]
    result = result.at[tuple(spot)].set(smallest)
    longest = shape.index(max(shape))
    spot[longest] = (spot[longest] + 1) % shape[longest]
    return result.at[tuple(spot)].set(high)


def shard_levels(key, extent, shards, least, high):
    factor_of = 1.0
    for dim, shards_of in shards:
        draws = jax.random.uniform(jax.random.fold_in(jax.random.fold_in(key, 6), dim), (shards_of,), jnp.float32, least / len(shards), high / len(shards))
        factor_of = factor_of * jnp.repeat(jnp.exp(draws), extent[dim] // shards_of).reshape((-1,) + (1,) * (len(extent) - 1 - dim))
    return factor_of


def gaussian(rng, dims, scale, bound, cuts=(), held_as=jnp.bfloat16):
    loudness = shard_levels(rng, dims, cuts, -0.22, 0.18) if cuts else 1.0
    drawn = jax.random.normal(rng, dims, jnp.float32) * scale * loudness
    return jnp.minimum(jnp.maximum(drawn, -bound), bound).astype(held_as)


def setup_inputs(seed: int = 0) -> dict:
    keys = jax.random.split(jax.random.key(seed), 5)
    return {
        "fixed": gaussian(keys[0], (BLOCKS, NZ, BX, BY), 1.0, 6.0, ((0, 8), (1, 4))),
        "moving": gaussian(keys[1], (BLOCKS, NZ, BX, BY), 1.0, 6.0, ((0, 8), (1, 4))),
        "block_place": jax.random.permutation(keys[2], BLOCKS).astype(jnp.int32),
        "tissue": with_ends((jax.random.randint(keys[3], (BLOCKS,), 0, 5) < 3).astype(jnp.int32), jax.random.fold_in(keys[3], 1), 0, 1),
    }


EXACT = lax.Precision.HIGHEST
EPSILON = 1e-05
STEP_LENGTH = 0.5
BOX_TAPS = [1.0 / 9.0] * 9
GAUSS_RAW = [math.exp(-(offset - 3) ** 2 / 4.5) for offset in range(7)]
GAUSS_TAPS = [value / sum(GAUSS_RAW) for value in GAUSS_RAW]

def tap_matrix(count, taps):
    radius = len(taps) // 2
    rows = jnp.arange(count)[:, None]
    cols = jnp.arange(count)[None, :]
    matrix = jnp.zeros((count, count), jnp.float32)
    for offset, weight in enumerate(taps):
        matrix = matrix + weight * (rows - cols == offset - radius).astype(jnp.float32)
    return matrix

def along_rows(field, matrix):
    return jnp.einsum('...xy,xu->...uy', field, matrix, precision=EXACT)

def along_cols(field, matrix):
    return jnp.einsum('...y,yv->...v', field, matrix, precision=EXACT)

def planes_filter(field, taps, count):
    total = jnp.zeros(field.shape[:-3] + (count,) + field.shape[-2:], jnp.float32)
    for offset, weight in enumerate(taps):
        total = total + weight * field[..., offset:offset + count, :, :]
    return total

def slope(field, axis):
    widths = [(0, 0)] * field.ndim
    widths[axis] = (1, 1)
    padded = jnp.pad(field, widths)
    length = field.shape[axis]
    upper = lax.slice_in_dim(padded, 2, length + 2, axis=axis)
    lower = lax.slice_in_dim(padded, 0, length, axis=axis)
    return 0.5 * (upper - lower)

def hat_rows(coords, count):
    where = jnp.clip((coords + 0.5) / SCALE - 0.5, 0.0, count - 1.0)
    marks = jnp.arange(count).astype(jnp.float32)
    return jnp.maximum(0.0, 1.0 - jnp.abs(where[..., None] - marks))

def statistics(means, fixed_c, warped_c):
    sii = means[2] - means[0] * means[0]
    sww = means[3] - means[1] * means[1]
    siw = means[4] - means[0] * means[1]
    denom = sii * sww + EPSILON
    similar = siw * siw / denom
    weight = 2.0 * siw / denom * (fixed_c - means[0] - siw / (sww + EPSILON) * (warped_c - means[1]))
    return (similar, weight)

def smooth_axis(field, axis):
    widths = [(0, 0)] * field.ndim
    widths[axis] = (1, 1)
    padded = jnp.pad(field, widths)
    length = field.shape[axis]
    upper = lax.slice_in_dim(padded, 2, length + 2, axis=axis)
    lower = lax.slice_in_dim(padded, 0, length, axis=axis)
    return 0.25 * lower + 0.5 * field + 0.25 * upper

def regularize(velocity, total, coarse_rows, coarse_cols):
    block_rows = velocity.shape[2] // coarse_rows
    coarse_depth = velocity.shape[1]
    grid = total.reshape(block_rows, GY, 3, coarse_depth, coarse_rows, coarse_cols)
    grid = grid.transpose(2, 3, 0, 4, 1, 5).reshape(velocity.shape)
    regular = smooth_axis(smooth_axis(smooth_axis(grid, 1), 2), 3)
    return velocity + STEP_LENGTH * regular / jnp.sqrt(jnp.mean(regular * regular) + EPSILON)

def block_step(fixed_b, moving_b, place_b, tissue_b, velocity, box_rows, box_cols, gauss_rows, gauss_cols):
    image_i = fixed_b.astype(jnp.float32)
    image_j = moving_b.astype(jnp.float32)
    block_row = place_b // GY
    block_col = place_b % GY
    row_hat = hat_rows((block_row * BX + jnp.arange(BX)).astype(jnp.float32), GX * CX)
    col_hat = hat_rows((block_col * BY + jnp.arange(BY)).astype(jnp.float32), GY * CY)
    depth_hat = hat_rows(jnp.arange(NZ).astype(jnp.float32), CZD)
    partial_value = jnp.einsum('ckab,xa->ckxb', velocity, row_hat, precision=EXACT)
    partial_value = jnp.einsum('ckxb,yb->ckxy', partial_value, col_hat, precision=EXACT)
    shift = jnp.einsum('zk,ckxy->czxy', depth_hat, partial_value, precision=EXACT)
    warped = image_j + shift[0] * slope(image_j, 0) + shift[1] * slope(image_j, 1) + shift[2] * slope(image_j, 2)
    fields = jnp.stack([image_i, warped, image_i * image_i, warped * warped, image_i * warped], 0)
    padded = jnp.pad(fields, ((0, 0), (4, 4), (0, 0), (0, 0)))
    means = planes_filter(padded, BOX_TAPS, NZ)
    means = along_cols(along_rows(means, box_rows), box_cols)
    similar, weight = statistics(means, image_i, warped)
    scale = weight * tissue_b.astype(jnp.float32)
    force = jnp.stack([scale * slope(warped, 0), scale * slope(warped, 1), scale * slope(warped, 2)], 0)
    padded = jnp.pad(force, ((0, 0), (3, 3), (0, 0), (0, 0)))
    smooth = planes_filter(padded, GAUSS_TAPS, NZ)
    smooth = along_cols(along_rows(smooth, gauss_rows), gauss_cols)
    piece = smooth.reshape(3, CZD, SCALE, CX, SCALE, CY, SCALE).sum(axis=(2, 4, 6))
    return (piece, similar)

def reference(fixed, moving, block_place, tissue):
    box_rows = tap_matrix(BX, BOX_TAPS)
    box_cols = tap_matrix(BY, BOX_TAPS)
    gauss_rows = tap_matrix(BX, GAUSS_TAPS)
    gauss_cols = tap_matrix(BY, GAUSS_TAPS)
    velocity = jnp.zeros((3, CZD, GX * CX, GY * CY), jnp.float32)
    positions = jnp.arange(BLOCKS)
    onehot = (positions[:, None] == block_place[None, :]).astype(jnp.float32)
    correlation = jnp.zeros((BLOCKS, NZ, BX, BY), jnp.float32)
    for rounds in range(ITERS):

        def one_block(items):
            return block_step(items[0], items[1], items[2], items[3], velocity, box_rows, box_cols, gauss_rows, gauss_cols)
        pieces, correlation = lax.map(one_block, (fixed, moving, block_place, tissue))
        total = jnp.dot(onehot, pieces.reshape(BLOCKS, -1), precision=EXACT)
        velocity = regularize(velocity, total, CX, CY)
    return (velocity, correlation)
```

```python
import math

import jax
import jax.numpy as jnp
from jax import lax
from jax.sharding import PartitionSpec as P

SCALE = 16
GY = 8
ITERS = 2


EXACT = lax.Precision.HIGHEST
EPSILON = 1e-05
STEP_LENGTH = 0.5
BOX_TAPS = [1.0 / 9.0] * 9
GAUSS_RAW = [math.exp(-((offset - 3) ** 2) / 4.5) for offset in range(7)]
GAUSS_TAPS = [value / sum(GAUSS_RAW) for value in GAUSS_RAW]


def with_halo(block, sides, width):
    for axis, dim in sides:
        count = lax.axis_size(axis)
        forward = [(i, i + 1) for i in range(count - 1)]
        backward = [(target, source) for source, target in forward]
        low = lax.ppermute(
            lax.slice_in_dim(block, block.shape[dim] - width, None, axis=dim), axis, forward
        )
        high = lax.ppermute(lax.slice_in_dim(block, 0, width, axis=dim), axis, backward)
        block = jnp.concatenate([low, block, high], axis=dim)
    return block


def tap_matrix(count, taps):
    radius = len(taps) // 2
    rows = jnp.arange(count)[:, None]
    cols = jnp.arange(count)[None, :]
    matrix = jnp.zeros((count, count), jnp.float32)
    for offset, weight in enumerate(taps):
        matrix = matrix + weight * (rows - cols == offset - radius).astype(jnp.float32)
    return matrix


def along_rows(field, matrix):
    return jnp.einsum("...xy,xu->...uy", field, matrix, precision=EXACT)


def along_cols(field, matrix):
    return jnp.einsum("...y,yv->...v", field, matrix, precision=EXACT)


def planes_filter(field, taps, count):
    total = jnp.zeros(field.shape[:-3] + (count,) + field.shape[-2:], jnp.float32)
    for offset, weight in enumerate(taps):
        total = total + weight * field[..., offset : offset + count, :, :]
    return total


def slope(field, axis):
    widths = [(0, 0)] * field.ndim
    widths[axis] = (1, 1)
    padded = jnp.pad(field, widths)
    length = field.shape[axis]
    upper = lax.slice_in_dim(padded, 2, length + 2, axis=axis)
    lower = lax.slice_in_dim(padded, 0, length, axis=axis)
    return 0.5 * (upper - lower)


def hat_rows(coords, count):
    where = jnp.clip((coords + 0.5) / SCALE - 0.5, 0.0, count - 1.0)
    marks = jnp.arange(count).astype(jnp.float32)
    return jnp.maximum(0.0, 1.0 - jnp.abs(where[..., None] - marks))


def statistics(means, fixed_c, warped_c):
    sii = means[2] - means[0] * means[0]
    sww = means[3] - means[1] * means[1]
    siw = means[4] - means[0] * means[1]
    denom = sii * sww + EPSILON
    similar = siw * siw / denom
    weight = (
        2.0 * siw / denom * (fixed_c - means[0] - siw / (sww + EPSILON) * (warped_c - means[1]))
    )
    return (similar, weight)


def smooth_axis(field, axis):
    widths = [(0, 0)] * field.ndim
    widths[axis] = (1, 1)
    padded = jnp.pad(field, widths)
    length = field.shape[axis]
    upper = lax.slice_in_dim(padded, 2, length + 2, axis=axis)
    lower = lax.slice_in_dim(padded, 0, length, axis=axis)
    return 0.25 * lower + 0.5 * field + 0.25 * upper


def regularize(velocity, total, coarse_rows, coarse_cols):
    block_rows = velocity.shape[2] // coarse_rows
    coarse_depth = velocity.shape[1]
    grid = total.reshape(block_rows, GY, 3, coarse_depth, coarse_rows, coarse_cols)
    grid = grid.transpose(2, 3, 0, 4, 1, 5).reshape(velocity.shape)
    regular = smooth_axis(smooth_axis(smooth_axis(grid, 1), 2), 3)
    return velocity + STEP_LENGTH * regular / jnp.sqrt(jnp.mean(regular * regular) + EPSILON)


def cell_weights(source, length):
    target = jnp.arange(length)
    taps = jnp.zeros((length, source.shape[0]), jnp.float32)
    for offset, weight in enumerate(GAUSS_TAPS):
        taps = taps + weight * (target[:, None] - source[None, :] == offset - 3).astype(jnp.float32)
    return taps.reshape(length // SCALE, SCALE, -1).sum(1)


def everywhere(value):
    count = lax.axis_size("blk") * lax.axis_size("gz")
    copies = jnp.broadcast_to(value[None], (count,) + value.shape)
    return lax.all_to_all(copies, ("blk", "gz"), 0, 0).reshape(-1, value.shape[-1])


def per_device(fixed, moving, block_place, tissue):
    slots, planes, row_side, col_side = fixed.shape
    depth_parts = lax.axis_size("gz")
    depth_index = lax.axis_index("gz")
    blocks = slots * lax.axis_size("blk")
    total_planes = planes * depth_parts
    coarse_depth = total_planes // SCALE
    coarse_rows = row_side // SCALE
    coarse_cols = col_side // SCALE
    grid_rows = blocks // GY * coarse_rows
    grid_cols = GY * coarse_cols
    stacked = jnp.stack([fixed, moving], 0)
    reach = 0
    haloed = with_halo(stacked, (("gz", 2),), 5)
    images = haloed.astype(jnp.float32)
    count_w = planes + 2 * (reach + 4)
    count_m = planes + 2 * reach
    fixed_w = images[0, :, 1 : 1 + count_w]
    moving_w = images[1, :, 1 : 1 + count_w]
    depth_slope = 0.5 * (images[1, :, 2 : 2 + count_w] - images[1, :, 0:count_w])
    row_slope = slope(moving_w, 2)
    col_slope = slope(moving_w, 3)
    depth_w = depth_index * planes - (reach + 4) + jnp.arange(count_w)
    inside_w = ((depth_w >= 0) & (depth_w < total_planes)).astype(jnp.float32)
    depth_hat = hat_rows(depth_w.astype(jnp.float32), coarse_depth)
    depth_m = depth_index * planes - reach + jnp.arange(count_m)
    inside_m = ((depth_m >= 0) & (depth_m < total_planes)).astype(jnp.float32)
    row_cells = jnp.arange(row_side)
    col_cells = jnp.arange(col_side)
    block_row = block_place // GY
    block_col = block_place % GY
    row_hat = hat_rows(
        (block_row[:, None] * row_side + row_cells[None, :]).astype(jnp.float32), grid_rows
    )
    col_hat = hat_rows(
        (block_col[:, None] * col_side + col_cells[None, :]).astype(jnp.float32), grid_cols
    )
    own_depth = depth_index * planes + jnp.arange(planes)
    cell_planes = cell_weights(own_depth, total_planes)
    cell_rows = cell_weights(jnp.arange(row_side), row_side).T
    cell_cols = cell_weights(jnp.arange(col_side), col_side).T
    box_rows = tap_matrix(row_side, BOX_TAPS)
    box_cols = tap_matrix(col_side, BOX_TAPS)
    tissue_scale = tissue.astype(jnp.float32)[:, None, None, None]
    positions = jnp.arange(blocks)
    velocity = jnp.zeros((3, coarse_depth, grid_rows, grid_cols), jnp.float32)
    correlation = jnp.zeros((slots, planes, row_side, col_side), jnp.float32)
    for rounds in range(ITERS):
        partial_value = jnp.einsum("ckab,sxa->sckxb", velocity, row_hat, precision=EXACT)
        partial_value = jnp.einsum("sckxb,syb->sckxy", partial_value, col_hat, precision=EXACT)
        shift = jnp.einsum("zk,sckxy->cszxy", depth_hat, partial_value, precision=EXACT)
        warped = moving_w + shift[0] * depth_slope + shift[1] * row_slope + shift[2] * col_slope
        warped = warped * inside_w[None, :, None, None]
        fields = jnp.stack(
            [fixed_w, warped, fixed_w * fixed_w, warped * warped, fixed_w * warped], 0
        )
        means = planes_filter(fields, BOX_TAPS, count_m)
        means = along_cols(along_rows(means, box_rows), box_cols)
        fixed_m = fixed_w[:, 4 : 4 + count_m]
        warped_m = warped[:, 4 : 4 + count_m]
        similar, weight = statistics(means, fixed_m, warped_m)
        scale = weight * tissue_scale * inside_m[None, :, None, None]
        depth_grad = 0.5 * (warped[:, 5 : 5 + count_m] - warped[:, 3 : 3 + count_m])
        force = jnp.stack(
            [scale * depth_grad, scale * slope(warped_m, 2), scale * slope(warped_m, 3)], 0
        )
        partial = jnp.einsum("cszxy,yb->cszxb", force, cell_cols, precision=EXACT)
        partial = jnp.einsum("cszxb,xa->cszab", partial, cell_rows, precision=EXACT)
        piece = jnp.einsum("kz,cszab->sckab", cell_planes, partial, precision=EXACT)
        piece = piece.reshape(slots, -1)
        message = jnp.concatenate([piece, block_place[:, None].astype(jnp.float32)], axis=1)
        received = everywhere(message)
        onehot = (positions[:, None] == received[None, :, -1].astype(jnp.int32)).astype(jnp.float32)
        total = jnp.dot(onehot, received[:, :-1], precision=EXACT)
        velocity = regularize(velocity, total, coarse_rows, coarse_cols)
        correlation = similar
    return (velocity, correlation)


def solution(mesh):
    return jax.shard_map(
        per_device,
        mesh=mesh,
        in_specs=(P("blk", "gz", None, None), P("blk", "gz", None, None), P("blk"), P("blk")),
        out_specs=(P(), P("blk", "gz", None, None)),
        check_vma=False,
    )
```

```python
import functools
import math

import jax
import jax.numpy as jnp
import numpy as np
from jax import lax
from jax.experimental import pallas as pl
from jax.experimental.pallas import tpu as pltpu
from jax.sharding import PartitionSpec as P

SCALE = 16
GY = 8
EPSILON = 1e-05
STEP_LENGTH = 0.5
GAUSS_RAW = [math.exp(-((offset - 3) ** 2) / 4.5) for offset in range(7)]
GAUSS_TAPS = [value / sum(GAUSS_RAW) for value in GAUSS_RAW]
REACH = 4
LANES = 128
F32 = jnp.float32
BF16 = jnp.bfloat16


def cell_weights(length):
    table = np.zeros((length // SCALE, length))
    for target in range(length):
        for offset, weight in enumerate(GAUSS_TAPS):
            source = target - (offset - 3)
            if 0 <= source < length:
                table[target // SCALE, source] += weight
    return table


def hat_table(length):
    count = length // SCALE
    where = np.clip((np.arange(length) + 0.5) / SCALE - 0.5, 0.0, count - 1.0)
    return np.maximum(0.0, 1.0 - np.abs(where[None, :] - np.arange(count)[:, None]))


def tables(parts, planes, row_side, col_side):
    total = parts * planes
    coarse = total // SCALE
    hats = np.zeros((coarse, total + 2 * REACH))
    hats[:, REACH : REACH + total] = hat_table(total)
    cells = cell_weights(total)
    wide = planes + 2 * REACH
    depth = np.stack(
        [
            np.concatenate(
                [hats[:, g * planes : g * planes + wide].reshape(-1)]
                + [cells[:, g * planes : (g + 1) * planes].reshape(-1)]
            )
            for g in range(parts)
        ]
    )
    depth = np.broadcast_to(depth[:, :, None], depth.shape + (LANES,))
    rows = np.broadcast_to(cell_weights(row_side)[:, :, None], (row_side // SCALE, row_side, LANES))
    cols = np.tile(cell_weights(col_side).T, (1, LANES // (col_side // SCALE)))
    band = np.abs(np.arange(col_side)[:, None] - np.arange(col_side)[None, :]) <= 4
    box = np.kron(np.eye(2), band)
    slope = np.zeros((col_side, col_side))
    for i in range(col_side - 1):
        slope[i + 1, i] = 0.5
        slope[i, i + 1] = -0.5
    return (
        np.asarray(depth, np.float32),
        np.asarray(rows, np.float32),
        np.asarray(cols, np.float32),
        jnp.asarray(box, BF16),
        jnp.asarray(slope, BF16),
    )


def spread_table(groups, coarse_rows, coarse_cols):
    lanes = np.arange(LANES)
    a, l = lanes // (GY * coarse_cols), lanes % (GY * coarse_cols)
    table = np.zeros((groups, LANES, LANES), np.float32)
    for g in range(groups):
        table[g, (g * coarse_rows + a) * coarse_cols + l % coarse_cols, lanes] = 1.0
    return table


def lane_index(shape):
    return lax.broadcasted_iota(jnp.int32, shape, len(shape) - 1)


def sublane_index(shape):
    return lax.broadcasted_iota(jnp.int32, shape, len(shape) - 2)


def tail(plane):
    return jnp.concatenate([plane, jnp.zeros((8, plane.shape[1]), plane.dtype)], axis=0)


def window_of_nine(items):
    two = [a + b for a, b in zip(items[:-1], items[1:])]
    four = [a + b for a, b in zip(two[:-2], two[2:])]
    eight = [a + b for a, b in zip(four[:-4], four[4:])]
    return [a + b for a, b in zip(eight[:-1], items[8:])]


def row_box(plane):
    side = plane.shape[0]
    padded = tail(plane)
    total = padded + pltpu.roll(padded, 1, 0)
    total = total + pltpu.roll(total, 2, 0)
    total = total + pltpu.roll(total, 4, 0)
    total = total + pltpu.roll(padded, 8, 0)
    return pltpu.roll(total, side + 8 - 4, 0)[:side]


def row_slope(plane):
    side = plane.shape[0]
    padded = tail(plane)
    return 0.5 * (pltpu.roll(padded, side + 7, 0)[:side] - pltpu.roll(padded, 1, 0)[:side])


def col_slope(plane):
    width = plane.shape[1]
    lane = lane_index(plane.shape)
    upper = jnp.where(lane < width - 1, pltpu.roll(plane, width - 1, 1), 0.0)
    lower = jnp.where(lane > 0, pltpu.roll(plane, 1, 1), 0.0)
    return 0.5 * (upper - lower)


def load_images(odd, fixed_ref, moving_ref, near_ref, far_ref, image, shifted):
    planes = fixed_ref.shape[1]
    image[REACH : REACH + planes] = fixed_ref[0].astype(F32)
    shifted[REACH + 1 : REACH + 1 + planes] = moving_ref[0].astype(F32)
    near = near_ref[...].astype(F32)
    far = far_ref[...].astype(F32)
    low = jnp.where(odd, near, far)
    high = jnp.where(odd, far, near)
    image[0:REACH] = low[0:REACH]
    image[REACH + planes :] = high[0:REACH]
    shifted[0 : REACH + 1] = low[REACH:]
    shifted[REACH + 1 + planes :] = high[REACH:]


def box_sums(fields, planes, side, sums, parts, box_ref):
    half = planes // 2
    count = 0
    for tile in range(side // 8):
        rows = slice(8 * tile, 8 * tile + 8)
        lists = fields(rows)
        count = len(lists)
        for f, items in enumerate(lists):
            for z, item in enumerate(window_of_nine(items)):
                sums[f, z, rows] = item
    for f in range(count):
        for z in range(planes):
            total = row_box(sums[f, z])
            rows = slice((f * half + z % half) * side, (f * half + z % half + 1) * side)
            lanes = slice((z // half) * LANES, (z // half + 1) * LANES)
            for part in range(3):
                rounded = total.astype(BF16)
                parts[part, rows, lanes] = rounded
                total = total - rounded.astype(F32)
    used = slice(0, count * half * side)
    box = box_ref[...]
    result = jnp.dot(parts[0, used], box, preferred_element_type=F32)
    result = result + jnp.dot(parts[1, used], box, preferred_element_type=F32)
    result = result + jnp.dot(parts[2, used], box, preferred_element_type=F32)

    def of(f, z):
        start = (f * half + z % half) * side
        lane = (z // half) * LANES
        return result[start : start + side, lane : lane + LANES]

    return of


def force_message(weights, warped, planes, depth_ref, part, rows_ref, cols_ref, mark, tissue):
    coarse = depth_ref.shape[1] // (2 * planes + 2 * REACH)
    first = coarse * (planes + 2 * REACH)
    coarse_rows, side, _ = rows_ref.shape
    total = [[None] * coarse for _ in range(3)]
    for z in range(planes):
        plane = warped(z)
        slopes = (0.5 * (warped(z + 1) - warped(z - 1)), row_slope(plane), col_slope(plane))
        for k in range(coarse):
            index = first + k * planes + z
            share = weights(z) * depth_ref[part, index : index + 1, :]
            for c in range(3):
                term = share * slopes[c]
                total[c][k] = term if z == 0 else total[c][k] + term
    tiles = []
    for c in range(3):
        for k in range(coarse):
            for a in range(coarse_rows):
                product = total[c][k] * rows_ref[a]
                tile = product[0:8]
                for start in range(8, side, 8):
                    tile = tile + product[start : start + 8]
                tiles.append(tile)
    sums = jnp.dot(
        jnp.concatenate(tiles, axis=0),
        cols_ref[...],
        precision=lax.Precision.HIGHEST,
        preferred_element_type=F32,
    )
    coarse_cols = LANES // SCALE
    lane = lane_index((8, LANES))
    picked = jnp.zeros((8, LANES), F32)
    for g in range(len(tiles)):
        picked = jnp.where(lane // coarse_cols == g, sums[8 * g : 8 * g + 8], picked)
    row = jnp.sum(picked, axis=0, keepdims=True) * tissue
    return jnp.where(lane[0:1] == len(tiles) * coarse_cols, mark, row)


def regular_grid(received, spread_ref, block_rows, coarse_rows, coarse_cols):
    groups = spread_ref.shape[0]
    used = groups * coarse_rows * coarse_cols
    width = GY * coarse_cols
    place = received[:, used : used + 1].astype(jnp.int32)
    lane = lane_index(received.shape)
    here = (place % GY) == (lane % width) // coarse_cols
    block_row = place // GY
    sub = sublane_index((8, LANES))
    grids = [jnp.zeros((8, LANES), F32) for _ in range(block_rows)]
    for g in range(groups):
        entry = jnp.dot(
            received, spread_ref[g], precision=lax.Precision.HIGHEST, preferred_element_type=F32
        )
        for r in range(block_rows):
            chosen = here if block_rows == 1 else here & (block_row == r)
            total = jnp.sum(jnp.where(chosen, entry, 0.0), axis=0, keepdims=True)
            grids[r] = jnp.where(sub == g, total, grids[r])
    even = sub % 2 == 0
    lane = lane_index((8, LANES))
    column = lane % width
    first = lane < width
    grids = [
        0.5 * g + 0.25 * jnp.where(even, pltpu.roll(g, 7, 0), pltpu.roll(g, 1, 0)) for g in grids
    ]
    other = [pltpu.roll(g, width, 1) for g in grids]
    none = jnp.zeros((8, LANES), F32)
    before = [none] + other[:-1]
    after = other[1:] + [none]
    grids = [
        0.5 * g + 0.25 * (o + jnp.where(first, b, a))
        for g, o, b, a in zip(grids, other, before, after)
    ]
    grids = [
        0.25 * jnp.where(column > 0, pltpu.roll(g, 1, 1), 0.0)
        + 0.5 * g
        + 0.25 * jnp.where(column < width - 1, pltpu.roll(g, LANES - 1, 1), 0.0)
        for g in grids
    ]
    grids = [jnp.where(sub < groups, g, 0.0) for g in grids]
    square = functools.reduce(lambda a, b: a + b, [g * g for g in grids])
    square = jnp.sum(jnp.sum(square, axis=1, keepdims=True), axis=0, keepdims=True)
    mean = square * (1.0 / (groups * block_rows * LANES))
    factor = STEP_LENGTH / jnp.sqrt(mean + EPSILON)
    return [g * factor for g in grids]


def pack_kernel(fixed_ref, moving_ref, near_ref, far_ref):
    planes = fixed_ref.shape[1]
    odd = lax.axis_index("gz") % 2
    for ref, low in ((near_ref, odd == 1), (far_ref, odd == 0)):
        ref[0:REACH] = fixed_ref[0, pl.ds(jnp.where(low, 0, planes - REACH), REACH)]
        ref[REACH:] = moving_ref[0, pl.ds(jnp.where(low, 0, planes - REACH - 1), REACH + 1)]


def first_kernel(
    fixed_ref, moving_ref, near_ref, far_ref, place_ref, tissue_ref,
    depth_ref, rows_ref, cols_ref, box_ref,
    message_ref, mean_ref, variance_ref,
    image, shifted, sums, parts, weight,
):
    _, planes, side, _ = fixed_ref.shape
    part = lax.axis_index("gz")
    load_images(part % 2 == 1, fixed_ref, moving_ref, near_ref, far_ref, image, shifted)
    wide = planes + 2 * REACH

    def fields(rows):
        i = [image[z, rows] for z in range(wide)]
        w = [shifted[z + 1, rows] for z in range(wide)]
        return (
            i,
            w,
            [a * a for a in i],
            [b * b for b in w],
            [a * b for a, b in zip(i, w)],
        )

    of = box_sums(fields, planes, side, sums, parts, box_ref)
    for z in range(planes):
        mean_i, mean_w, mean_ii, mean_ww, mean_iw = [of(f, z) * (1.0 / 729.0) for f in range(5)]
        sii = mean_ii - mean_i * mean_i
        sww = mean_ww - mean_w * mean_w
        siw = mean_iw - mean_i * mean_w
        mean_ref[z] = mean_i
        variance_ref[z] = sii
        ratio = siw / (sii * sww + EPSILON)
        weight[z] = (2.0 * ratio) * (
            (image[z + REACH] - mean_i)
            - siw / (sww + EPSILON) * (shifted[z + REACH + 1] - mean_w)
        )
    row = force_message(
        lambda z: weight[z],
        lambda z: shifted[z + REACH + 1],
        planes, depth_ref, part, rows_ref, cols_ref,
        place_ref[...].astype(F32), tissue_ref[...].astype(F32),
    )
    message_ref[...] = jnp.broadcast_to(row[None], message_ref.shape)


def second_kernel(
    received_ref, fixed_ref, moving_ref, near_ref, far_ref, place_ref, tissue_ref,
    mean_ref, variance_ref, depth_ref, rows_ref, cols_ref, box_ref, slope_ref, spread_ref,
    message_ref, map_ref, velocity_ref,
    image, shifted, warped, sums, parts, weight,
):
    _, planes, side, _ = fixed_ref.shape
    part = lax.axis_index("gz")
    load_images(part % 2 == 1, fixed_ref, moving_ref, near_ref, far_ref, image, shifted)
    wide = planes + 2 * REACH
    coarse_rows = rows_ref.shape[0]
    coarse_cols = LANES // SCALE
    block_rows = velocity_ref.shape[0] // 8
    coarse = depth_ref.shape[1] // (2 * planes + 2 * REACH)
    width = GY * coarse_cols

    grids = regular_grid(received_ref[...], spread_ref, block_rows, coarse_rows, coarse_cols)
    for r in range(block_rows):
        velocity_ref[8 * r : 8 * r + 8] = grids[r]

    place = place_ref[...]
    row_of, col_of = place // GY, place % GY
    y = (lane_index((1, LANES)) + col_of * LANES).astype(F32)
    where_y = jnp.clip((y + 0.5) * (1.0 / SCALE) - 0.5, 0.0, width - 1.0)
    entry = sublane_index((LANES, LANES))
    hat_y = jnp.maximum(0.0, 1.0 - jnp.abs(where_y - (entry % width).astype(F32)))
    hat_y = jnp.concatenate(
        [jnp.where(entry // width == a, hat_y, 0.0) for a in range(coarse_rows)], axis=1
    )
    along = jnp.dot(
        jnp.concatenate(grids, axis=0),
        hat_y,
        precision=lax.Precision.HIGHEST,
        preferred_element_type=F32,
    )
    x = (sublane_index((side, LANES)) + row_of * side).astype(F32)
    where_x = jnp.clip((x + 0.5) * (1.0 / SCALE) - 0.5, 0.0, block_rows * coarse_rows - 1.0)
    shift = [[jnp.zeros((side, LANES), F32) for _ in range(coarse)] for _ in range(3)]
    for r in range(block_rows):
        for a in range(coarse_rows):
            hat_x = jnp.maximum(0.0, 1.0 - jnp.abs(where_x - float(r * coarse_rows + a)))
            for c in range(3):
                for k in range(coarse):
                    g = 8 * r + c * coarse + k
                    line = along[g : g + 1, a * LANES : (a + 1) * LANES]
                    shift[c][k] = shift[c][k] + hat_x * line
    for z in range(wide):
        plane = shifted[z + 1]
        slopes = (
            0.5 * (shifted[z + 2] - shifted[z]),
            row_slope(plane),
            jnp.dot(plane.astype(BF16), slope_ref[...], preferred_element_type=F32),
        )
        hats = [depth_ref[part, k * wide + z : k * wide + z + 1, :] for k in range(coarse)]
        for c in range(3):
            u = hats[0] * shift[c][0]
            for k in range(1, coarse):
                u = u + hats[k] * shift[c][k]
            plane = plane + u * slopes[c]
        warped[z] = plane

    def fields(rows):
        i = [image[z, rows] for z in range(wide)]
        w = [warped[z, rows] for z in range(wide)]
        return (w, [b * b for b in w], [a * b for a, b in zip(i, w)])

    of = box_sums(fields, planes, side, sums, parts, box_ref)
    for z in range(planes):
        mean_w, mean_ww, mean_iw = [of(f, z) * (1.0 / 729.0) for f in range(3)]
        mean_i = mean_ref[z]
        sii = variance_ref[z]
        sww = mean_ww - mean_w * mean_w
        siw = mean_iw - mean_i * mean_w
        ratio = siw / (sii * sww + EPSILON)
        map_ref[0, z] = siw * ratio
        weight[z] = (2.0 * ratio) * (
            (image[z + REACH] - mean_i) - siw / (sww + EPSILON) * (warped[z + REACH] - mean_w)
        )
    row = force_message(
        lambda z: weight[z],
        lambda z: warped[z + REACH],
        planes, depth_ref, part, rows_ref, cols_ref,
        place.astype(F32), tissue_ref[...].astype(F32),
    )
    message_ref[...] = jnp.broadcast_to(row[None], message_ref.shape)


def last_kernel(received_ref, velocity_ref, spread_ref, out_ref):
    _, coarse, rows, width = out_ref.shape
    coarse_rows = LANES // width
    block_rows = rows // coarse_rows
    grids = regular_grid(
        received_ref[...], spread_ref, block_rows, coarse_rows, width // GY
    )
    for r in range(block_rows):
        velocity = velocity_ref[8 * r : 8 * r + 8] + grids[r]
        for c in range(3):
            for k in range(coarse):
                g = c * coarse + k
                for a in range(coarse_rows):
                    out_ref[c, k, r * coarse_rows + a : r * coarse_rows + a + 1, :] = velocity[
                        g : g + 1, a * width : (a + 1) * width
                    ]


def call(kernel, outs, scratch, *operands):
    vmem = pl.BlockSpec(memory_space=pltpu.VMEM)
    return pl.pallas_call(
        kernel,
        out_shape=[jax.ShapeDtypeStruct(shape, dtype) for shape, dtype in outs],
        in_specs=[vmem] * len(operands),
        out_specs=[vmem] * len(outs),
        scratch_shapes=[pltpu.VMEM(shape, dtype) for shape, dtype in scratch],
        compiler_params=pltpu.CompilerParams(vmem_limit_bytes=24 << 20),
    )(*operands)


def per_device(fixed, moving, block_place, tissue):
    slots, planes, side, width = fixed.shape
    assert slots == 1 and width == LANES
    depth_parts = lax.axis_size("gz")
    devices = lax.axis_size("blk") * depth_parts
    blocks = slots * lax.axis_size("blk")
    coarse = planes * depth_parts // SCALE
    coarse_rows, coarse_cols = side // SCALE, width // SCALE
    block_rows = blocks // GY
    place = block_place.reshape(1, 1)
    mask = tissue.reshape(1, 1)
    depth, rows, cols, box, slope = tables(depth_parts, planes, side, width)
    spread = spread_table(3 * coarse, coarse_rows, coarse_cols)

    near, far = call(
        pack_kernel, [((2 * REACH + 1, side, width), BF16)] * 2, [], fixed, moving
    )
    pairs = [(i, i + 1) for i in range(0, depth_parts - 1, 2)]
    near = lax.ppermute(near, "gz", pairs + [(b, a) for a, b in pairs])
    pairs = [(i, i + 1) for i in range(1, depth_parts - 1, 2)]
    far = lax.ppermute(far, "gz", pairs + [(b, a) for a, b in pairs])

    wide = planes + 2 * REACH
    field = (planes, side, width)
    message = ((devices, 1, LANES), F32)

    def scratch(fields):
        return [
            ((fields, planes, side, width), F32),
            ((3, fields * planes * side // 2, 2 * width), BF16),
            (field, F32),
        ]

    images = [((wide, side, width), F32), ((wide + 2, side, width), F32)]
    sent, mean, variance = call(
        first_kernel, [message, (field, F32), (field, F32)], images + scratch(5),
        fixed, moving, near, far, place, mask, depth, rows, cols, box,
    )
    received = lax.all_to_all(sent, ("blk", "gz"), 0, 0).reshape(devices, LANES)
    sent, correlation, velocity = call(
        second_kernel,
        [message, ((1,) + field, F32), ((8 * block_rows, LANES), F32)],
        images + [((wide, side, width), F32)] + scratch(3),
        received, fixed, moving, near, far, place, mask,
        mean, variance, depth, rows, cols, box, slope, spread,
    )
    received = lax.all_to_all(sent, ("blk", "gz"), 0, 0).reshape(devices, LANES)
    (velocity,) = call(
        last_kernel,
        [((3, coarse, block_rows * coarse_rows, GY * coarse_cols), F32)],
        [],
        received, velocity, spread,
    )
    return (velocity, correlation)


def solution(mesh):
    return jax.shard_map(
        per_device,
        mesh=mesh,
        in_specs=(P("blk", "gz", None, None), P("blk", "gz", None, None), P("blk"), P("blk")),
        out_specs=(P(), P("blk", "gz", None, None)),
        check_vma=False,
    )
```

```python
import functools
import math

import jax
import jax.numpy as jnp
from jax import lax
from jax.experimental import pallas as pl
from jax.experimental.pallas import tpu as pltpu
from jax.sharding import PartitionSpec as P

SCALE = 16
GY = 8
EPSILON = 1e-05
STEP_LENGTH = 0.5
GAUSS_RAW = [math.exp(-((offset - 3) ** 2) / 4.5) for offset in range(7)]
GAUSS_TAPS = [value / sum(GAUSS_RAW) for value in GAUSS_RAW]
REACH = 4
LANES = 128
F32 = jnp.float32
BF16 = jnp.bfloat16


def cell_weights(index, cell, length):
    total = jnp.zeros(index.shape, F32)
    for offset, weight in enumerate(GAUSS_TAPS):
        target = index + (offset - 3)
        inside = (target >= cell * SCALE) & (target < cell * SCALE + SCALE)
        total = total + jnp.where(inside, weight, 0.0)
    return total


def hat(index, cell, count):
    where = jnp.clip((index.astype(F32) + 0.5) * (1.0 / SCALE) - 0.5, 0.0, count - 1.0)
    return jnp.maximum(0.0, 1.0 - jnp.abs(where - cell.astype(F32)))


def lane_index(shape):
    return lax.broadcasted_iota(jnp.int32, shape, len(shape) - 1)


def sublane_index(shape):
    return lax.broadcasted_iota(jnp.int32, shape, len(shape) - 2)


def tail(plane):
    return jnp.concatenate([plane, jnp.zeros((8, plane.shape[1]), plane.dtype)], axis=0)


def split(value, count):
    parts = []
    for _ in range(count):
        parts.append(value.astype(BF16))
        value = value - parts[-1].astype(F32)
    return parts


def exact_dot(value, table):
    rows = value.shape[0]
    stacked = jnp.concatenate(split(value, 3), axis=0)
    product = jnp.dot(stacked, table, preferred_element_type=F32)
    return product[:rows] + product[rows : 2 * rows] + product[2 * rows :]


def window_of_nine(items):
    two = [a + b for a, b in zip(items[:-1], items[1:])]
    four = [a + b for a, b in zip(two[:-2], two[2:])]
    eight = [a + b for a, b in zip(four[:-4], four[4:])]
    return [a + b for a, b in zip(eight[:-1], items[8:])]


def row_box(plane):
    side = plane.shape[0]
    padded = tail(plane)
    total = padded + pltpu.roll(padded, 1, 0)
    total = total + pltpu.roll(total, 2, 0)
    total = total + pltpu.roll(total, 4, 0)
    total = total + pltpu.roll(padded, 8, 0)
    return pltpu.roll(total, side + 8 - 4, 0)[:side]


def row_slope(plane):
    side = plane.shape[0]
    padded = tail(plane)
    return 0.5 * (pltpu.roll(padded, side + 7, 0)[:side] - pltpu.roll(padded, 1, 0)[:side])


def col_slope(plane):
    width = plane.shape[1]
    lane = lane_index(plane.shape)
    upper = jnp.where(lane < width - 1, pltpu.roll(plane, width - 1, 1), 0.0)
    lower = jnp.where(lane > 0, pltpu.roll(plane, 1, 1), 0.0)
    return 0.5 * (upper - lower)


def load_images(odd, fixed_ref, moving_ref, near_ref, far_ref, image, shifted):
    planes = fixed_ref.shape[0]
    image[REACH : REACH + planes] = fixed_ref[...].astype(F32)
    shifted[REACH + 1 : REACH + 1 + planes] = moving_ref[...].astype(F32)
    near = near_ref[...].astype(F32)
    far = far_ref[...].astype(F32)
    low = jnp.where(odd, near, far)
    high = jnp.where(odd, far, near)
    image[0:REACH] = low[0:REACH]
    image[REACH + planes :] = high[0:REACH]
    shifted[0 : REACH + 1] = low[REACH:]
    shifted[REACH + 1 + planes :] = high[REACH:]


def box_sums(fields, planes, side, sums, parts, box_ref):
    half = planes // 2
    count = 0
    for tile in range(side // 8):
        rows = slice(8 * tile, 8 * tile + 8)
        lists = fields(rows)
        count = len(lists)
        for f, items in enumerate(lists):
            for z, item in enumerate(window_of_nine(items)):
                sums[f, z, rows] = item
    for f in range(count):
        for z in range(planes):
            total = row_box(sums[f, z])
            rows = slice((f * half + z % half) * side, (f * half + z % half + 1) * side)
            lanes = slice((z // half) * LANES, (z // half + 1) * LANES)
            for part, rounded in enumerate(split(total, 3)):
                parts[part, rows, lanes] = rounded
    used = slice(0, count * half * side)
    box = box_ref[...]
    result = jnp.dot(parts[0, used], box, preferred_element_type=F32)
    result = result + jnp.dot(parts[1, used], box, preferred_element_type=F32)
    result = result + jnp.dot(parts[2, used], box, preferred_element_type=F32)

    def of(f, z):
        start = (f * half + z % half) * side
        lane = (z // half) * LANES
        return result[start : start + side, lane : lane + LANES]

    return of


def force_message(weights, warped, planes, cells_ref, rows_ref, cols_ref, marks_ref):
    coarse = cells_ref.shape[0] // planes
    coarse_rows, side, _ = rows_ref.shape
    total = [[None] * coarse for _ in range(3)]
    for z in range(planes):
        plane = warped(z)
        slopes = (0.5 * (warped(z + 1) - warped(z - 1)), row_slope(plane), col_slope(plane))
        for k in range(coarse):
            index = k * planes + z
            share = weights(z) * cells_ref[index : index + 1, :]
            for c in range(3):
                term = share * slopes[c]
                total[c][k] = term if z == 0 else total[c][k] + term
    tiles = []
    for c in range(3):
        for k in range(coarse):
            for a in range(coarse_rows):
                product = total[c][k] * rows_ref[a]
                tile = product[0:8]
                for start in range(8, side, 8):
                    tile = tile + product[start : start + 8]
                tiles.append(tile)
    sums = exact_dot(jnp.concatenate(tiles, axis=0), cols_ref[...])
    sums = sums[:, :LANES] + sums[:, LANES:]
    coarse_cols = LANES // SCALE
    lane = lane_index((8, LANES))
    picked = jnp.zeros((8, LANES), F32)
    for g in range(len(tiles)):
        picked = jnp.where(lane // coarse_cols == g, sums[8 * g : 8 * g + 8], picked)
    row = jnp.sum(picked, axis=0, keepdims=True) * marks_ref[1:2]
    return jnp.where(lane[0:1] == len(tiles) * coarse_cols, marks_ref[0:1], row)


def regular_grid(received, spread_ref, block_rows, coarse_rows, coarse_cols):
    groups = spread_ref.shape[1] // LANES
    used = groups * coarse_rows * coarse_cols
    width = GY * coarse_cols
    place = received[:, used : used + 1].astype(jnp.int32)
    lane = lane_index(received.shape)
    here = (place % GY) == (lane % width) // coarse_cols
    block_row = place // GY
    sub = sublane_index((8, LANES))
    grids = [jnp.zeros((8, LANES), F32) for _ in range(block_rows)]
    entries = exact_dot(received, spread_ref[...])
    for g in range(groups):
        entry = entries[:, g * LANES : (g + 1) * LANES]
        for r in range(block_rows):
            chosen = here if block_rows == 1 else here & (block_row == r)
            total = jnp.sum(jnp.where(chosen, entry, 0.0), axis=0, keepdims=True)
            grids[r] = jnp.where(sub == g, total, grids[r])
    even = sub % 2 == 0
    lane = lane_index((8, LANES))
    column = lane % width
    first = lane < width
    grids = [
        0.5 * g + 0.25 * jnp.where(even, pltpu.roll(g, 7, 0), pltpu.roll(g, 1, 0)) for g in grids
    ]
    other = [pltpu.roll(g, width, 1) for g in grids]
    none = jnp.zeros((8, LANES), F32)
    before = [none] + other[:-1]
    after = other[1:] + [none]
    grids = [
        0.5 * g + 0.25 * (o + jnp.where(first, b, a))
        for g, o, b, a in zip(grids, other, before, after)
    ]
    grids = [
        0.25 * jnp.where(column > 0, pltpu.roll(g, 1, 1), 0.0)
        + 0.5 * g
        + 0.25 * jnp.where(column < width - 1, pltpu.roll(g, LANES - 1, 1), 0.0)
        for g in grids
    ]
    grids = [jnp.where(sub < groups, g, 0.0) for g in grids]
    square = functools.reduce(lambda a, b: a + b, [g * g for g in grids])
    square = jnp.sum(jnp.sum(square, axis=1, keepdims=True), axis=0, keepdims=True)
    mean = square * (1.0 / (groups * block_rows * LANES))
    factor = STEP_LENGTH / jnp.sqrt(mean + EPSILON)
    return [g * factor for g in grids]


def pack_kernel(fixed_hbm, moving_hbm, near_ref, far_ref, fixed_ref, moving_ref, sems):
    copies = [
        pltpu.make_async_copy(source.at[0], target, sems.at[i])
        for i, (source, target) in enumerate(((fixed_hbm, fixed_ref), (moving_hbm, moving_ref)))
    ]
    for copy in copies:
        copy.start()
    planes = fixed_ref.shape[0]
    part = lax.axis_index("gz")
    odd = part % 2
    inner = (part > 0) & (part < lax.axis_size("gz") - 1)
    for copy in copies:
        copy.wait()
    for ref, low, keep in ((far_ref, odd == 0, inner), (near_ref, odd == 1, None)):
        i = fixed_ref[pl.ds(jnp.where(low, 0, planes - REACH), REACH)]
        j = moving_ref[pl.ds(jnp.where(low, 0, planes - REACH - 1), REACH + 1)]
        if keep is not None:
            i = jnp.where(keep, i.astype(F32), 0.0).astype(BF16)
            j = jnp.where(keep, j.astype(F32), 0.0).astype(BF16)
        ref[0:REACH] = i
        ref[REACH:] = j


def table_kernel(
    both_ref,
    marks_ref, hats_ref, cells_ref, rows_ref, cols_ref, box_ref, slope_ref, spread_ref, hat_x_ref, hat_y_ref,
    *, planes, block_rows,
):
    part = lax.axis_index("gz")
    total = planes * lax.axis_size("gz")
    coarse_rows, side, _ = rows_ref.shape
    coarse_cols = LANES // SCALE
    width = GY * coarse_cols
    wide = planes + 2 * REACH
    row = sublane_index(hats_ref.shape)
    z = part * planes + row % wide - REACH
    hats_ref[...] = jnp.where((z >= 0) & (z < total), hat(z, row // wide, total // SCALE), 0.0)
    row = sublane_index(cells_ref.shape)
    cells_ref[...] = cell_weights(part * planes + row % planes, row // planes, total)
    for a in range(coarse_rows):
        rows_ref[a] = cell_weights(sublane_index((side, LANES)), a, side)
    square = (LANES, LANES)
    cols = cell_weights(sublane_index(square), lane_index(square) % coarse_cols, LANES)
    for i, value in enumerate(split(cols, 2)):
        cols_ref[:, i * LANES : (i + 1) * LANES] = value
    apart = sublane_index(square) - lane_index(square)
    band = jnp.where(jnp.abs(apart) <= 4, 1.0, 0.0).astype(BF16)
    box_ref[...] = jnp.zeros(box_ref.shape, BF16)
    for i in range(2):
        box_ref[i * LANES : (i + 1) * LANES, i * LANES : (i + 1) * LANES] = band
    slope_ref[...] = jnp.where(apart == 1, 0.5, jnp.where(apart == -1, -0.5, 0.0)).astype(BF16)
    lane = lane_index(square)
    source = (lane // width) * coarse_cols + lane % coarse_cols
    for g in range(spread_ref.shape[1] // LANES):
        hit = sublane_index(square) == source + g * coarse_rows * coarse_cols
        spread_ref[:, g * LANES : (g + 1) * LANES] = jnp.where(hit, 1.0, 0.0).astype(BF16)
    row = sublane_index(marks_ref.shape)
    marks_ref[...] = jnp.where(row == 0, both_ref[0:1, 0:1], both_ref[1:2, 0:1]).astype(F32)
    place = both_ref[0:1, 0:1]
    y = lane + (place % GY) * LANES
    entry = sublane_index(square)
    hat_y = hat(y, entry % width, width)
    for a in range(coarse_rows):
        chosen = jnp.where(entry // width == a, hat_y, 0.0).astype(BF16)
        hat_y_ref[:, a * LANES : (a + 1) * LANES] = chosen
    x = sublane_index((side, LANES)) + (place // GY) * side
    for r in range(block_rows * coarse_rows):
        hat_x_ref[r] = hat(x, jnp.full((1, 1), r, jnp.int32), block_rows * coarse_rows)


def first_kernel(
    fixed_ref, moving_ref, near_ref, far_ref, marks_ref,
    cells_ref, rows_ref, cols_ref, box_ref,
    message_ref, mean_ref, variance_ref,
    image, shifted, sums, parts, weight,
):
    planes, side, _ = fixed_ref.shape
    odd = lax.axis_index("gz") % 2 == 1
    load_images(odd, fixed_ref, moving_ref, near_ref, far_ref, image, shifted)
    wide = planes + 2 * REACH

    def fields(rows):
        i = [image[z, rows] for z in range(wide)]
        w = [shifted[z + 1, rows] for z in range(wide)]
        return (
            i,
            w,
            [a * a for a in i],
            [b * b for b in w],
            [a * b for a, b in zip(i, w)],
        )

    of = box_sums(fields, planes, side, sums, parts, box_ref)
    for z in range(planes):
        mean_i, mean_w, mean_ii, mean_ww, mean_iw = [of(f, z) * (1.0 / 729.0) for f in range(5)]
        sii = mean_ii - mean_i * mean_i
        sww = mean_ww - mean_w * mean_w
        siw = mean_iw - mean_i * mean_w
        mean_ref[z] = mean_i
        variance_ref[z] = sii
        ratio = siw / (sii * sww + EPSILON)
        weight[z] = (2.0 * ratio) * (
            (image[z + REACH] - mean_i)
            - siw / (sww + EPSILON) * (shifted[z + REACH + 1] - mean_w)
        )
    row = force_message(
        lambda z: weight[z],
        lambda z: shifted[z + REACH + 1],
        planes, cells_ref, rows_ref, cols_ref, marks_ref,
    )
    message_ref[...] = jnp.broadcast_to(row[None], message_ref.shape)


def second_kernel(
    received_ref, fixed_ref, moving_ref, near_ref, far_ref, marks_ref,
    mean_ref, variance_ref, hats_ref, cells_ref, rows_ref, cols_ref, box_ref, slope_ref,
    spread_ref, hat_x_ref, hat_y_ref,
    message_ref, map_ref, velocity_ref,
    image, shifted, warped, sums, parts, weight,
):
    planes, side, _ = fixed_ref.shape
    odd = lax.axis_index("gz") % 2 == 1
    load_images(odd, fixed_ref, moving_ref, near_ref, far_ref, image, shifted)
    wide = planes + 2 * REACH
    coarse_rows = rows_ref.shape[0]
    coarse_cols = LANES // SCALE
    block_rows = velocity_ref.shape[0] // 8
    coarse = hats_ref.shape[0] // wide

    grids = regular_grid(received_ref[...], spread_ref, block_rows, coarse_rows, coarse_cols)
    for r in range(block_rows):
        velocity_ref[8 * r : 8 * r + 8] = grids[r]
    along = exact_dot(jnp.concatenate(grids, axis=0), hat_y_ref[...])
    shift = [[None] * coarse for _ in range(3)]
    for r in range(block_rows):
        for a in range(coarse_rows):
            hat_x = hat_x_ref[r * coarse_rows + a]
            for c in range(3):
                for k in range(coarse):
                    g = 8 * r + c * coarse + k
                    term = hat_x * along[g : g + 1, a * LANES : (a + 1) * LANES]
                    shift[c][k] = term if r + a == 0 else shift[c][k] + term
    inner = shifted[1 : wide + 1].reshape(wide * side, LANES).astype(BF16)
    across = jnp.dot(inner, slope_ref[...], preferred_element_type=F32)
    for z in range(wide):
        plane = shifted[z + 1]
        slopes = (
            0.5 * (shifted[z + 2] - shifted[z]),
            row_slope(plane),
            across[z * side : (z + 1) * side],
        )
        hats = [hats_ref[k * wide + z : k * wide + z + 1, :] for k in range(coarse)]
        for c in range(3):
            u = hats[0] * shift[c][0]
            for k in range(1, coarse):
                u = u + hats[k] * shift[c][k]
            plane = plane + u * slopes[c]
        warped[z] = plane

    def fields(rows):
        i = [image[z, rows] for z in range(wide)]
        w = [warped[z, rows] for z in range(wide)]
        return (w, [b * b for b in w], [a * b for a, b in zip(i, w)])

    of = box_sums(fields, planes, side, sums, parts, box_ref)
    for z in range(planes):
        mean_w, mean_ww, mean_iw = [of(f, z) * (1.0 / 729.0) for f in range(3)]
        mean_i = mean_ref[z]
        sii = variance_ref[z]
        sww = mean_ww - mean_w * mean_w
        siw = mean_iw - mean_i * mean_w
        ratio = siw / (sii * sww + EPSILON)
        map_ref[z] = siw * ratio
        weight[z] = (2.0 * ratio) * (
            (image[z + REACH] - mean_i) - siw / (sww + EPSILON) * (warped[z + REACH] - mean_w)
        )
    row = force_message(
        lambda z: weight[z],
        lambda z: warped[z + REACH],
        planes, cells_ref, rows_ref, cols_ref, marks_ref,
    )
    message_ref[...] = jnp.broadcast_to(row[None], message_ref.shape)


def last_kernel(received_ref, velocity_ref, spread_ref, map_ref, out_ref, map_hbm, sem):
    copy = pltpu.make_async_copy(map_ref, map_hbm.at[0], sem)
    copy.start()
    _, coarse, rows, width = out_ref.shape
    coarse_rows = LANES // width
    block_rows = rows // coarse_rows
    grids = regular_grid(received_ref[...], spread_ref, block_rows, coarse_rows, width // GY)
    for r in range(block_rows):
        velocity = velocity_ref[8 * r : 8 * r + 8] + grids[r]
        for c in range(3):
            for k in range(coarse):
                g = c * coarse + k
                for a in range(coarse_rows):
                    out_ref[c, k, r * coarse_rows + a : r * coarse_rows + a + 1, :] = velocity[
                        g : g + 1, a * width : (a + 1) * width
                    ]
    copy.wait()


def far_pairs(blocks, parts):
    pairs = []
    for block in range(blocks):
        for part in range(1, parts - 1, 2):
            low, high = block * parts + part, block * parts + part + 1
            pairs += [(low, high), (high, low)]
        for part in (0, parts - 1):
            pairs.append((block * parts + part, (block ^ 1) * parts + part))
    return pairs


VMEM = pl.BlockSpec(memory_space=pltpu.VMEM)
HBM = pl.BlockSpec(memory_space=pl.ANY)


def call(kernel, outs, scratch, *operands, in_specs=None, out_specs=None):
    return pl.pallas_call(
        kernel,
        out_shape=[jax.ShapeDtypeStruct(shape, dtype) for shape, dtype in outs],
        in_specs=in_specs or [VMEM] * len(operands),
        out_specs=out_specs or [VMEM] * len(outs),
        scratch_shapes=scratch,
        compiler_params=pltpu.CompilerParams(vmem_limit_bytes=24 << 20),
    )(*operands)


def per_device(fixed, moving, block_place, tissue):
    slots, planes, side, width = fixed.shape
    assert slots == 1 and width == LANES
    depth_parts = lax.axis_size("gz")
    devices = lax.axis_size("blk") * depth_parts
    blocks = slots * lax.axis_size("blk")
    coarse = planes * depth_parts // SCALE
    coarse_rows, coarse_cols = side // SCALE, width // SCALE
    block_rows = blocks // GY
    wide = planes + 2 * REACH
    field = (planes, side, width)
    halo = ((2 * REACH + 1, side, width), BF16)

    near, far, fixed, moving = call(
        pack_kernel,
        [halo, halo, (field, BF16), (field, BF16)],
        [pltpu.SemaphoreType.DMA((2,))],
        pltpu.with_memory_space_constraint(fixed, pltpu.HBM),
        pltpu.with_memory_space_constraint(moving, pltpu.HBM),
        in_specs=[HBM] * 2,
    )
    far = lax.ppermute(far, ("blk", "gz"), far_pairs(lax.axis_size("blk"), depth_parts))
    pairs = [(i, i + 1) for i in range(0, depth_parts, 2)]
    near = lax.ppermute(near, "gz", pairs + [(b, a) for a, b in pairs])
    marks, hats, cells, rows, cols, box, slope, spread, hat_x, hat_y = call(
        functools.partial(table_kernel, planes=planes, block_rows=block_rows),
        [
            ((8, width), F32),
            ((coarse * wide, width), F32),
            ((coarse * planes, width), F32),
            ((coarse_rows, side, width), F32),
            ((width, 2 * width), BF16),
            ((2 * width, 2 * width), BF16),
            ((width, width), BF16),
            ((width, 3 * coarse * width), BF16),
            ((block_rows * coarse_rows, side, width), F32),
            ((width, coarse_rows * width), BF16),
        ],
        [],
        jnp.stack([block_place, tissue]),
    )

    message = ((devices, 1, LANES), F32)

    def scratch(fields):
        return [
            pltpu.VMEM((fields, planes, side, width), F32),
            pltpu.VMEM((3, fields * planes * side // 2, 2 * width), BF16),
            pltpu.VMEM(field, F32),
        ]

    images = [pltpu.VMEM((wide, side, width), F32), pltpu.VMEM((wide + 2, side, width), F32)]
    sent, mean, variance = call(
        first_kernel, [message, (field, F32), (field, F32)], images + scratch(5),
        fixed, moving, near, far, marks, cells, rows, cols, box,
    )
    received = lax.all_to_all(sent, ("blk", "gz"), 0, 0).reshape(devices, LANES)
    sent, correlation, velocity = call(
        second_kernel,
        [message, (field, F32), ((8 * block_rows, LANES), F32)],
        images + [pltpu.VMEM((wide, side, width), F32)] + scratch(3),
        received, fixed, moving, near, far, marks,
        mean, variance, hats, cells, rows, cols, box, slope, spread, hat_x, hat_y,
    )
    received = lax.all_to_all(sent, ("blk", "gz"), 0, 0).reshape(devices, LANES)
    return tuple(
        call(
            last_kernel,
            [
                ((3, coarse, block_rows * coarse_rows, GY * coarse_cols), F32),
                ((slots,) + field, F32),
            ],
            [pltpu.SemaphoreType.DMA(())],
            received, velocity, spread, correlation,
            out_specs=[VMEM, HBM],
        )
    )


def solution(mesh):
    return jax.shard_map(
        per_device,
        mesh=mesh,
        in_specs=(P("blk", "gz", None, None), P("blk", "gz", None, None), P("blk"), P("blk")),
        out_specs=(P(), P("blk", "gz", None, None)),
        check_vma=False,
    )
```

```python
import functools
import math

import jax
import jax.numpy as jnp
from jax import lax
from jax.experimental import pallas as pl
from jax.experimental.pallas import tpu as pltpu
from jax.sharding import PartitionSpec as P

SCALE = 16
GY = 8
EPSILON = 1e-05
STEP_LENGTH = 0.5
GAUSS_RAW = [math.exp(-((offset - 3) ** 2) / 4.5) for offset in range(7)]
GAUSS_TAPS = [value / sum(GAUSS_RAW) for value in GAUSS_RAW]
REACH = 4
PAD = 8
LANES = 128
F32 = jnp.float32
BF16 = jnp.bfloat16


def cell_weights(index, cell):
    total = jnp.zeros(index.shape, F32)
    for offset, weight in enumerate(GAUSS_TAPS):
        target = index + (offset - 3)
        inside = (target >= cell * SCALE) & (target < cell * SCALE + SCALE)
        total = total + jnp.where(inside, weight, 0.0)
    return total


def hat(index, cell, count):
    where = jnp.clip((index.astype(F32) + 0.5) * (1.0 / SCALE) - 0.5, 0.0, count - 1.0)
    return jnp.maximum(0.0, 1.0 - jnp.abs(where - cell.astype(F32)))


def lane_index(shape):
    return lax.broadcasted_iota(jnp.int32, shape, len(shape) - 1)


def sublane_index(shape):
    return lax.broadcasted_iota(jnp.int32, shape, len(shape) - 2)


def split(value, count):
    parts = []
    for _ in range(count):
        parts.append(value.astype(BF16))
        value = value - parts[-1].astype(F32)
    return parts


def exact_dot(value, table):
    rows = value.shape[0]
    stacked = jnp.concatenate(split(value, 3), axis=0)
    product = jnp.dot(stacked, table, preferred_element_type=F32)
    return product[:rows] + product[rows : 2 * rows] + product[2 * rows :]


def window_of_nine(items):
    two = [a + b for a, b in zip(items[:-1], items[1:])]
    four = [a + b for a, b in zip(two[:-2], two[2:])]
    eight = [a + b for a, b in zip(four[:-4], four[4:])]
    return [a + b for a, b in zip(eight[:-1], items[8:])]


def padded_rows(side):
    return slice(PAD, PAD + side)


def clear_edges(ref, side):
    edge = jnp.zeros(ref.shape[:-2] + (PAD, LANES), F32)
    ref[..., 0:PAD, :] = edge
    ref[..., PAD + side :, :] = edge


def row_box(padded, three, side):
    count = side + 8
    three[...] = (
        padded[PAD - 5 : PAD - 5 + count]
        + padded[PAD - 4 : PAD - 4 + count]
        + padded[PAD - 3 : PAD - 3 + count]
    )
    return three[1 : 1 + side] + three[4 : 4 + side] + three[7 : 7 + side]


def row_difference(padded, side):
    return padded[PAD + 1 : PAD + 1 + side] - padded[PAD - 1 : PAD - 1 + side]


def col_difference(plane):
    width = plane.shape[1]
    lane = lane_index(plane.shape)
    upper = jnp.where(lane < width - 1, pltpu.roll(plane, width - 1, 1), 0.0)
    lower = jnp.where(lane > 0, pltpu.roll(plane, 1, 1), 0.0)
    return upper - lower


def load_images(odd, fixed_ref, moving_ref, near_ref, far_ref, image, shifted):
    planes, side, _ = fixed_ref.shape
    rows = padded_rows(side)
    clear_edges(shifted, side)
    image[REACH : REACH + planes] = fixed_ref[...].astype(F32)
    shifted[REACH + 1 : REACH + 1 + planes, rows] = moving_ref[...].astype(F32)
    for ref, low in ((near_ref, odd), (far_ref, ~odd)):
        start = jnp.where(low, 0, REACH + planes)
        image[pl.ds(start, REACH)] = ref[0:REACH].astype(F32)
        start = jnp.where(low, 0, REACH + 1 + planes)
        shifted[pl.ds(start, REACH + 1), rows] = ref[REACH:].astype(F32)


def box_sums(fields, planes, side, sums, threes, parts, box_ref):
    half = planes // 2
    count = sums.shape[0]
    clear_edges(sums, side)
    for tile in range(side // 8):
        for f, items in enumerate(fields(8 * tile)):
            for z, item in enumerate(window_of_nine(items)):
                sums[f, z, PAD + 8 * tile : PAD + 8 * tile + 8] = item
    for f in range(count):
        for z in range(planes):
            total = row_box(sums.at[f, z], threes.at[f, z], side)
            rows = slice((f * half + z % half) * side, (f * half + z % half + 1) * side)
            for part, rounded in enumerate(split(total, 3)):
                lane = (2 * part + z // half) * LANES
                parts[rows, lane : lane + LANES] = rounded
    result = jnp.dot(parts[...], box_ref[...], preferred_element_type=F32)

    def of(f, z):
        start = (f * half + z % half) * side
        lane = (z // half) * LANES
        return result[start : start + side, lane : lane + LANES]

    return of


def force_message(weights, warped, planes, cells_ref, rows_ref, cols_ref, marks_ref):
    coarse = cells_ref.shape[0] // planes
    coarse_rows, side, _ = rows_ref.shape
    rows = padded_rows(side)
    total = [[None] * coarse for _ in range(3)]
    for z in range(planes):
        slopes = (
            warped(z + 1)[rows] - warped(z - 1)[rows],
            row_difference(warped(z), side),
            col_difference(warped(z)[rows]),
        )
        for k in range(coarse):
            index = k * planes + z
            share = weights(z) * cells_ref[index : index + 1, :]
            for c in range(3):
                term = share * slopes[c]
                total[c][k] = term if z == 0 else total[c][k] + term
    tiles = []
    for c in range(3):
        for k in range(coarse):
            for a in range(coarse_rows):
                product = total[c][k] * rows_ref[a]
                tile = product[0:8]
                for start in range(8, side, 8):
                    tile = tile + product[start : start + 8]
                tiles.append(tile)
    sums = exact_dot(jnp.concatenate(tiles, axis=0), cols_ref[...])
    sums = sums[:, :LANES] + sums[:, LANES:]
    coarse_cols = LANES // SCALE
    lane = lane_index((8, LANES))
    picked = jnp.zeros((8, LANES), F32)
    for g in range(len(tiles)):
        picked = jnp.where(lane // coarse_cols == g, sums[8 * g : 8 * g + 8], picked)
    row = jnp.sum(picked, axis=0, keepdims=True) * marks_ref[1:2]
    return jnp.where(lane[0:1] == len(tiles) * coarse_cols, marks_ref[0:1], row)


def regular_grid(received, spread_ref, block_rows, coarse_rows, coarse_cols):
    groups = spread_ref.shape[1] // LANES
    used = groups * coarse_rows * coarse_cols
    width = GY * coarse_cols
    place = received[:, used : used + 1].astype(jnp.int32)
    lane = lane_index(received.shape)
    here = (place % GY) == (lane % width) // coarse_cols
    block_row = place // GY
    sub = sublane_index((8, LANES))
    grids = [jnp.zeros((8, LANES), F32) for _ in range(block_rows)]
    entries = exact_dot(received, spread_ref[...])
    for g in range(groups):
        entry = entries[:, g * LANES : (g + 1) * LANES]
        for r in range(block_rows):
            chosen = here if block_rows == 1 else here & (block_row == r)
            total = jnp.sum(jnp.where(chosen, entry, 0.0), axis=0, keepdims=True)
            grids[r] = jnp.where(sub == g, total, grids[r])
    even = sub % 2 == 0
    lane = lane_index((8, LANES))
    column = lane % width
    first = lane < width
    grids = [
        0.5 * g + 0.25 * jnp.where(even, pltpu.roll(g, 7, 0), pltpu.roll(g, 1, 0)) for g in grids
    ]
    other = [pltpu.roll(g, width, 1) for g in grids]
    none = jnp.zeros((8, LANES), F32)
    before = [none] + other[:-1]
    after = other[1:] + [none]
    grids = [
        0.5 * g + 0.25 * (o + jnp.where(first, b, a))
        for g, o, b, a in zip(grids, other, before, after)
    ]
    grids = [
        0.25 * jnp.where(column > 0, pltpu.roll(g, 1, 1), 0.0)
        + 0.5 * g
        + 0.25 * jnp.where(column < width - 1, pltpu.roll(g, LANES - 1, 1), 0.0)
        for g in grids
    ]
    grids = [jnp.where(sub < groups, g, 0.0) for g in grids]
    square = functools.reduce(lambda a, b: a + b, [g * g for g in grids])
    square = jnp.sum(jnp.sum(square, axis=1, keepdims=True), axis=0, keepdims=True)
    mean = square * (1.0 / (groups * block_rows * LANES))
    factor = STEP_LENGTH / jnp.sqrt(mean + EPSILON)
    return [g * factor for g in grids]


def pack_kernel(fixed_hbm, moving_hbm, near_ref, far_ref, fixed_ref, moving_ref, sems):
    copies = [
        pltpu.make_async_copy(source.at[0], target, sems.at[i])
        for i, (source, target) in enumerate(((fixed_hbm, fixed_ref), (moving_hbm, moving_ref)))
    ]
    for copy in copies:
        copy.start()
    planes = fixed_ref.shape[0]
    part = lax.axis_index("gz")
    odd = part % 2
    inner = (part > 0) & (part < lax.axis_size("gz") - 1)
    for copy in copies:
        copy.wait()
    for ref, low, keep in ((far_ref, odd == 0, inner), (near_ref, odd == 1, None)):
        i = fixed_ref[pl.ds(jnp.where(low, 0, planes - REACH), REACH)]
        j = moving_ref[pl.ds(jnp.where(low, 0, planes - REACH - 1), REACH + 1)]
        if keep is not None:
            i = jnp.where(keep, i.astype(F32), 0.0).astype(BF16)
            j = jnp.where(keep, j.astype(F32), 0.0).astype(BF16)
        ref[0:REACH] = i
        ref[REACH:] = j


def table_kernel(
    both_ref,
    marks_ref, hats_ref, cells_ref, rows_ref, cols_ref, box_ref, slope_ref, spread_ref, hat_x_ref, hat_y_ref,
    *, planes, block_rows,
):
    part = lax.axis_index("gz")
    total = planes * lax.axis_size("gz")
    coarse_rows, side, _ = rows_ref.shape
    coarse_cols = LANES // SCALE
    width = GY * coarse_cols
    wide = planes + 2 * REACH
    row = sublane_index(hats_ref.shape)
    z = part * planes + row % wide - REACH
    hats_ref[...] = jnp.where((z >= 0) & (z < total), hat(z, row // wide, total // SCALE), 0.0)
    row = sublane_index(cells_ref.shape)
    cells_ref[...] = cell_weights(part * planes + row % planes, row // planes)
    for a in range(coarse_rows):
        rows_ref[a] = 0.5 * cell_weights(sublane_index((side, LANES)), a)
    square = (LANES, LANES)
    cols = cell_weights(sublane_index(square), lane_index(square) % coarse_cols)
    for i, value in enumerate(split(cols, 2)):
        cols_ref[:, i * LANES : (i + 1) * LANES] = value
    apart = sublane_index(square) - lane_index(square)
    band = jnp.where(jnp.abs(apart) <= 4, 1.0, 0.0).astype(BF16)
    box_ref[...] = jnp.zeros(box_ref.shape, BF16)
    for i in range(6):
        lane = (i % 2) * LANES
        box_ref[i * LANES : (i + 1) * LANES, lane : lane + LANES] = band
    slope_ref[...] = jnp.where(apart == 1, 1.0, jnp.where(apart == -1, -1.0, 0.0)).astype(BF16)
    lane = lane_index(square)
    source = (lane // width) * coarse_cols + lane % coarse_cols
    for g in range(spread_ref.shape[1] // LANES):
        hit = sublane_index(square) == source + g * coarse_rows * coarse_cols
        spread_ref[:, g * LANES : (g + 1) * LANES] = jnp.where(hit, 1.0, 0.0).astype(BF16)
    row = sublane_index(marks_ref.shape)
    marks_ref[...] = jnp.where(row == 0, both_ref[0:1, 0:1], both_ref[1:2, 0:1]).astype(F32)
    place = both_ref[0:1, 0:1]
    y = lane + (place % GY) * LANES
    entry = sublane_index(square)
    hat_y = hat(y, entry % width, width)
    for a in range(coarse_rows):
        chosen = jnp.where(entry // width == a, hat_y, 0.0).astype(BF16)
        hat_y_ref[:, a * LANES : (a + 1) * LANES] = chosen
    x = sublane_index((side, LANES)) + (place // GY) * side
    for r in range(block_rows * coarse_rows):
        hat_x_ref[r] = 0.5 * hat(x, jnp.full((1, 1), r, jnp.int32), block_rows * coarse_rows)


def first_kernel(
    fixed_ref, moving_ref, near_ref, far_ref, marks_ref,
    cells_ref, rows_ref, cols_ref, box_ref,
    message_ref, mean_ref, variance_ref,
    image, shifted, sums, threes, parts, weight,
):
    planes, side, _ = fixed_ref.shape
    odd = lax.axis_index("gz") % 2 == 1
    load_images(odd, fixed_ref, moving_ref, near_ref, far_ref, image, shifted)
    wide = planes + 2 * REACH

    def fields(start):
        i = [image[z, start : start + 8] for z in range(wide)]
        w = [shifted[z + 1, PAD + start : PAD + start + 8] for z in range(wide)]
        return (
            i,
            w,
            [a * a for a in i],
            [b * b for b in w],
            [a * b for a, b in zip(i, w)],
        )

    of = box_sums(fields, planes, side, sums, threes, parts, box_ref)
    for z in range(planes):
        mean_i, mean_w, mean_ii, mean_ww, mean_iw = [of(f, z) * (1.0 / 729.0) for f in range(5)]
        sii = mean_ii - mean_i * mean_i
        sww = mean_ww - mean_w * mean_w
        siw = mean_iw - mean_i * mean_w
        mean_ref[z] = mean_i
        variance_ref[z] = sii
        ratio = siw / (sii * sww + EPSILON)
        weight[z] = (2.0 * ratio) * (
            (image[z + REACH] - mean_i)
            - siw / (sww + EPSILON) * (shifted[z + REACH + 1, padded_rows(side)] - mean_w)
        )
    row = force_message(
        lambda z: weight[z],
        lambda z: shifted.at[z + REACH + 1],
        planes, cells_ref, rows_ref, cols_ref, marks_ref,
    )
    message_ref[...] = jnp.broadcast_to(row[None], message_ref.shape)


def second_kernel(
    received_ref, fixed_ref, moving_ref, near_ref, far_ref, marks_ref,
    mean_ref, variance_ref, hats_ref, cells_ref, rows_ref, cols_ref, box_ref, slope_ref,
    spread_ref, hat_x_ref, hat_y_ref,
    message_ref, map_ref, velocity_ref,
    image, shifted, warped, sums, threes, parts, weight,
):
    planes, side, _ = fixed_ref.shape
    odd = lax.axis_index("gz") % 2 == 1
    load_images(odd, fixed_ref, moving_ref, near_ref, far_ref, image, shifted)
    wide = planes + 2 * REACH
    coarse_rows = rows_ref.shape[0]
    coarse_cols = LANES // SCALE
    block_rows = velocity_ref.shape[0] // 8
    coarse = hats_ref.shape[0] // wide

    grids = regular_grid(received_ref[...], spread_ref, block_rows, coarse_rows, coarse_cols)
    for r in range(block_rows):
        velocity_ref[8 * r : 8 * r + 8] = grids[r]
    along = exact_dot(jnp.concatenate(grids, axis=0), hat_y_ref[...])
    shift = [[None] * coarse for _ in range(3)]
    for r in range(block_rows):
        for a in range(coarse_rows):
            hat_x = hat_x_ref[r * coarse_rows + a]
            for c in range(3):
                for k in range(coarse):
                    g = 8 * r + c * coarse + k
                    term = hat_x * along[g : g + 1, a * LANES : (a + 1) * LANES]
                    shift[c][k] = term if r + a == 0 else shift[c][k] + term
    rows = padded_rows(side)
    inner = shifted[1 : wide + 1, rows].reshape(wide * side, LANES).astype(BF16)
    across = jnp.dot(inner, slope_ref[...], preferred_element_type=F32)
    for z in range(wide):
        plane = shifted[z + 1, rows]
        slopes = (
            shifted[z + 2, rows] - shifted[z, rows],
            row_difference(shifted.at[z + 1], side),
            across[z * side : (z + 1) * side],
        )
        hats = [hats_ref[k * wide + z : k * wide + z + 1, :] for k in range(coarse)]
        for c in range(3):
            u = hats[0] * shift[c][0]
            for k in range(1, coarse):
                u = u + hats[k] * shift[c][k]
            plane = plane + u * slopes[c]
        warped[z, rows] = plane
    clear_edges(warped, side)

    def fields(start):
        i = [image[z, start : start + 8] for z in range(wide)]
        w = [warped[z, PAD + start : PAD + start + 8] for z in range(wide)]
        return (w, [b * b for b in w], [a * b for a, b in zip(i, w)])

    of = box_sums(fields, planes, side, sums, threes, parts, box_ref)
    for z in range(planes):
        mean_w, mean_ww, mean_iw = [of(f, z) * (1.0 / 729.0) for f in range(3)]
        mean_i = mean_ref[z]
        sii = variance_ref[z]
        sww = mean_ww - mean_w * mean_w
        siw = mean_iw - mean_i * mean_w
        ratio = siw / (sii * sww + EPSILON)
        map_ref[z] = siw * ratio
        weight[z] = (2.0 * ratio) * (
            (image[z + REACH] - mean_i) - siw / (sww + EPSILON) * (warped[z + REACH, padded_rows(side)] - mean_w)
        )
    row = force_message(
        lambda z: weight[z],
        lambda z: warped.at[z + REACH],
        planes, cells_ref, rows_ref, cols_ref, marks_ref,
    )
    message_ref[...] = jnp.broadcast_to(row[None], message_ref.shape)


def last_kernel(received_ref, velocity_ref, spread_ref, map_ref, out_ref, map_hbm, sem):
    copy = pltpu.make_async_copy(map_ref, map_hbm.at[0], sem)
    copy.start()
    _, coarse, rows, width = out_ref.shape
    coarse_rows = LANES // width
    block_rows = rows // coarse_rows
    grids = regular_grid(received_ref[...], spread_ref, block_rows, coarse_rows, width // GY)
    for r in range(block_rows):
        velocity = velocity_ref[8 * r : 8 * r + 8] + grids[r]
        for c in range(3):
            for k in range(coarse):
                g = c * coarse + k
                for a in range(coarse_rows):
                    out_ref[c, k, r * coarse_rows + a : r * coarse_rows + a + 1, :] = velocity[
                        g : g + 1, a * width : (a + 1) * width
                    ]
    copy.wait()


def far_pairs(blocks, parts):
    pairs = []
    for block in range(blocks):
        for part in range(1, parts - 1, 2):
            low, high = block * parts + part, block * parts + part + 1
            pairs += [(low, high), (high, low)]
        for part in (0, parts - 1):
            pairs.append((block * parts + part, (block ^ 1) * parts + part))
    return pairs


VMEM = pl.BlockSpec(memory_space=pltpu.VMEM)
HBM = pl.BlockSpec(memory_space=pl.ANY)


def call(kernel, outs, scratch, *operands, in_specs=None, out_specs=None):
    return pl.pallas_call(
        kernel,
        out_shape=[jax.ShapeDtypeStruct(shape, dtype) for shape, dtype in outs],
        in_specs=in_specs or [VMEM] * len(operands),
        out_specs=out_specs or [VMEM] * len(outs),
        scratch_shapes=scratch,
        compiler_params=pltpu.CompilerParams(vmem_limit_bytes=24 << 20),
    )(*operands)


def per_device(fixed, moving, block_place, tissue):
    slots, planes, side, width = fixed.shape
    assert slots == 1 and width == LANES
    depth_parts = lax.axis_size("gz")
    devices = lax.axis_size("blk") * depth_parts
    blocks = slots * lax.axis_size("blk")
    coarse = planes * depth_parts // SCALE
    coarse_rows, coarse_cols = side // SCALE, width // SCALE
    block_rows = blocks // GY
    wide = planes + 2 * REACH
    field = (planes, side, width)
    halo = ((2 * REACH + 1, side, width), BF16)

    near, far, fixed, moving = call(
        pack_kernel,
        [halo, halo, (field, BF16), (field, BF16)],
        [pltpu.SemaphoreType.DMA((2,))],
        pltpu.with_memory_space_constraint(fixed, pltpu.HBM),
        pltpu.with_memory_space_constraint(moving, pltpu.HBM),
        in_specs=[HBM] * 2,
    )
    far = lax.ppermute(far, ("blk", "gz"), far_pairs(lax.axis_size("blk"), depth_parts))
    pairs = [(i, i + 1) for i in range(0, depth_parts, 2)]
    near = lax.ppermute(near, "gz", pairs + [(b, a) for a, b in pairs])
    marks, hats, cells, rows, cols, box, slope, spread, hat_x, hat_y = call(
        functools.partial(table_kernel, planes=planes, block_rows=block_rows),
        [
            ((8, width), F32),
            ((coarse * wide, width), F32),
            ((coarse * planes, width), F32),
            ((coarse_rows, side, width), F32),
            ((width, 2 * width), BF16),
            ((6 * width, 2 * width), BF16),
            ((width, width), BF16),
            ((width, 3 * coarse * width), BF16),
            ((block_rows * coarse_rows, side, width), F32),
            ((width, coarse_rows * width), BF16),
        ],
        [],
        jnp.stack([block_place, tissue]),
    )

    message = ((devices, 1, LANES), F32)

    def scratch(fields):
        return [
            pltpu.VMEM((fields, planes, side + 2 * PAD, width), F32),
            pltpu.VMEM((fields, planes, side + 8, width), F32),
            pltpu.VMEM((fields * planes * side // 2, 6 * width), BF16),
            pltpu.VMEM(field, F32),
        ]

    images = [
        pltpu.VMEM((wide, side, width), F32),
        pltpu.VMEM((wide + 2, side + 2 * PAD, width), F32),
    ]
    sent, mean, variance = call(
        first_kernel, [message, (field, F32), (field, F32)], images + scratch(5),
        fixed, moving, near, far, marks, cells, rows, cols, box,
    )
    received = lax.all_to_all(sent, ("blk", "gz"), 0, 0).reshape(devices, LANES)
    sent, correlation, velocity = call(
        second_kernel,
        [message, (field, F32), ((8 * block_rows, LANES), F32)],
        images + [pltpu.VMEM((wide, side + 2 * PAD, width), F32)] + scratch(3),
        received, fixed, moving, near, far, marks,
        mean, variance, hats, cells, rows, cols, box, slope, spread, hat_x, hat_y,
    )
    received = lax.all_to_all(sent, ("blk", "gz"), 0, 0).reshape(devices, LANES)
    return tuple(
        call(
            last_kernel,
            [
                ((3, coarse, block_rows * coarse_rows, GY * coarse_cols), F32),
                ((slots,) + field, F32),
            ],
            [pltpu.SemaphoreType.DMA(())],
            received, velocity, spread, correlation,
            out_specs=[VMEM, HBM],
        )
    )


def solution(mesh):
    return jax.shard_map(
        per_device,
        mesh=mesh,
        in_specs=(P("blk", "gz", None, None), P("blk", "gz", None, None), P("blk"), P("blk")),
        out_specs=(P(), P("blk", "gz", None, None)),
        check_vma=False,
    )
```

```python
import functools
import math

import jax
import jax.numpy as jnp
from jax import lax
from jax.experimental import pallas as pl
from jax.experimental.pallas import tpu as pltpu
from jax.sharding import PartitionSpec as P

SCALE = 16
GY = 8
EPSILON = 1e-05
STEP_LENGTH = 0.5
GAUSS_RAW = [math.exp(-((offset - 3) ** 2) / 4.5) for offset in range(7)]
GAUSS_TAPS = [value / sum(GAUSS_RAW) for value in GAUSS_RAW]
REACH = 4
PAD = 8
LANES = 128
F32 = jnp.float32
BF16 = jnp.bfloat16


def cell_weights(index, cell):
    total = jnp.zeros(index.shape, F32)
    for offset, weight in enumerate(GAUSS_TAPS):
        target = index + (offset - 3)
        inside = (target >= cell * SCALE) & (target < cell * SCALE + SCALE)
        total = total + jnp.where(inside, weight, 0.0)
    return total


def hat(index, cell, count):
    where = jnp.clip((index.astype(F32) + 0.5) * (1.0 / SCALE) - 0.5, 0.0, count - 1.0)
    return jnp.maximum(0.0, 1.0 - jnp.abs(where - cell.astype(F32)))


def lane_index(shape):
    return lax.broadcasted_iota(jnp.int32, shape, len(shape) - 1)


def sublane_index(shape):
    return lax.broadcasted_iota(jnp.int32, shape, len(shape) - 2)


def split(value, count):
    parts = []
    for _ in range(count):
        parts.append(value.astype(BF16))
        value = value - parts[-1].astype(F32)
    return parts


def exact_dot(value, table):
    rows = value.shape[0]
    stacked = jnp.concatenate(split(value, 3), axis=0)
    product = jnp.dot(stacked, table, preferred_element_type=F32)
    return product[:rows] + product[rows : 2 * rows] + product[2 * rows :]


def window_of_nine(items):
    two = [a + b for a, b in zip(items[:-1], items[1:])]
    four = [a + b for a, b in zip(two[:-2], two[2:])]
    eight = [a + b for a, b in zip(four[:-4], four[4:])]
    return [a + b for a, b in zip(eight[:-1], items[8:])]


def padded_rows(side):
    return slice(PAD, PAD + side)


def clear_edges(ref, side):
    edge = jnp.zeros(ref.shape[:-2] + (PAD, LANES), F32)
    ref[..., 0:PAD, :] = edge
    ref[..., PAD + side :, :] = edge


def row_box(padded, three, side):
    count = side + 8
    three[...] = (
        padded[PAD - 5 : PAD - 5 + count]
        + padded[PAD - 4 : PAD - 4 + count]
        + padded[PAD - 3 : PAD - 3 + count]
    )
    return three[1 : 1 + side] + three[4 : 4 + side] + three[7 : 7 + side]


def row_difference(padded, side):
    return padded[PAD + 1 : PAD + 1 + side] - padded[PAD - 1 : PAD - 1 + side]


def col_difference(plane):
    width = plane.shape[1]
    lane = lane_index(plane.shape)
    upper = jnp.where(lane < width - 1, pltpu.roll(plane, width - 1, 1), 0.0)
    lower = jnp.where(lane > 0, pltpu.roll(plane, 1, 1), 0.0)
    return upper - lower


def load_images(odd, fixed_ref, moving_ref, near_ref, far_ref, halves, image, shifted):
    planes, side, _ = fixed_ref.shape
    rows = padded_rows(side)
    below = jnp.where(odd, 0, 1)
    halves[below] = near_ref[...]
    halves[1 - below] = far_ref[...]
    clear_edges(shifted, side)
    image[0:REACH] = halves[0, 0:REACH].astype(F32)
    image[REACH : REACH + planes] = fixed_ref[...].astype(F32)
    image[REACH + planes :] = halves[1, 0:REACH].astype(F32)
    shifted[0 : REACH + 1, rows] = halves[0, REACH:].astype(F32)
    shifted[REACH + 1 : REACH + 1 + planes, rows] = moving_ref[...].astype(F32)
    shifted[REACH + 1 + planes :, rows] = halves[1, REACH:].astype(F32)


def box_sums(fields, planes, side, sums, threes, parts, box_ref):
    half = planes // 2
    count = sums.shape[0]
    clear_edges(sums, side)
    for tile in range(side // 8):
        for f, items in enumerate(fields(8 * tile)):
            for z, item in enumerate(window_of_nine(items)):
                sums[f, z, PAD + 8 * tile : PAD + 8 * tile + 8] = item
    for f in range(count):
        for z in range(planes):
            total = row_box(sums.at[f, z], threes.at[f, z], side)
            rows = slice((f * half + z % half) * side, (f * half + z % half + 1) * side)
            for part, rounded in enumerate(split(total, 3)):
                lane = (2 * part + z // half) * LANES
                parts[rows, lane : lane + LANES] = rounded
    result = jnp.dot(parts[...], box_ref[...], preferred_element_type=F32)

    def of(f, z):
        start = (f * half + z % half) * side
        lane = (z // half) * LANES
        return result[start : start + side, lane : lane + LANES]

    return of


def column_boxes(fixed, moving, side, single, double, box_ref):
    for i in range(REACH):
        for h in range(2):
            lane = h * LANES
            planes = (fixed(i, h), moving(i, h))
            for f, plane in enumerate(planes):
                start = (f * REACH + i) * side
                single[start : start + side, lane : lane + LANES] = plane
            a, b = (plane.astype(F32) for plane in planes)
            for f, product in enumerate((a * a, b * b, a * b)):
                start = (f * REACH + i) * side
                high, low = split(product, 2)
                double[start : start + side, lane : lane + LANES] = high
                double[start : start + side, 2 * LANES + lane : 3 * LANES + lane] = low
    ones = jnp.dot(single[...], box_ref[0 : 2 * LANES], preferred_element_type=F32)
    twos = jnp.dot(double[...], box_ref[0 : 4 * LANES], preferred_element_type=F32)

    def of(f, i, h):
        source, f = (ones, f) if f < 2 else (twos, f - 2)
        start = (f * REACH + i) * side
        return source[start : start + side, h * LANES : (h + 1) * LANES]

    return of


def running(items):
    total = [items[0]]
    for item in items[1:]:
        total.append(total[-1] + item)
    return total


def force_message(weights, warped, planes, cells_ref, rows_ref, cols_ref, marks_ref):
    coarse = cells_ref.shape[0] // planes
    coarse_rows, side, _ = rows_ref.shape
    rows = padded_rows(side)
    total = [[None] * coarse for _ in range(3)]
    for z in range(planes):
        slopes = (
            warped(z + 1)[rows] - warped(z - 1)[rows],
            row_difference(warped(z), side),
            col_difference(warped(z)[rows]),
        )
        for k in range(coarse):
            index = k * planes + z
            share = weights(z) * cells_ref[index : index + 1, :]
            for c in range(3):
                term = share * slopes[c]
                total[c][k] = term if z == 0 else total[c][k] + term
    tiles = []
    for c in range(3):
        for k in range(coarse):
            for a in range(coarse_rows):
                product = total[c][k] * rows_ref[a]
                tile = product[0:8]
                for start in range(8, side, 8):
                    tile = tile + product[start : start + 8]
                tiles.append(tile)
    sums = exact_dot(jnp.concatenate(tiles, axis=0), cols_ref[...])
    sums = sums[:, :LANES] + sums[:, LANES:]
    coarse_cols = LANES // SCALE
    lane = lane_index((8, LANES))
    picked = jnp.zeros((8, LANES), F32)
    for g in range(len(tiles)):
        picked = jnp.where(lane // coarse_cols == g, sums[8 * g : 8 * g + 8], picked)
    row = jnp.sum(picked, axis=0, keepdims=True) * marks_ref[1:2]
    return jnp.where(lane[0:1] == len(tiles) * coarse_cols, marks_ref[0:1], row)


def regular_grid(received, spread_ref, coarse, block_rows, coarse_rows, coarse_cols):
    groups = 3 * coarse
    used = groups * coarse_rows * coarse_cols
    width = GY * coarse_cols
    place = received[:, used : used + 1].astype(jnp.int32)
    here = (place % GY) == lane_index(received.shape) // coarse_cols
    block_row = place // GY
    sub = sublane_index((8, LANES))
    entries = exact_dot(received, spread_ref[...])
    grids = []
    for r in range(block_rows):
        chosen = here if block_rows == 1 else here & (block_row == r)
        for a in range(coarse_rows):
            grid = jnp.zeros((8, LANES), F32)
            for g in range(groups):
                start = (a * groups + g) * LANES
                entry = jnp.where(chosen, entries[:, start : start + LANES], 0.0)
                grid = jnp.where(sub == g, jnp.sum(entry, axis=0, keepdims=True), grid)
            grids.append(grid)
    none = [jnp.zeros((8, LANES), F32)]
    grids = [
        0.5 * g + 0.25 * (before + after)
        for g, before, after in zip(grids, none + grids[:-1], grids[1:] + none)
    ]
    inside = lane_index((8, LANES)) < width
    grids = [
        jnp.where(
            inside, 0.5 * g + 0.25 * (pltpu.roll(g, 1, 1) + pltpu.roll(g, LANES - 1, 1)), 0.0
        )
        for g in grids
    ]
    square = functools.reduce(lambda a, b: a + b, [g * g for g in grids])
    square = jnp.sum(jnp.sum(square, axis=0, keepdims=True), axis=1, keepdims=True)
    mean = square * (1.0 / (groups * len(grids) * width))
    factor = STEP_LENGTH / jnp.sqrt(mean + EPSILON)
    return [g * factor for g in grids]


def pack_kernel(fixed_hbm, moving_hbm, near_ref, far_ref, fixed_ref, moving_ref, sems):
    copies = [
        pltpu.make_async_copy(source.at[0], target, sems.at[i])
        for i, (source, target) in enumerate(((fixed_hbm, fixed_ref), (moving_hbm, moving_ref)))
    ]
    for copy in copies:
        copy.start()
    planes = fixed_ref.shape[0]
    part = lax.axis_index("gz")
    odd = part % 2
    inner = (part > 0) & (part < lax.axis_size("gz") - 1)
    for copy in copies:
        copy.wait()
    for ref, low, keep in ((far_ref, odd == 0, inner), (near_ref, odd == 1, None)):
        i = fixed_ref[pl.ds(jnp.where(low, 0, planes - REACH), REACH)]
        j = moving_ref[pl.ds(jnp.where(low, 0, planes - REACH - 1), REACH + 1)]
        if keep is not None:
            i = jnp.where(keep, i.astype(F32), 0.0).astype(BF16)
            j = jnp.where(keep, j.astype(F32), 0.0).astype(BF16)
        ref[0:REACH] = i
        ref[REACH:] = j


def table_kernel(
    both_ref, fixed_ref, moving_ref,
    marks_ref, hats_ref, cells_ref, rows_ref, cols_ref, box_ref, slope_ref, spread_ref, hat_x_ref, hat_y_ref,
    own_ref, single, double, sums, threes,
    *, block_rows,
):
    planes = fixed_ref.shape[0]
    part = lax.axis_index("gz")
    total = planes * lax.axis_size("gz")
    coarse_rows, side, _ = rows_ref.shape
    coarse_cols = LANES // SCALE
    width = GY * coarse_cols
    wide = planes + 2 * REACH
    row = sublane_index(hats_ref.shape)
    z = part * planes + row % wide - REACH
    hats_ref[...] = jnp.where((z >= 0) & (z < total), hat(z, row // wide, total // SCALE), 0.0)
    row = sublane_index(cells_ref.shape)
    cells_ref[...] = cell_weights(part * planes + row % planes, row // planes)
    for a in range(coarse_rows):
        rows_ref[a] = 0.5 * cell_weights(sublane_index((side, LANES)), a)
    square = (LANES, LANES)
    cols = cell_weights(sublane_index(square), lane_index(square) % coarse_cols)
    for i, value in enumerate(split(cols, 2)):
        cols_ref[:, i * LANES : (i + 1) * LANES] = value
    apart = sublane_index(square) - lane_index(square)
    band = jnp.where(jnp.abs(apart) <= 4, 1.0, 0.0).astype(BF16)
    box_ref[...] = jnp.zeros(box_ref.shape, BF16)
    for i in range(6):
        lane = (i % 2) * LANES
        box_ref[i * LANES : (i + 1) * LANES, lane : lane + LANES] = band
    slope_ref[...] = jnp.where(apart == 1, 1.0, jnp.where(apart == -1, -1.0, 0.0)).astype(BF16)
    lane = lane_index(square)
    entry = sublane_index(square)
    coarse = total // SCALE
    group = coarse_rows * coarse_cols
    for a in range(coarse_rows):
        for c in range(3):
            for k in range(coarse):
                value = jnp.zeros(square, F32)
                for other, weight in ((k - 1, 0.25), (k, 0.5), (k + 1, 0.25)):
                    if 0 <= other < coarse:
                        start = (c * coarse + other) * group + a * coarse_cols
                        hit = (entry == start + lane % coarse_cols) & (lane < width)
                        value = jnp.where(hit, weight, value)
                start = ((a * 3 + c) * coarse + k) * LANES
                spread_ref[:, start : start + LANES] = value.astype(BF16)
    row = sublane_index(marks_ref.shape)
    marks_ref[...] = jnp.where(row == 0, both_ref[0:1, 0:1], both_ref[1:2, 0:1]).astype(F32)
    place = both_ref[0:1, 0:1]
    y = lane + (place % GY) * LANES
    hat_y_ref[...] = jnp.where(entry < width, hat(y, entry, width), 0.0).astype(BF16)
    x = sublane_index((side, LANES)) + (place // GY) * side
    for r in range(block_rows * coarse_rows):
        hat_x_ref[r] = 0.5 * hat(x, jnp.full((1, 1), r, jnp.int32), block_rows * coarse_rows)

    of = column_boxes(
        lambda i, h: fixed_ref[i + REACH * h],
        lambda i, h: moving_ref[i + REACH * h],
        side, single, double, box_ref,
    )
    clear_edges(sums, side)
    for f in range(5):
        boxed = [of(f, i, h) for h in range(2) for i in range(REACH)]
        up, down = running(boxed), running(boxed[::-1])[::-1]
        for z in range(planes):
            sums[f, z, padded_rows(side)] = up[z + REACH] if z < REACH else down[z - REACH]
            own_ref[f, z] = row_box(sums.at[f, z], threes.at[f, z], side)


def first_kernel(
    fixed_ref, moving_ref, near_ref, far_ref, marks_ref,
    cells_ref, rows_ref, cols_ref, box_ref, own_ref,
    message_ref, mean_ref, variance_ref, image, shifted,
    halves, single, double, sums, threes, weight,
):
    planes, side, _ = fixed_ref.shape
    odd = lax.axis_index("gz") % 2 == 1
    load_images(odd, fixed_ref, moving_ref, near_ref, far_ref, halves, image, shifted)
    of = column_boxes(
        lambda i, h: halves[h, i],
        lambda i, h: halves[h, REACH + i + 1 - h],
        side, single, double, box_ref,
    )
    clear_edges(sums, side)
    for f in range(5):
        below = running([of(f, i, 0) for i in range(REACH)][::-1])[::-1]
        above = running([of(f, i, 1) for i in range(REACH)])
        for z, item in enumerate(below + above):
            sums[f, z, padded_rows(side)] = item
    for z in range(planes):
        mean_i, mean_w, mean_ii, mean_ww, mean_iw = [
            (row_box(sums.at[f, z], threes.at[f, z], side) + own_ref[f, z]) * (1.0 / 729.0)
            for f in range(5)
        ]
        sii = mean_ii - mean_i * mean_i
        sww = mean_ww - mean_w * mean_w
        siw = mean_iw - mean_i * mean_w
        mean_ref[z] = mean_i
        variance_ref[z] = sii
        ratio = siw / (sii * sww + EPSILON)
        weight[z] = (2.0 * ratio) * (
            (image[z + REACH] - mean_i)
            - siw / (sww + EPSILON) * (shifted[z + REACH + 1, padded_rows(side)] - mean_w)
        )
    row = force_message(
        lambda z: weight[z],
        lambda z: shifted.at[z + REACH + 1],
        planes, cells_ref, rows_ref, cols_ref, marks_ref,
    )
    message_ref[...] = jnp.broadcast_to(row[None], message_ref.shape)


def second_kernel(
    received_ref, image, shifted, marks_ref,
    mean_ref, variance_ref, hats_ref, cells_ref, rows_ref, cols_ref, box_ref, slope_ref,
    spread_ref, hat_x_ref, hat_y_ref,
    message_ref, map_ref, velocity_ref,
    slopes, warped, sums, threes, parts, weight,
):
    planes, side, _ = mean_ref.shape
    wide = planes + 2 * REACH
    coarse_rows = rows_ref.shape[0]
    coarse_cols = LANES // SCALE
    block_rows = velocity_ref.shape[0] // 8 // coarse_rows
    coarse = hats_ref.shape[0] // wide
    rows = padded_rows(side)
    inner = shifted[1 : wide + 1, rows].reshape(wide * side, LANES).astype(BF16)
    across = jnp.dot(inner, slope_ref[...], preferred_element_type=F32)
    for z in range(wide):
        slopes[0, z] = shifted[z + 2, rows] - shifted[z, rows]
        slopes[1, z] = row_difference(shifted.at[z + 1], side)
        slopes[2, z] = across[z * side : (z + 1) * side]

    grids = regular_grid(
        received_ref[...], spread_ref, coarse, block_rows, coarse_rows, coarse_cols
    )
    for r, grid in enumerate(grids):
        velocity_ref[8 * r : 8 * r + 8] = grid
    along = exact_dot(jnp.concatenate(grids, axis=0), hat_y_ref[...])
    shift = [[None] * coarse for _ in range(3)]
    for r in range(len(grids)):
        for c in range(3):
            for k in range(coarse):
                g = 8 * r + c * coarse + k
                term = hat_x_ref[r] * along[g : g + 1]
                shift[c][k] = term if r == 0 else shift[c][k] + term
    for z in range(wide):
        plane = shifted[z + 1, rows]
        hats = [hats_ref[k * wide + z : k * wide + z + 1, :] for k in range(coarse)]
        for c in range(3):
            u = hats[0] * shift[c][0]
            for k in range(1, coarse):
                u = u + hats[k] * shift[c][k]
            plane = plane + u * slopes[c, z]
        warped[z, rows] = plane
    clear_edges(warped, side)

    def fields(start):
        i = [image[z, start : start + 8] for z in range(wide)]
        w = [warped[z, PAD + start : PAD + start + 8] for z in range(wide)]
        return (w, [b * b for b in w], [a * b for a, b in zip(i, w)])

    of = box_sums(fields, planes, side, sums, threes, parts, box_ref)
    for z in range(planes):
        mean_w, mean_ww, mean_iw = [of(f, z) * (1.0 / 729.0) for f in range(3)]
        mean_i = mean_ref[z]
        sii = variance_ref[z]
        sww = mean_ww - mean_w * mean_w
        siw = mean_iw - mean_i * mean_w
        ratio = siw / (sii * sww + EPSILON)
        map_ref[z] = siw * ratio
        weight[z] = (2.0 * ratio) * (
            (image[z + REACH] - mean_i) - siw / (sww + EPSILON) * (warped[z + REACH, padded_rows(side)] - mean_w)
        )
    row = force_message(
        lambda z: weight[z],
        lambda z: warped.at[z + REACH],
        planes, cells_ref, rows_ref, cols_ref, marks_ref,
    )
    message_ref[...] = jnp.broadcast_to(row[None], message_ref.shape)


def last_kernel(
    received_ref, velocity_ref, spread_ref, map_ref, out_hbm, map_hbm, out_ref, sems
):
    map_copy = pltpu.make_async_copy(map_ref, map_hbm.at[0], sems.at[0])
    map_copy.start()
    _, coarse, rows, width = out_ref.shape
    coarse_cols = width // GY
    coarse_rows = spread_ref.shape[1] // (3 * coarse * LANES)
    block_rows = rows // coarse_rows
    grids = regular_grid(
        received_ref[...], spread_ref, coarse, block_rows, coarse_rows, coarse_cols
    )
    for r, grid in enumerate(grids):
        velocity = velocity_ref[8 * r : 8 * r + 8] + grid
        for c in range(3):
            for k in range(coarse):
                g = c * coarse + k
                out_ref[c, k, r : r + 1, :] = velocity[g : g + 1, :width]
    out_copy = pltpu.make_async_copy(out_ref, out_hbm, sems.at[1])
    out_copy.start()
    map_copy.wait()
    out_copy.wait()


def far_pairs(blocks, parts):
    pairs = []
    for block in range(blocks):
        for part in range(1, parts - 1, 2):
            low, high = block * parts + part, block * parts + part + 1
            pairs += [(low, high), (high, low)]
        for part in (0, parts - 1):
            pairs.append((block * parts + part, (block ^ 1) * parts + part))
    return pairs


VMEM = pl.BlockSpec(memory_space=pltpu.VMEM)
HBM = pl.BlockSpec(memory_space=pl.ANY)


def call(kernel, outs, scratch, *operands, in_specs=None, out_specs=None):
    return pl.pallas_call(
        kernel,
        out_shape=[jax.ShapeDtypeStruct(shape, dtype) for shape, dtype in outs],
        in_specs=in_specs or [VMEM] * len(operands),
        out_specs=out_specs or [VMEM] * len(outs),
        scratch_shapes=scratch,
        compiler_params=pltpu.CompilerParams(vmem_limit_bytes=24 << 20),
    )(*operands)


def per_device(fixed, moving, block_place, tissue):
    slots, planes, side, width = fixed.shape
    assert slots == 1 and width == LANES and planes == 2 * REACH
    depth_parts = lax.axis_size("gz")
    devices = lax.axis_size("blk") * depth_parts
    blocks = slots * lax.axis_size("blk")
    coarse = planes * depth_parts // SCALE
    coarse_rows, coarse_cols = side // SCALE, width // SCALE
    block_rows = blocks // GY
    wide = planes + 2 * REACH
    field = (planes, side, width)
    halo = ((2 * REACH + 1, side, width), BF16)

    near, far, fixed, moving = call(
        pack_kernel,
        [halo, halo, (field, BF16), (field, BF16)],
        [pltpu.SemaphoreType.DMA((2,))],
        pltpu.with_memory_space_constraint(fixed, pltpu.HBM),
        pltpu.with_memory_space_constraint(moving, pltpu.HBM),
        in_specs=[HBM] * 2,
    )
    far = lax.ppermute(far, ("blk", "gz"), far_pairs(lax.axis_size("blk"), depth_parts))
    pairs = [(i, i + 1) for i in range(0, depth_parts, 2)]
    near = lax.ppermute(near, "gz", pairs + [(b, a) for a, b in pairs])
    boxes = [
        pltpu.VMEM((2 * REACH * side, 2 * width), BF16),
        pltpu.VMEM((3 * REACH * side, 4 * width), BF16),
        pltpu.VMEM((5, planes, side + 2 * PAD, width), F32),
        pltpu.VMEM((5, planes, side + 8, width), F32),
    ]
    marks, hats, cells, rows, cols, box, slope, spread, hat_x, hat_y, own = call(
        functools.partial(table_kernel, block_rows=block_rows),
        [
            ((8, width), F32),
            ((coarse * wide, width), F32),
            ((coarse * planes, width), F32),
            ((coarse_rows, side, width), F32),
            ((width, 2 * width), BF16),
            ((6 * width, 2 * width), BF16),
            ((width, width), BF16),
            ((width, coarse_rows * 3 * coarse * width), BF16),
            ((block_rows * coarse_rows, side, width), F32),
            ((width, width), BF16),
            ((5,) + field, F32),
        ],
        boxes,
        jnp.stack([block_place, tissue]), fixed, moving,
    )

    message = ((devices, 1, LANES), F32)

    sent, mean, variance, image, shifted = call(
        first_kernel,
        [
            message,
            (field, F32),
            (field, F32),
            ((wide, side, width), F32),
            ((wide + 2, side + 2 * PAD, width), F32),
        ],
        [pltpu.VMEM((2,) + halo[0], BF16)] + boxes + [pltpu.VMEM(field, F32)],
        fixed, moving, near, far, marks, cells, rows, cols, box, own,
    )
    received = lax.all_to_all(sent, ("blk", "gz"), 0, 0).reshape(devices, LANES)
    sent, correlation, velocity = call(
        second_kernel,
        [message, (field, F32), ((8 * block_rows * coarse_rows, LANES), F32)],
        [
            pltpu.VMEM((3, wide, side, width), F32),
            pltpu.VMEM((wide, side + 2 * PAD, width), F32),
            pltpu.VMEM((3, planes, side + 2 * PAD, width), F32),
            pltpu.VMEM((3, planes, side + 8, width), F32),
            pltpu.VMEM((3 * planes * side // 2, 6 * width), BF16),
            pltpu.VMEM(field, F32),
        ],
        received, image, shifted, marks,
        mean, variance, hats, cells, rows, cols, box, slope, spread, hat_x, hat_y,
    )
    received = lax.all_to_all(sent, ("blk", "gz"), 0, 0).reshape(devices, LANES)
    grid = (3, coarse, block_rows * coarse_rows, GY * coarse_cols)
    return tuple(
        call(
            last_kernel,
            [(grid, F32), ((slots,) + field, F32)],
            [pltpu.VMEM(grid, F32), pltpu.SemaphoreType.DMA((2,))],
            received, velocity, spread, correlation,
            out_specs=[HBM, HBM],
        )
    )


def solution(mesh):
    return jax.shard_map(
        per_device,
        mesh=mesh,
        in_specs=(P("blk", "gz", None, None), P("blk", "gz", None, None), P("blk"), P("blk")),
        out_specs=(P(), P("blk", "gz", None, None)),
        check_vma=False,
    )
```

```python
import functools
import math

import jax
import jax.numpy as jnp
from jax import lax
from jax.experimental import pallas as pl
from jax.experimental.pallas import tpu as pltpu
from jax.sharding import PartitionSpec as P

SCALE = 16
GY = 8
EPSILON = 1e-05
STEP_LENGTH = 0.5
GAUSS_RAW = [math.exp(-((offset - 3) ** 2) / 4.5) for offset in range(7)]
GAUSS_TAPS = [value / sum(GAUSS_RAW) for value in GAUSS_RAW]
REACH = 4
PAD = 8
LANES = 128
F32 = jnp.float32
BF16 = jnp.bfloat16


def cell_weights(index, cell):
    total = jnp.zeros(index.shape, F32)
    for offset, weight in enumerate(GAUSS_TAPS):
        target = index + (offset - 3)
        inside = (target >= cell * SCALE) & (target < cell * SCALE + SCALE)
        total = total + jnp.where(inside, weight, 0.0)
    return total


def hat(index, cell, count):
    where = jnp.clip((index.astype(F32) + 0.5) * (1.0 / SCALE) - 0.5, 0.0, count - 1.0)
    return jnp.maximum(0.0, 1.0 - jnp.abs(where - cell.astype(F32)))


def lane_index(shape):
    return lax.broadcasted_iota(jnp.int32, shape, len(shape) - 1)


def sublane_index(shape):
    return lax.broadcasted_iota(jnp.int32, shape, len(shape) - 2)


def split(value, count):
    parts = []
    for _ in range(count):
        parts.append(value.astype(BF16))
        value = value - parts[-1].astype(F32)
    return parts


def close_dot(value, table):
    rows = value.shape[0]
    product = jnp.dot(
        jnp.concatenate(split(value, 2), axis=0), table, preferred_element_type=F32
    )
    return product[:rows] + product[rows:]


def window_of_nine(items):
    two = [a + b for a, b in zip(items[:-1], items[1:])]
    four = [a + b for a, b in zip(two[:-2], two[2:])]
    eight = [a + b for a, b in zip(four[:-4], four[4:])]
    return [a + b for a, b in zip(eight[:-1], items[8:])]


def padded_rows(side):
    return slice(PAD, PAD + side)


def clear_edges(ref, side):
    edge = jnp.zeros(ref.shape[:-2] + (PAD, LANES), F32)
    ref[..., 0:PAD, :] = edge
    ref[..., PAD + side :, :] = edge


def row_box(padded, three, side):
    count = side + 8
    three[...] = (
        padded[PAD - 5 : PAD - 5 + count]
        + padded[PAD - 4 : PAD - 4 + count]
        + padded[PAD - 3 : PAD - 3 + count]
    )
    return three[1 : 1 + side] + three[4 : 4 + side] + three[7 : 7 + side]


def row_difference(padded, side):
    return padded[PAD + 1 : PAD + 1 + side] - padded[PAD - 1 : PAD - 1 + side]


def col_difference(plane):
    width = plane.shape[1]
    lane = lane_index(plane.shape)
    upper = jnp.where(lane < width - 1, pltpu.roll(plane, width - 1, 1), 0.0)
    lower = jnp.where(lane > 0, pltpu.roll(plane, 1, 1), 0.0)
    return upper - lower


def load_images(odd, fixed_ref, moving_ref, near_ref, far_ref, halves, image, shifted):
    planes, side, _ = fixed_ref.shape
    rows = padded_rows(side)
    below = jnp.where(odd, 0, 1)
    halves[below] = near_ref[...]
    halves[1 - below] = far_ref[...]
    clear_edges(shifted, side)
    image[0:REACH] = halves[0, 0:REACH].astype(F32)
    image[REACH : REACH + planes] = fixed_ref[...].astype(F32)
    image[REACH + planes :] = halves[1, 0:REACH].astype(F32)
    shifted[0 : REACH + 1, rows] = halves[0, REACH:].astype(F32)
    shifted[REACH + 1 : REACH + 1 + planes, rows] = moving_ref[...].astype(F32)
    shifted[REACH + 1 + planes :, rows] = halves[1, REACH:].astype(F32)


def box_sums(fields, planes, side, sums, threes, parts, box_ref):
    half = planes // 2
    count = sums.shape[0]
    clear_edges(sums, side)
    for tile in range(side // 8):
        for f, items in enumerate(fields(8 * tile)):
            for z, item in enumerate(window_of_nine(items)):
                sums[f, z, PAD + 8 * tile : PAD + 8 * tile + 8] = item
    step = half // 4
    results = []
    for first in range(0, half, step):
        for i in range(first, first + step):
            for f in range(count):
                start = (i * count + f) * side
                for h in range(2):
                    z = i + h * half
                    total = row_box(sums.at[f, z], threes.at[f, z], side)
                    for part, rounded in enumerate(split(total, 3)):
                        lane = (2 * part + h) * LANES
                        parts[start : start + side, lane : lane + LANES] = rounded
        used = slice(first * count * side, (first + step) * count * side)
        results.append(jnp.dot(parts[used], box_ref[...], preferred_element_type=F32))

    def of(f, z):
        i, lane = z % half, (z // half) * LANES
        start = ((i % step) * count + f) * side
        return results[i // step][start : start + side, lane : lane + LANES]

    return of


def column_boxes(fixed, moving, side, single, double, box_ref):
    step = REACH // 1
    results = []
    for first in range(0, REACH, step):
        for i in range(first, first + step):
            for h in range(2):
                lane = h * LANES
                planes = (fixed(i, h), moving(i, h))
                for f, plane in enumerate(planes):
                    start = (2 * i + f) * side
                    single[start : start + side, lane : lane + LANES] = plane
                a, b = (plane.astype(F32) for plane in planes)
                for f, product in enumerate((a * a, b * b, a * b)):
                    start = (3 * i + f) * side
                    high, low = split(product, 2)
                    double[start : start + side, lane : lane + LANES] = high
                    double[start : start + side, 2 * LANES + lane : 3 * LANES + lane] = low
        ones = single[2 * first * side : 2 * (first + step) * side]
        twos = double[3 * first * side : 3 * (first + step) * side]
        results.append(
            (
                jnp.dot(ones, box_ref[0 : 2 * LANES], preferred_element_type=F32),
                jnp.dot(twos, box_ref[0 : 4 * LANES], preferred_element_type=F32),
            )
        )

    def of(f, i, h):
        source, count, f = (0, 2, f) if f < 2 else (1, 3, f - 2)
        start = ((i % step) * count + f) * side
        return results[i // step][source][start : start + side, h * LANES : (h + 1) * LANES]

    return of


def running(items):
    total = [items[0]]
    for item in items[1:]:
        total.append(total[-1] + item)
    return total


def force_message(weights, warped, planes, cells_ref, rows_ref, cols_ref, marks_ref):
    coarse = cells_ref.shape[0] // planes
    coarse_rows, side, _ = rows_ref.shape
    rows = padded_rows(side)
    total = [[None] * coarse for _ in range(3)]
    for z in range(planes):
        slopes = (
            warped(z + 1)[rows] - warped(z - 1)[rows],
            row_difference(warped(z), side),
            col_difference(warped(z)[rows]),
        )
        for k in range(coarse):
            index = k * planes + z
            share = weights(z) * cells_ref[index : index + 1, :]
            for c in range(3):
                term = share * slopes[c]
                total[c][k] = term if z == 0 else total[c][k] + term
    tiles = []
    for c in range(3):
        for k in range(coarse):
            for a in range(coarse_rows):
                product = total[c][k] * rows_ref[a]
                tile = product[0:8]
                for start in range(8, side, 8):
                    tile = tile + product[start : start + 8]
                tiles.append(tile)
    sums = close_dot(jnp.concatenate(tiles, axis=0), cols_ref[...])
    sums = sums[:, :LANES] + sums[:, LANES:]
    coarse_cols = LANES // SCALE
    lane = lane_index((8, LANES))
    picked = jnp.zeros((8, LANES), F32)
    for g in range(len(tiles)):
        picked = jnp.where(lane // coarse_cols == g, sums[8 * g : 8 * g + 8], picked)
    row = jnp.sum(picked, axis=0, keepdims=True) * marks_ref[1:2]
    return jnp.where(lane[0:1] == len(tiles) * coarse_cols, marks_ref[0:1], row)


def regular_grid(received, spread_ref, coarse, block_rows, coarse_rows, coarse_cols):
    groups = 3 * coarse
    used = groups * coarse_rows * coarse_cols
    width = GY * coarse_cols
    place = received[:, used : used + 1].astype(jnp.int32)
    here = (place % GY) == lane_index(received.shape) // coarse_cols
    block_row = place // GY
    sub = sublane_index((8, LANES))
    entries = close_dot(received, spread_ref[...])
    grids = []
    for r in range(block_rows):
        chosen = here if block_rows == 1 else here & (block_row == r)
        for a in range(coarse_rows):
            grid = jnp.zeros((8, LANES), F32)
            for g in range(groups):
                start = (a * groups + g) * LANES
                entry = jnp.where(chosen, entries[:, start : start + LANES], 0.0)
                grid = jnp.where(sub == g, jnp.sum(entry, axis=0, keepdims=True), grid)
            grids.append(grid)
    none = [jnp.zeros((8, LANES), F32)]
    grids = [
        0.5 * g + 0.25 * (before + after)
        for g, before, after in zip(grids, none + grids[:-1], grids[1:] + none)
    ]
    inside = lane_index((8, LANES)) < width
    grids = [
        jnp.where(
            inside, 0.5 * g + 0.25 * (pltpu.roll(g, 1, 1) + pltpu.roll(g, LANES - 1, 1)), 0.0
        )
        for g in grids
    ]
    square = functools.reduce(lambda a, b: a + b, [g * g for g in grids])
    square = jnp.sum(jnp.sum(square, axis=0, keepdims=True), axis=1, keepdims=True)
    mean = square * (1.0 / (groups * len(grids) * width))
    return grids, STEP_LENGTH / jnp.sqrt(mean + EPSILON)


def pack_kernel(fixed_hbm, moving_hbm, near_ref, far_ref, fixed_ref, moving_ref, sems):
    copies = [
        pltpu.make_async_copy(source.at[0], target, sems.at[i])
        for i, (source, target) in enumerate(((fixed_hbm, fixed_ref), (moving_hbm, moving_ref)))
    ]
    for copy in copies:
        copy.start()
    planes = fixed_ref.shape[0]
    part = lax.axis_index("gz")
    odd = part % 2
    inner = (part > 0) & (part < lax.axis_size("gz") - 1)
    for copy in copies:
        copy.wait()
    for ref, low, keep in ((far_ref, odd == 0, inner), (near_ref, odd == 1, None)):
        i = fixed_ref[pl.ds(jnp.where(low, 0, planes - REACH), REACH)]
        j = moving_ref[pl.ds(jnp.where(low, 0, planes - REACH - 1), REACH + 1)]
        if keep is not None:
            i = jnp.where(keep, i.astype(F32), 0.0).astype(BF16)
            j = jnp.where(keep, j.astype(F32), 0.0).astype(BF16)
        ref[0:REACH] = i
        ref[REACH:] = j


def table_kernel(
    both_ref, fixed_ref, moving_ref,
    marks_ref, hats_ref, cells_ref, rows_ref, cols_ref, box_ref, slope_ref, spread_ref, hat_x_ref, hat_y_ref,
    own_ref, across_ref, single, double, sums, threes,
    *, block_rows,
):
    planes = fixed_ref.shape[0]
    part = lax.axis_index("gz")
    total = planes * lax.axis_size("gz")
    coarse_rows, side, _ = rows_ref.shape
    coarse_cols = LANES // SCALE
    width = GY * coarse_cols
    wide = planes + 2 * REACH
    row = sublane_index(hats_ref.shape)
    z = part * planes + row % wide - REACH
    hats_ref[...] = jnp.where((z >= 0) & (z < total), hat(z, row // wide, total // SCALE), 0.0)
    row = sublane_index(cells_ref.shape)
    cells_ref[...] = cell_weights(part * planes + row % planes, row // planes)
    for a in range(coarse_rows):
        rows_ref[a] = 0.5 * cell_weights(sublane_index((side, LANES)), a)
    square = (LANES, LANES)
    cols = cell_weights(sublane_index(square), lane_index(square) % coarse_cols)
    for i, value in enumerate(split(cols, 2)):
        cols_ref[:, i * LANES : (i + 1) * LANES] = value
    apart = sublane_index(square) - lane_index(square)
    band = jnp.where(jnp.abs(apart) <= 4, 1.0, 0.0).astype(BF16)
    box_ref[...] = jnp.zeros(box_ref.shape, BF16)
    for i in range(6):
        lane = (i % 2) * LANES
        box_ref[i * LANES : (i + 1) * LANES, lane : lane + LANES] = band
    slope = jnp.where(apart == 1, 1.0, jnp.where(apart == -1, -1.0, 0.0)).astype(BF16)
    slope_ref[...] = slope
    across = jnp.dot(
        moving_ref[...].reshape(planes * side, LANES), slope, preferred_element_type=F32
    )
    across_ref[...] = across.reshape(across_ref.shape)
    lane = lane_index(square)
    entry = sublane_index(square)
    coarse = total // SCALE
    group = coarse_rows * coarse_cols
    for a in range(coarse_rows):
        for c in range(3):
            for k in range(coarse):
                value = jnp.zeros(square, F32)
                for other, weight in ((k - 1, 0.25), (k, 0.5), (k + 1, 0.25)):
                    if 0 <= other < coarse:
                        start = (c * coarse + other) * group + a * coarse_cols
                        hit = (entry == start + lane % coarse_cols) & (lane < width)
                        value = jnp.where(hit, weight, value)
                start = ((a * 3 + c) * coarse + k) * LANES
                spread_ref[:, start : start + LANES] = value.astype(BF16)
    row = sublane_index(marks_ref.shape)
    marks_ref[...] = jnp.where(row == 0, both_ref[0:1, 0:1], both_ref[1:2, 0:1]).astype(F32)
    place = both_ref[0:1, 0:1]
    y = lane + (place % GY) * LANES
    hat_y_ref[...] = jnp.where(entry < width, hat(y, entry, width), 0.0).astype(BF16)
    x = sublane_index((side, LANES)) + (place // GY) * side
    for r in range(block_rows * coarse_rows):
        hat_x_ref[r] = 0.5 * hat(x, jnp.full((1, 1), r, jnp.int32), block_rows * coarse_rows)

    of = column_boxes(
        lambda i, h: fixed_ref[i + REACH * h],
        lambda i, h: moving_ref[i + REACH * h],
        side, single, double, box_ref,
    )
    clear_edges(sums, side)
    for f in range(5):
        boxed = [of(f, i, h) for h in range(2) for i in range(REACH)]
        up, down = running(boxed), running(boxed[::-1])[::-1]
        for z in range(planes):
            sums[f, z, padded_rows(side)] = up[z + REACH] if z < REACH else down[z - REACH]
            own_ref[f, z] = row_box(sums.at[f, z], threes.at[f, z], side)


def first_kernel(
    fixed_ref, moving_ref, near_ref, far_ref, marks_ref,
    cells_ref, rows_ref, cols_ref, box_ref, slope_ref, own_ref,
    message_ref, mean_ref, variance_ref, image, shifted, across_ref,
    halves, single, double, sums, threes, weight,
):
    planes, side, _ = fixed_ref.shape
    odd = lax.axis_index("gz") % 2 == 1
    load_images(odd, fixed_ref, moving_ref, near_ref, far_ref, halves, image, shifted)
    of = column_boxes(
        lambda i, h: halves[h, i],
        lambda i, h: halves[h, REACH + i + 1 - h],
        side, single, double, box_ref,
    )
    for h in range(2):
        planes_h = halves[h, REACH + 1 - h : 2 * REACH + 1 - h]
        across = jnp.dot(
            planes_h.reshape(REACH * side, LANES), slope_ref[...], preferred_element_type=F32
        )
        across_ref[h] = across.reshape(across_ref.shape[1:])
    clear_edges(sums, side)
    for f in range(5):
        below = running([of(f, i, 0) for i in range(REACH)][::-1])[::-1]
        above = running([of(f, i, 1) for i in range(REACH)])
        for z, item in enumerate(below + above):
            sums[f, z, padded_rows(side)] = item
    for z in range(planes):
        mean_i, mean_w, mean_ii, mean_ww, mean_iw = [
            (row_box(sums.at[f, z], threes.at[f, z], side) + own_ref[f, z]) * (1.0 / 729.0)
            for f in range(5)
        ]
        sii = mean_ii - mean_i * mean_i
        sww = mean_ww - mean_w * mean_w
        siw = mean_iw - mean_i * mean_w
        mean_ref[z] = mean_i
        variance_ref[z] = sii
        ratio = siw / (sii * sww + EPSILON)
        weight[z] = (2.0 * ratio) * (
            (image[z + REACH] - mean_i)
            - siw / (sww + EPSILON) * (shifted[z + REACH + 1, padded_rows(side)] - mean_w)
        )
    row = force_message(
        lambda z: weight[z],
        lambda z: shifted.at[z + REACH + 1],
        planes, cells_ref, rows_ref, cols_ref, marks_ref,
    )
    message_ref[...] = jnp.broadcast_to(row[None], message_ref.shape)


def second_kernel(
    received_ref, image, shifted, marks_ref,
    mean_ref, variance_ref, hats_ref, cells_ref, rows_ref, cols_ref, box_ref, own_across_ref,
    across_ref, spread_ref, hat_x_ref, hat_y_ref,
    message_ref, map_ref, velocity_ref,
    slopes, warped, sums, threes, parts, weight,
):
    planes, side, _ = mean_ref.shape
    wide = planes + 2 * REACH
    coarse_rows = rows_ref.shape[0]
    coarse_cols = LANES // SCALE
    block_rows = velocity_ref.shape[0] // 8 // coarse_rows
    coarse = hats_ref.shape[0] // wide
    rows = padded_rows(side)
    for z in range(wide):
        slopes[0, z] = shifted[z + 2, rows] - shifted[z, rows]
        slopes[1, z] = row_difference(shifted.at[z + 1], side)

    grids, factor = regular_grid(
        received_ref[...], spread_ref, coarse, block_rows, coarse_rows, coarse_cols
    )
    along = close_dot(jnp.concatenate(grids, axis=0), hat_y_ref[...]) * factor
    for r, grid in enumerate(grids):
        velocity_ref[8 * r : 8 * r + 8] = grid * factor
    shift = [[None] * coarse for _ in range(3)]
    for r in range(len(grids)):
        for c in range(3):
            for k in range(coarse):
                g = 8 * r + c * coarse + k
                term = hat_x_ref[r] * along[g : g + 1]
                shift[c][k] = term if r == 0 else shift[c][k] + term
    change = [[shift[c][k] - shift[c][0] for k in range(coarse)] for c in range(3)]
    for z in range(wide):
        plane = shifted[z + 1, rows]
        hats = [hats_ref[k * wide + z : k * wide + z + 1, :] for k in range(coarse)]
        inside = functools.reduce(lambda a, b: a + b, hats)
        if z < REACH:
            across = across_ref[0, z]
        elif z < REACH + planes:
            across = own_across_ref[z - REACH]
        else:
            across = across_ref[1, z - REACH - planes]
        for c, slope in enumerate((slopes[0, z], slopes[1, z], across)):
            if c == 0 and not REACH <= z < REACH + planes:
                slope = slope * inside
            u = shift[c][0]
            for k in range(1, coarse):
                u = u + hats[k] * change[c][k]
            plane = plane + u * slope
        warped[z, rows] = plane
    clear_edges(warped, side)

    def fields(start):
        i = [image[z, start : start + 8] for z in range(wide)]
        w = [warped[z, PAD + start : PAD + start + 8] for z in range(wide)]
        return (w, [b * b for b in w], [a * b for a, b in zip(i, w)])

    of = box_sums(fields, planes, side, sums, threes, parts, box_ref)
    for z in range(planes):
        mean_w, mean_ww, mean_iw = [of(f, z) * (1.0 / 729.0) for f in range(3)]
        mean_i = mean_ref[z]
        sii = variance_ref[z]
        sww = mean_ww - mean_w * mean_w
        siw = mean_iw - mean_i * mean_w
        ratio = siw / (sii * sww + EPSILON)
        map_ref[z] = siw * ratio
        weight[z] = (2.0 * ratio) * (
            (image[z + REACH] - mean_i) - siw / (sww + EPSILON) * (warped[z + REACH, padded_rows(side)] - mean_w)
        )
    row = force_message(
        lambda z: weight[z],
        lambda z: warped.at[z + REACH],
        planes, cells_ref, rows_ref, cols_ref, marks_ref,
    )
    message_ref[...] = jnp.broadcast_to(row[None], message_ref.shape)


def last_kernel(
    received_ref, velocity_ref, spread_ref, map_ref, out_hbm, map_hbm, out_ref, sems
):
    map_copy = pltpu.make_async_copy(map_ref, map_hbm.at[0], sems.at[0])
    map_copy.start()
    _, coarse, rows, width = out_ref.shape
    coarse_cols = width // GY
    coarse_rows = spread_ref.shape[1] // (3 * coarse * LANES)
    block_rows = rows // coarse_rows
    grids, factor = regular_grid(
        received_ref[...], spread_ref, coarse, block_rows, coarse_rows, coarse_cols
    )
    for r, grid in enumerate(grids):
        velocity = velocity_ref[8 * r : 8 * r + 8] + grid * factor
        for c in range(3):
            for k in range(coarse):
                g = c * coarse + k
                out_ref[c, k, r : r + 1, :] = velocity[g : g + 1, :width]
    out_copy = pltpu.make_async_copy(out_ref, out_hbm, sems.at[1])
    out_copy.start()
    map_copy.wait()
    out_copy.wait()


def far_pairs(blocks, parts):
    pairs = []
    for block in range(blocks):
        for part in range(1, parts - 1, 2):
            low, high = block * parts + part, block * parts + part + 1
            pairs += [(low, high), (high, low)]
        for part in (0, parts - 1):
            pairs.append((block * parts + part, (block ^ 1) * parts + part))
    return pairs


VMEM = pl.BlockSpec(memory_space=pltpu.VMEM)
HBM = pl.BlockSpec(memory_space=pl.ANY)


def call(kernel, outs, scratch, *operands, in_specs=None, out_specs=None):
    return pl.pallas_call(
        kernel,
        out_shape=[jax.ShapeDtypeStruct(shape, dtype) for shape, dtype in outs],
        in_specs=in_specs or [VMEM] * len(operands),
        out_specs=out_specs or [VMEM] * len(outs),
        scratch_shapes=scratch,
        compiler_params=pltpu.CompilerParams(vmem_limit_bytes=24 << 20),
    )(*operands)


def per_device(fixed, moving, block_place, tissue):
    slots, planes, side, width = fixed.shape
    assert slots == 1 and width == LANES and planes == 2 * REACH
    depth_parts = lax.axis_size("gz")
    devices = lax.axis_size("blk") * depth_parts
    blocks = slots * lax.axis_size("blk")
    coarse = planes * depth_parts // SCALE
    coarse_rows, coarse_cols = side // SCALE, width // SCALE
    block_rows = blocks // GY
    wide = planes + 2 * REACH
    field = (planes, side, width)
    halo = ((2 * REACH + 1, side, width), BF16)

    near, far, fixed, moving = call(
        pack_kernel,
        [halo, halo, (field, BF16), (field, BF16)],
        [pltpu.SemaphoreType.DMA((2,))],
        pltpu.with_memory_space_constraint(fixed, pltpu.HBM),
        pltpu.with_memory_space_constraint(moving, pltpu.HBM),
        in_specs=[HBM] * 2,
    )
    far = lax.ppermute(far, ("blk", "gz"), far_pairs(lax.axis_size("blk"), depth_parts))
    pairs = [(i, i + 1) for i in range(0, depth_parts, 2)]
    near = lax.ppermute(near, "gz", pairs + [(b, a) for a, b in pairs])
    boxes = [
        pltpu.VMEM((2 * REACH * side, 2 * width), BF16),
        pltpu.VMEM((3 * REACH * side, 4 * width), BF16),
        pltpu.VMEM((5, planes, side + 2 * PAD, width), F32),
        pltpu.VMEM((5, planes, side + 8, width), F32),
    ]
    marks, hats, cells, rows, cols, box, slope, spread, hat_x, hat_y, own, own_across = call(
        functools.partial(table_kernel, block_rows=block_rows),
        [
            ((8, width), F32),
            ((coarse * wide, width), F32),
            ((coarse * planes, width), F32),
            ((coarse_rows, side, width), F32),
            ((width, 2 * width), BF16),
            ((6 * width, 2 * width), BF16),
            ((width, width), BF16),
            ((width, coarse_rows * 3 * coarse * width), BF16),
            ((block_rows * coarse_rows, side, width), F32),
            ((width, width), BF16),
            ((5,) + field, F32),
            (field, F32),
        ],
        boxes,
        jnp.stack([block_place, tissue]), fixed, moving,
    )

    message = ((devices, 1, LANES), F32)

    sent, mean, variance, image, shifted, across = call(
        first_kernel,
        [
            message,
            (field, F32),
            (field, F32),
            ((wide, side, width), F32),
            ((wide + 2, side + 2 * PAD, width), F32),
            ((2, REACH, side, width), F32),
        ],
        [pltpu.VMEM((2,) + halo[0], BF16)] + boxes + [pltpu.VMEM(field, F32)],
        fixed, moving, near, far, marks, cells, rows, cols, box, slope, own,
    )
    received = lax.all_to_all(sent, ("blk", "gz"), 0, 0).reshape(devices, LANES)
    sent, correlation, velocity = call(
        second_kernel,
        [message, (field, F32), ((8 * block_rows * coarse_rows, LANES), F32)],
        [
            pltpu.VMEM((2, wide, side, width), F32),
            pltpu.VMEM((wide, side + 2 * PAD, width), F32),
            pltpu.VMEM((3, planes, side + 2 * PAD, width), F32),
            pltpu.VMEM((3, planes, side + 8, width), F32),
            pltpu.VMEM((3 * planes * side // 2, 6 * width), BF16),
            pltpu.VMEM(field, F32),
        ],
        received, image, shifted, marks,
        mean, variance, hats, cells, rows, cols, box, own_across, across,
        spread, hat_x, hat_y,
    )
    received = lax.all_to_all(sent, ("blk", "gz"), 0, 0).reshape(devices, LANES)
    grid = (3, coarse, block_rows * coarse_rows, GY * coarse_cols)
    return tuple(
        call(
            last_kernel,
            [(grid, F32), ((slots,) + field, F32)],
            [pltpu.VMEM(grid, F32), pltpu.SemaphoreType.DMA((2,))],
            received, velocity, spread, correlation,
            out_specs=[HBM, HBM],
        )
    )


def solution(mesh):
    return jax.shard_map(
        per_device,
        mesh=mesh,
        in_specs=(P("blk", "gz", None, None), P("blk", "gz", None, None), P("blk"), P("blk")),
        out_specs=(P(), P("blk", "gz", None, None)),
        check_vma=False,
    )
```

```python
import functools
import math

import jax
import jax.numpy as jnp
from jax import lax
from jax.experimental import pallas as pl
from jax.experimental.pallas import tpu as pltpu
from jax.sharding import PartitionSpec as P

SCALE = 16
GY = 8
EPSILON = 1e-05
STEP_LENGTH = 0.5
GAUSS_RAW = [math.exp(-((offset - 3) ** 2) / 4.5) for offset in range(7)]
GAUSS_TAPS = [value / sum(GAUSS_RAW) for value in GAUSS_RAW]
REACH = 4
PAD = 8
LANES = 128
F32 = jnp.float32
BF16 = jnp.bfloat16


def cell_weights(index, cell):
    total = jnp.zeros(index.shape, F32)
    for offset, weight in enumerate(GAUSS_TAPS):
        target = index + (offset - 3)
        inside = (target >= cell * SCALE) & (target < cell * SCALE + SCALE)
        total = total + jnp.where(inside, weight, 0.0)
    return total


def hat(index, cell, count):
    where = jnp.clip((index.astype(F32) + 0.5) * (1.0 / SCALE) - 0.5, 0.0, count - 1.0)
    return jnp.maximum(0.0, 1.0 - jnp.abs(where - cell.astype(F32)))


def lane_index(shape):
    return lax.broadcasted_iota(jnp.int32, shape, len(shape) - 1)


def sublane_index(shape):
    return lax.broadcasted_iota(jnp.int32, shape, len(shape) - 2)


def split(value, count):
    parts = []
    for _ in range(count):
        parts.append(value.astype(BF16))
        value = value - parts[-1].astype(F32)
    return parts


def close_dot(value, table):
    rows = value.shape[0]
    product = jnp.dot(
        jnp.concatenate(split(value, 2), axis=0), table, preferred_element_type=F32
    )
    return product[:rows] + product[rows:]


def window_of_nine(items):
    two = [a + b for a, b in zip(items[:-1], items[1:])]
    four = [a + b for a, b in zip(two[:-2], two[2:])]
    eight = [a + b for a, b in zip(four[:-4], four[4:])]
    return [a + b for a, b in zip(eight[:-1], items[8:])]


def padded_rows(side):
    return slice(PAD, PAD + side)


def clear_edges(ref, side):
    edge = jnp.zeros(ref.shape[:-2] + (PAD, LANES), F32)
    ref[..., 0:PAD, :] = edge
    ref[..., PAD + side :, :] = edge


def row_box(padded, three, side):
    count = side + 8
    three[...] = (
        padded[PAD - 5 : PAD - 5 + count]
        + padded[PAD - 4 : PAD - 4 + count]
        + padded[PAD - 3 : PAD - 3 + count]
    )
    return three[1 : 1 + side] + three[4 : 4 + side] + three[7 : 7 + side]


def row_difference(padded, side):
    return padded[PAD + 1 : PAD + 1 + side] - padded[PAD - 1 : PAD - 1 + side]


def col_difference(plane):
    width = plane.shape[1]
    lane = lane_index(plane.shape)
    upper = jnp.where(lane < width - 1, pltpu.roll(plane, width - 1, 1), 0.0)
    lower = jnp.where(lane > 0, pltpu.roll(plane, 1, 1), 0.0)
    return upper - lower


def box_sums(fields, planes, side, sums, threes, parts, box_ref):
    half = planes // 2
    count = sums.shape[0]
    clear_edges(sums, side)
    for tile in range(side // 8):
        for f, items in enumerate(fields(8 * tile)):
            for z, item in enumerate(window_of_nine(items)):
                sums[f, z, PAD + 8 * tile : PAD + 8 * tile + 8] = item
    step = half // 4
    results = []
    for first in range(0, half, step):
        for i in range(first, first + step):
            for f in range(count):
                start = (i * count + f) * side
                for h in range(2):
                    z = i + h * half
                    total = row_box(sums.at[f, z], threes.at[f, z], side)
                    for part, rounded in enumerate(split(total, 3)):
                        lane = (2 * part + h) * LANES
                        parts[start : start + side, lane : lane + LANES] = rounded
        used = slice(first * count * side, (first + step) * count * side)
        results.append(jnp.dot(parts[used], box_ref[...], preferred_element_type=F32))

    def of(f, z):
        i, lane = z % half, (z // half) * LANES
        start = ((i % step) * count + f) * side
        return results[i // step][start : start + side, lane : lane + LANES]

    return of


def column_boxes(fixed, moving, side, single, double, box_ref):
    step = REACH // 1
    results = []
    for first in range(0, REACH, step):
        for i in range(first, first + step):
            for h in range(2):
                lane = h * LANES
                planes = (fixed(i, h), moving(i, h))
                for f, plane in enumerate(planes):
                    start = (2 * i + f) * side
                    single[start : start + side, lane : lane + LANES] = plane
                a, b = (plane.astype(F32) for plane in planes)
                for f, product in enumerate((a * a, b * b, a * b)):
                    start = (3 * i + f) * side
                    high, low = split(product, 2)
                    double[start : start + side, lane : lane + LANES] = high
                    double[start : start + side, 2 * LANES + lane : 3 * LANES + lane] = low
        ones = single[2 * first * side : 2 * (first + step) * side]
        twos = double[3 * first * side : 3 * (first + step) * side]
        results.append(
            (
                jnp.dot(ones, box_ref[0 : 2 * LANES], preferred_element_type=F32),
                jnp.dot(twos, box_ref[0 : 4 * LANES], preferred_element_type=F32),
            )
        )

    def of(f, i, h):
        source, count, f = (0, 2, f) if f < 2 else (1, 3, f - 2)
        start = ((i % step) * count + f) * side
        return results[i // step][source][start : start + side, h * LANES : (h + 1) * LANES]

    return of


def running(items):
    total = [items[0]]
    for item in items[1:]:
        total.append(total[-1] + item)
    return total


def force_message(weights, slopes, planes, cells_ref, rows_ref, cols_ref, marks_ref):
    coarse = cells_ref.shape[0] // planes
    coarse_rows, side, _ = rows_ref.shape
    total = [[None] * coarse for _ in range(3)]
    for z in range(planes):
        directions = slopes(z)
        for k in range(coarse):
            index = k * planes + z
            share = weights(z) * cells_ref[index : index + 1, :]
            for c in range(3):
                term = share * directions[c]
                total[c][k] = term if z == 0 else total[c][k] + term
    tiles = []
    for c in range(3):
        for k in range(coarse):
            for a in range(coarse_rows):
                product = total[c][k] * rows_ref[a]
                tile = product[0:8]
                for start in range(8, side, 8):
                    tile = tile + product[start : start + 8]
                tiles.append(tile)
    sums = close_dot(jnp.concatenate(tiles, axis=0), cols_ref[...])
    sums = sums[:, :LANES] + sums[:, LANES:]
    coarse_cols = LANES // SCALE
    lane = lane_index((8, LANES))
    picked = jnp.zeros((8, LANES), F32)
    for g in range(len(tiles)):
        picked = jnp.where(lane // coarse_cols == g, sums[8 * g : 8 * g + 8], picked)
    row = jnp.sum(picked, axis=0, keepdims=True) * marks_ref[1:2]
    return jnp.where(lane[0:1] == len(tiles) * coarse_cols, marks_ref[0:1], row)


def regular_grid(received, spread_ref, coarse, block_rows, coarse_rows, coarse_cols):
    groups = 3 * coarse
    used = groups * coarse_rows * coarse_cols
    width = GY * coarse_cols
    place = received[:, used : used + 1].astype(jnp.int32)
    here = (place % GY) == lane_index(received.shape) // coarse_cols
    block_row = place // GY
    sub = sublane_index((8, LANES))
    entries = close_dot(received, spread_ref[...])
    grids = []
    for r in range(block_rows):
        chosen = here if block_rows == 1 else here & (block_row == r)
        for a in range(coarse_rows):
            grid = jnp.zeros((8, LANES), F32)
            for g in range(groups):
                start = (a * groups + g) * LANES
                entry = jnp.where(chosen, entries[:, start : start + LANES], 0.0)
                grid = jnp.where(sub == g, jnp.sum(entry, axis=0, keepdims=True), grid)
            grids.append(grid)
    none = [jnp.zeros((8, LANES), F32)]
    grids = [
        0.5 * g + 0.25 * (before + after)
        for g, before, after in zip(grids, none + grids[:-1], grids[1:] + none)
    ]
    before_columns = grids
    inside = lane_index((8, LANES)) < width
    grids = [
        jnp.where(
            inside, 0.5 * g + 0.25 * (pltpu.roll(g, 1, 1) + pltpu.roll(g, LANES - 1, 1)), 0.0
        )
        for g in grids
    ]
    square = functools.reduce(lambda a, b: a + b, [g * g for g in grids])
    square = jnp.sum(jnp.sum(square, axis=0, keepdims=True), axis=1, keepdims=True)
    mean = square * (1.0 / (groups * len(grids) * width))
    return before_columns, grids, STEP_LENGTH / jnp.sqrt(mean + EPSILON)


def pack_kernel(fixed_hbm, moving_hbm, near_ref, far_ref, fixed_ref, moving_ref, sems):
    copies = [
        pltpu.make_async_copy(source.at[0], target, sems.at[i])
        for i, (source, target) in enumerate(((fixed_hbm, fixed_ref), (moving_hbm, moving_ref)))
    ]
    for copy in copies:
        copy.start()
    planes = fixed_ref.shape[0]
    part = lax.axis_index("gz")
    odd = part % 2
    inner = (part > 0) & (part < lax.axis_size("gz") - 1)
    for copy in copies:
        copy.wait()
    for ref, low, keep in ((far_ref, odd == 0, inner), (near_ref, odd == 1, None)):
        i = fixed_ref[pl.ds(jnp.where(low, 0, planes - REACH), REACH)]
        j = moving_ref[pl.ds(jnp.where(low, 0, planes - REACH - 1), REACH + 1)]
        if keep is not None:
            i = jnp.where(keep, i.astype(F32), 0.0).astype(BF16)
            j = jnp.where(keep, j.astype(F32), 0.0).astype(BF16)
        ref[0:REACH] = i
        ref[REACH:] = j


def table_kernel(
    both_ref, fixed_ref, moving_ref,
    marks_ref, hats_ref, cells_ref, rows_ref, cols_ref, box_ref, slope_ref, spread_ref, hat_x_ref, hat_y_ref,
    own_ref, image_ref, planes_ref, down_ref, across_ref,
    single, double, sums, threes,
    *, block_rows,
):
    planes = fixed_ref.shape[0]
    part = lax.axis_index("gz")
    total = planes * lax.axis_size("gz")
    coarse_rows, side, _ = rows_ref.shape
    coarse_cols = LANES // SCALE
    width = GY * coarse_cols
    wide = planes + 2 * REACH
    row = sublane_index(hats_ref.shape)
    z = part * planes + row % wide - REACH
    hats_ref[...] = jnp.where((z >= 0) & (z < total), hat(z, row // wide, total // SCALE), 0.0)
    row = sublane_index(cells_ref.shape)
    cells_ref[...] = cell_weights(part * planes + row % planes, row // planes)
    for a in range(coarse_rows):
        rows_ref[a] = 0.5 * cell_weights(sublane_index((side, LANES)), a)
    square = (LANES, LANES)
    cols = cell_weights(sublane_index(square), lane_index(square) % coarse_cols)
    for i, value in enumerate(split(cols, 2)):
        cols_ref[:, i * LANES : (i + 1) * LANES] = value
    apart = sublane_index(square) - lane_index(square)
    band = jnp.where(jnp.abs(apart) <= 4, 1.0, 0.0).astype(BF16)
    box_ref[...] = jnp.zeros(box_ref.shape, BF16)
    for i in range(6):
        lane = (i % 2) * LANES
        box_ref[i * LANES : (i + 1) * LANES, lane : lane + LANES] = band
    slope = jnp.where(apart == 1, 1.0, jnp.where(apart == -1, -1.0, 0.0)).astype(BF16)
    slope_ref[...] = slope
    across = jnp.dot(
        moving_ref[...].reshape(planes * side, LANES), slope, preferred_element_type=F32
    )
    across_ref[...] = across.reshape(across_ref.shape)
    image_ref[...] = fixed_ref[...].astype(F32)
    clear_edges(planes_ref, side)
    planes_ref[:, padded_rows(side)] = moving_ref[...].astype(F32)
    for z in range(planes):
        down_ref[z] = row_difference(planes_ref.at[z], side)
    lane = lane_index(square)
    entry = sublane_index(square)
    coarse = total // SCALE
    group = coarse_rows * coarse_cols
    for a in range(coarse_rows):
        for c in range(3):
            for k in range(coarse):
                value = jnp.zeros(square, F32)
                for other, weight in ((k - 1, 0.25), (k, 0.5), (k + 1, 0.25)):
                    if 0 <= other < coarse:
                        start = (c * coarse + other) * group + a * coarse_cols
                        hit = (entry == start + lane % coarse_cols) & (lane < width)
                        value = jnp.where(hit, weight, value)
                start = ((a * 3 + c) * coarse + k) * LANES
                spread_ref[:, start : start + LANES] = value.astype(BF16)
    row = sublane_index(marks_ref.shape)
    marks_ref[...] = jnp.where(row == 0, both_ref[0:1, 0:1], both_ref[1:2, 0:1]).astype(F32)
    place = both_ref[0:1, 0:1]
    y = lane + (place % GY) * LANES
    hat_y = jnp.where(entry < width, hat(y, entry, width), 0.0)
    hat_y = 0.5 * hat_y + 0.25 * (pltpu.roll(hat_y, 1, 0) + pltpu.roll(hat_y, LANES - 1, 0))
    hat_y_ref[...] = jnp.where(entry < width, hat_y, 0.0).astype(BF16)
    x = sublane_index((side, LANES)) + (place // GY) * side
    for r in range(block_rows * coarse_rows):
        hat_x_ref[r] = 0.5 * hat(x, jnp.full((1, 1), r, jnp.int32), block_rows * coarse_rows)

    of = column_boxes(
        lambda i, h: fixed_ref[i + REACH * h],
        lambda i, h: moving_ref[i + REACH * h],
        side, single, double, box_ref,
    )
    clear_edges(sums, side)
    for f in range(5):
        boxed = [of(f, i, h) for h in range(2) for i in range(REACH)]
        up, down = running(boxed), running(boxed[::-1])[::-1]
        for z in range(planes):
            sums[f, z, padded_rows(side)] = up[z + REACH] if z < REACH else down[z - REACH]
            own_ref[f, z] = row_box(sums.at[f, z], threes.at[f, z], side)


def first_kernel(
    image_ref, planes_ref, down_ref, across_ref, near_ref, far_ref, marks_ref,
    cells_ref, rows_ref, cols_ref, box_ref, own_ref,
    message_ref, mean_ref, variance_ref, halves,
    single, double, sums, threes, weight,
):
    planes, side, _ = image_ref.shape
    rows = padded_rows(side)
    below = lax.rem(lax.axis_index("gz") + 1, 2)
    halves[below] = near_ref[...]
    halves[1 - below] = far_ref[...]
    of = column_boxes(
        lambda i, h: halves[h, i],
        lambda i, h: halves[h, REACH + i + 1 - h],
        side, single, double, box_ref,
    )
    clear_edges(sums, side)
    for f in range(5):
        low = running([of(f, i, 0) for i in range(REACH)][::-1])[::-1]
        high = running([of(f, i, 1) for i in range(REACH)])
        for z, item in enumerate(low + high):
            sums[f, z, padded_rows(side)] = item
    for z in range(planes):
        mean_i, mean_w, mean_ii, mean_ww, mean_iw = [
            (row_box(sums.at[f, z], threes.at[f, z], side) + own_ref[f, z]) * (1.0 / 729.0)
            for f in range(5)
        ]
        sii = mean_ii - mean_i * mean_i
        sww = mean_ww - mean_w * mean_w
        siw = mean_iw - mean_i * mean_w
        mean_ref[z] = mean_i
        variance_ref[z] = sii
        ratio = siw / (sii * sww + EPSILON)
        weight[z] = (2.0 * ratio) * (
            (image_ref[z] - mean_i) - siw / (sww + EPSILON) * (planes_ref[z, rows] - mean_w)
        )

    def plane(z):
        if z < 0:
            return halves[0, 2 * REACH + 1 + z].astype(F32)
        return planes_ref[z, rows] if z < planes else halves[1, REACH + z - planes].astype(F32)

    row = force_message(
        lambda z: weight[z],
        lambda z: (plane(z + 1) - plane(z - 1), down_ref[z], across_ref[z]),
        planes, cells_ref, rows_ref, cols_ref, marks_ref,
    )
    message_ref[...] = jnp.broadcast_to(row[None], message_ref.shape)


def second_kernel(
    received_ref, halves, image_ref, planes_ref, down_ref, across_ref, marks_ref,
    mean_ref, variance_ref, hats_ref, cells_ref, rows_ref, cols_ref, box_ref, slope_ref,
    spread_ref, hat_x_ref, hat_y_ref,
    message_ref, map_ref, velocity_ref,
    images, outer, outer_across, slopes, shift_ref, warped, sums, threes, parts, weight,
):
    planes, side, _ = mean_ref.shape
    wide = planes + 2 * REACH
    coarse_rows = rows_ref.shape[0]
    coarse_cols = LANES // SCALE
    block_rows = velocity_ref.shape[0] // 8 // coarse_rows
    coarse = hats_ref.shape[0] // wide
    rows = padded_rows(side)

    def image(z):
        if z < 0:
            return images.at[0, z + REACH]
        return image_ref.at[z] if z < planes else images.at[1, z - planes]

    def moving(z):
        if z < 0:
            return outer.at[0, z + REACH + 1]
        return planes_ref.at[z] if z < planes else outer.at[1, z - planes]

    before_columns, grids, factor = regular_grid(
        received_ref[...], spread_ref, coarse, block_rows, coarse_rows, coarse_cols
    )
    along = close_dot(jnp.concatenate(before_columns, axis=0), hat_y_ref[...]) * factor
    for r, grid in enumerate(grids):
        velocity_ref[8 * r : 8 * r + 8] = grid * factor
    shift = [[None] * coarse for _ in range(3)]
    for r in range(len(grids)):
        for c in range(3):
            for k in range(coarse):
                g = 8 * r + c * coarse + k
                term = hat_x_ref[r] * along[g : g + 1]
                shift[c][k] = term if r == 0 else shift[c][k] + term
    for c in range(3):
        for k in range(coarse):
            shift_ref[c, k] = shift[c][k] if k == 0 else shift[c][k] - shift[c][0]

    clear_edges(outer, side)
    for h in range(2):
        images[h] = halves[h, 0:REACH].astype(F32)
        outer[h, :, rows] = halves[h, REACH:].astype(F32)
        across = jnp.dot(
            halves[h, REACH + 1 - h : 2 * REACH + 1 - h].reshape(REACH * side, LANES),
            slope_ref[...],
            preferred_element_type=F32,
        )
        outer_across[h] = across.reshape(outer_across.shape[1:])
    for z in range(-REACH, planes + REACH):
        slope = moving(z + 1)[rows] - moving(z - 1)[rows]
        if not 0 <= z < planes:
            hats = [hats_ref[pl.ds(k * wide + z + REACH, 1), :] for k in range(coarse)]
            slope = slope * functools.reduce(lambda a, b: a + b, hats)
            slopes[1, z + REACH] = row_difference(moving(z), side)
        slopes[0, z + REACH] = slope

    @pl.when(lax.axis_index("gz") >= 0)
    def _():
        for z in range(-REACH, planes + REACH):
            hats = [hats_ref[pl.ds(k * wide + z + REACH, 1), :] for k in range(coarse)]
            if z < 0:
                down, across = slopes[1, z + REACH], outer_across[0, z + REACH]
            elif z < planes:
                down, across = down_ref[z], across_ref[z]
            else:
                down, across = slopes[1, z + REACH], outer_across[1, z - planes]
            plane = moving(z)[rows]
            for c, slope in enumerate((slopes[0, z + REACH], down, across)):
                u = shift_ref[c, 0]
                for k in range(1, coarse):
                    u = u + hats[k] * shift_ref[c, k]
                plane = plane + u * slope
            warped[z + REACH, rows] = plane
        clear_edges(warped, side)

        def fields(start):
            i = [image(z)[start : start + 8] for z in range(-REACH, planes + REACH)]
            w = [warped[z, PAD + start : PAD + start + 8] for z in range(wide)]
            return (w, [b * b for b in w], [a * b for a, b in zip(i, w)])

        of = box_sums(fields, planes, side, sums, threes, parts, box_ref)
        for z in range(planes):
            mean_w, mean_ww, mean_iw = [of(f, z) * (1.0 / 729.0) for f in range(3)]
            mean_i = mean_ref[z]
            sii = variance_ref[z]
            sww = mean_ww - mean_w * mean_w
            siw = mean_iw - mean_i * mean_w
            ratio = siw / (sii * sww + EPSILON)
            map_ref[z] = siw * ratio
            weight[z] = (2.0 * ratio) * (
                (image_ref[z] - mean_i)
                - siw / (sww + EPSILON) * (warped[z + REACH, rows] - mean_w)
            )
        row = force_message(
            lambda z: weight[z],
            lambda z: (
                warped[z + REACH + 1, rows] - warped[z + REACH - 1, rows],
                row_difference(warped.at[z + REACH], side),
                col_difference(warped[z + REACH, rows]),
            ),
            planes, cells_ref, rows_ref, cols_ref, marks_ref,
        )
        message_ref[...] = jnp.broadcast_to(row[None], message_ref.shape)


def last_kernel(
    received_ref, velocity_ref, spread_ref, map_ref, out_hbm, map_hbm, out_ref, sems
):
    map_copy = pltpu.make_async_copy(map_ref, map_hbm.at[0], sems.at[0])
    map_copy.start()
    _, coarse, rows, width = out_ref.shape
    coarse_cols = width // GY
    coarse_rows = spread_ref.shape[1] // (3 * coarse * LANES)
    block_rows = rows // coarse_rows
    _, grids, factor = regular_grid(
        received_ref[...], spread_ref, coarse, block_rows, coarse_rows, coarse_cols
    )
    for r, grid in enumerate(grids):
        velocity = velocity_ref[8 * r : 8 * r + 8] + grid * factor
        for c in range(3):
            for k in range(coarse):
                g = c * coarse + k
                out_ref[c, k, r : r + 1, :] = velocity[g : g + 1, :width]
    out_copy = pltpu.make_async_copy(out_ref, out_hbm, sems.at[1])
    out_copy.start()
    map_copy.wait()
    out_copy.wait()


def far_pairs(blocks, parts):
    pairs = []
    for block in range(blocks):
        for part in range(1, parts - 1, 2):
            low, high = block * parts + part, block * parts + part + 1
            pairs += [(low, high), (high, low)]
        for part in (0, parts - 1):
            pairs.append((block * parts + part, (block ^ 1) * parts + part))
    return pairs


VMEM = pl.BlockSpec(memory_space=pltpu.VMEM)
HBM = pl.BlockSpec(memory_space=pl.ANY)


def call(kernel, outs, scratch, *operands, in_specs=None, out_specs=None):
    return pl.pallas_call(
        kernel,
        out_shape=[jax.ShapeDtypeStruct(shape, dtype) for shape, dtype in outs],
        in_specs=in_specs or [VMEM] * len(operands),
        out_specs=out_specs or [VMEM] * len(outs),
        scratch_shapes=scratch,
        compiler_params=pltpu.CompilerParams(vmem_limit_bytes=24 << 20),
    )(*operands)


def per_device(fixed, moving, block_place, tissue):
    slots, planes, side, width = fixed.shape
    assert slots == 1 and width == LANES and planes == 2 * REACH
    depth_parts = lax.axis_size("gz")
    devices = lax.axis_size("blk") * depth_parts
    blocks = slots * lax.axis_size("blk")
    coarse = planes * depth_parts // SCALE
    coarse_rows, coarse_cols = side // SCALE, width // SCALE
    block_rows = blocks // GY
    wide = planes + 2 * REACH
    field = (planes, side, width)
    halo = ((2 * REACH + 1, side, width), BF16)

    near, far, fixed, moving = call(
        pack_kernel,
        [halo, halo, (field, BF16), (field, BF16)],
        [pltpu.SemaphoreType.DMA((2,))],
        pltpu.with_memory_space_constraint(fixed, pltpu.HBM),
        pltpu.with_memory_space_constraint(moving, pltpu.HBM),
        in_specs=[HBM] * 2,
    )
    far = lax.ppermute(far, ("blk", "gz"), far_pairs(lax.axis_size("blk"), depth_parts))
    pairs = [(i, i + 1) for i in range(0, depth_parts, 2)]
    near = lax.ppermute(near, "gz", pairs + [(b, a) for a, b in pairs])
    boxes = [
        pltpu.VMEM((2 * REACH * side, 2 * width), BF16),
        pltpu.VMEM((3 * REACH * side, 4 * width), BF16),
        pltpu.VMEM((5, planes, side + 2 * PAD, width), F32),
        pltpu.VMEM((5, planes, side + 8, width), F32),
    ]
    (
        marks, hats, cells, rows, cols, box, slope, spread, hat_x, hat_y,
        own, image, padded, down, across,
    ) = call(
        functools.partial(table_kernel, block_rows=block_rows),
        [
            ((8, width), F32),
            ((coarse * wide, width), F32),
            ((coarse * planes, width), F32),
            ((coarse_rows, side, width), F32),
            ((width, 2 * width), BF16),
            ((6 * width, 2 * width), BF16),
            ((width, width), BF16),
            ((width, coarse_rows * 3 * coarse * width), BF16),
            ((block_rows * coarse_rows, side, width), F32),
            ((width, width), BF16),
            ((5,) + field, F32),
            (field, F32),
            ((planes, side + 2 * PAD, width), F32),
            (field, F32),
            (field, F32),
        ],
        boxes,
        jnp.stack([block_place, tissue]), fixed, moving,
    )

    message = ((devices, 1, LANES), F32)

    sent, mean, variance, halves = call(
        first_kernel,
        [message, (field, F32), (field, F32), ((2,) + halo[0], BF16)],
        boxes + [pltpu.VMEM(field, F32)],
        image, padded, down, across, near, far, marks, cells, rows, cols, box, own,
    )
    received = lax.all_to_all(sent, ("blk", "gz"), 0, 0).reshape(devices, LANES)
    sent, correlation, velocity = call(
        second_kernel,
        [message, (field, F32), ((8 * block_rows * coarse_rows, LANES), F32)],
        [
            pltpu.VMEM((2, REACH, side, width), F32),
            pltpu.VMEM((2, REACH + 1, side + 2 * PAD, width), F32),
            pltpu.VMEM((2, REACH, side, width), F32),
            pltpu.VMEM((2, wide, side, width), F32),
            pltpu.VMEM((3, coarse, side, width), F32),
            pltpu.VMEM((wide, side + 2 * PAD, width), F32),
            pltpu.VMEM((3, planes, side + 2 * PAD, width), F32),
            pltpu.VMEM((3, planes, side + 8, width), F32),
            pltpu.VMEM((3 * planes * side // 2, 6 * width), BF16),
            pltpu.VMEM(field, F32),
        ],
        received, halves, image, padded, down, across, marks,
        mean, variance, hats, cells, rows, cols, box, slope,
        spread, hat_x, hat_y,
    )
    received = lax.all_to_all(sent, ("blk", "gz"), 0, 0).reshape(devices, LANES)
    grid = (3, coarse, block_rows * coarse_rows, GY * coarse_cols)
    return tuple(
        call(
            last_kernel,
            [(grid, F32), ((slots,) + field, F32)],
            [pltpu.VMEM(grid, F32), pltpu.SemaphoreType.DMA((2,))],
            received, velocity, spread, correlation,
            out_specs=[HBM, HBM],
        )
    )


def solution(mesh):
    return jax.shard_map(
        per_device,
        mesh=mesh,
        in_specs=(P("blk", "gz", None, None), P("blk", "gz", None, None), P("blk"), P("blk")),
        out_specs=(P(), P("blk", "gz", None, None)),
        check_vma=False,
    )
```

```python
import functools
import math

import jax
import jax.numpy as jnp
from jax import lax
from jax.experimental import pallas as pl
from jax.experimental.pallas import tpu as pltpu
from jax.sharding import PartitionSpec as P

SCALE = 16
GY = 8
EPSILON = 1e-05
STEP_LENGTH = 0.5
GAUSS_RAW = [math.exp(-((offset - 3) ** 2) / 4.5) for offset in range(7)]
GAUSS_TAPS = [value / sum(GAUSS_RAW) for value in GAUSS_RAW]
REACH = 4
PAD = 8
LANES = 128
F32 = jnp.float32
BF16 = jnp.bfloat16


def cell_weights(index, cell):
    total = jnp.zeros(index.shape, F32)
    for offset, weight in enumerate(GAUSS_TAPS):
        target = index + (offset - 3)
        inside = (target >= cell * SCALE) & (target < cell * SCALE + SCALE)
        total = total + jnp.where(inside, weight, 0.0)
    return total


def hat(index, cell, count):
    where = jnp.clip((index.astype(F32) + 0.5) * (1.0 / SCALE) - 0.5, 0.0, count - 1.0)
    return jnp.maximum(0.0, 1.0 - jnp.abs(where - cell.astype(F32)))


def lane_index(shape):
    return lax.broadcasted_iota(jnp.int32, shape, len(shape) - 1)


def sublane_index(shape):
    return lax.broadcasted_iota(jnp.int32, shape, len(shape) - 2)


def split(value, count):
    parts = []
    for _ in range(count):
        parts.append(value.astype(BF16))
        value = value - parts[-1].astype(F32)
    return parts


def close_dot(value, table):
    rows = value.shape[0]
    product = jnp.dot(
        jnp.concatenate(split(value, 2), axis=0), table, preferred_element_type=F32
    )
    return product[:rows] + product[rows:]


def window_of_nine(items):
    two = [a + b for a, b in zip(items[:-1], items[1:])]
    four = [a + b for a, b in zip(two[:-2], two[2:])]
    eight = [a + b for a, b in zip(four[:-4], four[4:])]
    return [a + b for a, b in zip(eight[:-1], items[8:])]


def padded_rows(side):
    return slice(PAD, PAD + side)


def clear_edges(ref, side):
    edge = jnp.zeros(ref.shape[:-2] + (PAD, LANES), F32)
    ref[..., 0:PAD, :] = edge
    ref[..., PAD + side :, :] = edge


def row_box(value, padded, three):
    side = value.shape[0]
    rows = padded_rows(side)
    middle = padded[PAD - 1 : PAD - 1 + side] + value + padded[PAD + 1 : PAD + 1 + side]
    three[0:PAD] = padded[1 : PAD + 1]
    three[rows] = middle
    three[PAD + side :] = padded[PAD + side - 1 : 2 * PAD + side - 1]
    return three[PAD - 3 : PAD - 3 + side] + middle + three[PAD + 3 : PAD + 3 + side]


def row_difference(padded, side):
    return padded[PAD + 1 : PAD + 1 + side] - padded[PAD - 1 : PAD - 1 + side]


def col_difference(plane):
    width = plane.shape[1]
    lane = lane_index(plane.shape)
    upper = jnp.where(lane < width - 1, pltpu.roll(plane, width - 1, 1), 0.0)
    lower = jnp.where(lane > 0, pltpu.roll(plane, 1, 1), 0.0)
    return upper - lower


def box_sums(fields, planes, side, sums, threes, parts, box_ref):
    half = planes // 2
    count = sums.shape[0]
    clear_edges(sums, side)
    for tile in range(side // 8):
        for f, items in enumerate(fields(8 * tile)):
            for z, item in enumerate(window_of_nine(items)):
                sums[f, z, PAD + 8 * tile : PAD + 8 * tile + 8] = item
    step = half // 4
    results = []
    for first in range(0, half, step):
        for i in range(first, first + step):
            for f in range(count):
                start = (i * count + f) * side
                for h in range(2):
                    z = i + h * half
                    total = row_box(sums[f, z, padded_rows(side)], sums.at[f, z], threes.at[f, z])
                    for part, rounded in enumerate(split(total, 3)):
                        lane = (2 * part + h) * LANES
                        parts[start : start + side, lane : lane + LANES] = rounded
        used = slice(first * count * side, (first + step) * count * side)
        results.append(jnp.dot(parts[used], box_ref[...], preferred_element_type=F32))

    def of(f, z):
        i, lane = z % half, (z // half) * LANES
        start = ((i % step) * count + f) * side
        return results[i // step][start : start + side, lane : lane + LANES]

    return of


def column_boxes(fixed, moving, side, single, double, box_ref):
    step = REACH // 1
    results = []
    for first in range(0, REACH, step):
        for i in range(first, first + step):
            for h in range(2):
                lane = h * LANES
                planes = (fixed(i, h), moving(i, h))
                for f, plane in enumerate(planes):
                    start = (2 * i + f) * side
                    single[start : start + side, lane : lane + LANES] = plane
                a, b = (plane.astype(F32) for plane in planes)
                for f, product in enumerate((a * a, b * b, a * b)):
                    start = (3 * i + f) * side
                    high, low = split(product, 2)
                    double[start : start + side, lane : lane + LANES] = high
                    double[start : start + side, 2 * LANES + lane : 3 * LANES + lane] = low
        ones = single[2 * first * side : 2 * (first + step) * side]
        twos = double[3 * first * side : 3 * (first + step) * side]
        results.append(
            (
                jnp.dot(ones, box_ref[0 : 2 * LANES], preferred_element_type=F32),
                jnp.dot(twos, box_ref[0 : 4 * LANES], preferred_element_type=F32),
            )
        )

    def of(f, i, h):
        source, count, f = (0, 2, f) if f < 2 else (1, 3, f - 2)
        start = ((i % step) * count + f) * side
        return results[i // step][source][start : start + side, h * LANES : (h + 1) * LANES]

    return of


def running(items):
    total = [items[0]]
    for item in items[1:]:
        total.append(total[-1] + item)
    return total


def force_message(weights, slopes, planes, cells_ref, rows_ref, cols_ref, marks_ref):
    coarse = cells_ref.shape[0] // planes
    coarse_rows, side, _ = rows_ref.shape
    total = [[None] * coarse for _ in range(3)]
    for z in range(planes):
        directions = slopes(z)
        for k in range(coarse):
            index = k * planes + z
            share = weights(z) * cells_ref[index : index + 1, :]
            for c in range(3):
                term = share * directions[c]
                total[c][k] = term if z == 0 else total[c][k] + term
    tiles = []
    for c in range(3):
        for k in range(coarse):
            for a in range(coarse_rows):
                product = total[c][k] * rows_ref[a]
                tile = product[0:8]
                for start in range(8, side, 8):
                    tile = tile + product[start : start + 8]
                tiles.append(tile)
    sums = close_dot(jnp.concatenate(tiles, axis=0), cols_ref[...])
    sums = sums[:, :LANES] + sums[:, LANES:]
    coarse_cols = LANES // SCALE
    lane = lane_index((8, LANES))
    picked = jnp.zeros((8, LANES), F32)
    for g in range(len(tiles)):
        picked = jnp.where(lane // coarse_cols == g, sums[8 * g : 8 * g + 8], picked)
    row = jnp.sum(picked, axis=0, keepdims=True) * marks_ref[1:2]
    return jnp.where(lane[0:1] == len(tiles) * coarse_cols, marks_ref[0:1], row)


def regular_grid(received, spread_ref, coarse, block_rows, coarse_rows, coarse_cols):
    groups = 3 * coarse
    used = groups * coarse_rows * coarse_cols
    width = GY * coarse_cols
    place = received[:, used : used + 1].astype(jnp.int32)
    here = (place % GY) == lane_index(received.shape) // coarse_cols
    block_row = place // GY
    sub = sublane_index((8, LANES))
    entries = close_dot(received, spread_ref[...])
    grids = []
    for r in range(block_rows):
        chosen = here if block_rows == 1 else here & (block_row == r)
        for a in range(coarse_rows):
            grid = jnp.zeros((8, LANES), F32)
            for g in range(groups):
                start = (a * groups + g) * LANES
                entry = jnp.where(chosen, entries[:, start : start + LANES], 0.0)
                grid = jnp.where(sub == g, jnp.sum(entry, axis=0, keepdims=True), grid)
            grids.append(grid)
    none = [jnp.zeros((8, LANES), F32)]
    grids = [
        0.5 * g + 0.25 * (before + after)
        for g, before, after in zip(grids, none + grids[:-1], grids[1:] + none)
    ]
    before_columns = grids
    inside = lane_index((8, LANES)) < width
    grids = [
        jnp.where(
            inside, 0.5 * g + 0.25 * (pltpu.roll(g, 1, 1) + pltpu.roll(g, LANES - 1, 1)), 0.0
        )
        for g in grids
    ]
    square = functools.reduce(lambda a, b: a + b, [g * g for g in grids])
    square = jnp.sum(jnp.sum(square, axis=0, keepdims=True), axis=1, keepdims=True)
    mean = square * (1.0 / (groups * len(grids) * width))
    return before_columns, grids, STEP_LENGTH / jnp.sqrt(mean + EPSILON)


def pack_kernel(fixed_hbm, moving_hbm, near_ref, far_ref, fixed_ref, moving_ref, sems):
    copies = [
        pltpu.make_async_copy(source.at[0], target, sems.at[i])
        for i, (source, target) in enumerate(((fixed_hbm, fixed_ref), (moving_hbm, moving_ref)))
    ]
    for copy in copies:
        copy.start()
    planes = fixed_ref.shape[0]
    part = lax.axis_index("gz")
    odd = part % 2
    inner = (part > 0) & (part < lax.axis_size("gz") - 1)
    for copy in copies:
        copy.wait()
    for ref, low, keep in ((far_ref, odd == 0, inner), (near_ref, odd == 1, None)):
        i = fixed_ref[pl.ds(jnp.where(low, 0, planes - REACH), REACH)]
        j = moving_ref[pl.ds(jnp.where(low, 0, planes - REACH - 1), REACH + 1)]
        if keep is not None:
            i = jnp.where(keep, i.astype(F32), 0.0).astype(BF16)
            j = jnp.where(keep, j.astype(F32), 0.0).astype(BF16)
        ref[0:REACH] = i
        ref[REACH:] = j


def table_kernel(
    both_ref, fixed_ref, moving_ref,
    marks_ref, hats_ref, cells_ref, rows_ref, cols_ref, box_ref, slope_ref, spread_ref, hat_x_ref, hat_y_ref,
    own_ref, image_ref, planes_ref, down_ref, across_ref,
    single, double, sums, threes,
    *, block_rows,
):
    planes = fixed_ref.shape[0]
    part = lax.axis_index("gz")
    total = planes * lax.axis_size("gz")
    coarse_rows, side, _ = rows_ref.shape
    coarse_cols = LANES // SCALE
    width = GY * coarse_cols
    wide = planes + 2 * REACH
    row = sublane_index(hats_ref.shape)
    z = part * planes + row % wide - REACH
    hats_ref[...] = jnp.where((z >= 0) & (z < total), hat(z, row // wide, total // SCALE), 0.0)
    row = sublane_index(cells_ref.shape)
    cells_ref[...] = cell_weights(part * planes + row % planes, row // planes)
    for a in range(coarse_rows):
        rows_ref[a] = 0.5 * cell_weights(sublane_index((side, LANES)), a)
    square = (LANES, LANES)
    cols = cell_weights(sublane_index(square), lane_index(square) % coarse_cols)
    for i, value in enumerate(split(cols, 2)):
        cols_ref[:, i * LANES : (i + 1) * LANES] = value
    apart = sublane_index(square) - lane_index(square)
    band = jnp.where(jnp.abs(apart) <= 4, 1.0, 0.0).astype(BF16)
    box_ref[...] = jnp.zeros(box_ref.shape, BF16)
    for i in range(6):
        lane = (i % 2) * LANES
        box_ref[i * LANES : (i + 1) * LANES, lane : lane + LANES] = band
    slope = jnp.where(apart == 1, 1.0, jnp.where(apart == -1, -1.0, 0.0)).astype(BF16)
    slope_ref[...] = slope
    across = jnp.dot(
        moving_ref[...].reshape(planes * side, LANES), slope, preferred_element_type=F32
    )
    across_ref[...] = across.reshape(across_ref.shape)
    image_ref[...] = fixed_ref[...].astype(F32)
    clear_edges(planes_ref, side)
    planes_ref[:, padded_rows(side)] = moving_ref[...].astype(F32)
    for z in range(planes):
        down_ref[z] = row_difference(planes_ref.at[z], side)
    lane = lane_index(square)
    entry = sublane_index(square)
    coarse = total // SCALE
    group = coarse_rows * coarse_cols
    for a in range(coarse_rows):
        for c in range(3):
            for k in range(coarse):
                value = jnp.zeros(square, F32)
                for other, weight in ((k - 1, 0.25), (k, 0.5), (k + 1, 0.25)):
                    if 0 <= other < coarse:
                        start = (c * coarse + other) * group + a * coarse_cols
                        hit = (entry == start + lane % coarse_cols) & (lane < width)
                        value = jnp.where(hit, weight, value)
                start = ((a * 3 + c) * coarse + k) * LANES
                spread_ref[:, start : start + LANES] = value.astype(BF16)
    row = sublane_index(marks_ref.shape)
    marks_ref[...] = jnp.where(row == 0, both_ref[0:1, 0:1], both_ref[1:2, 0:1]).astype(F32)
    place = both_ref[0:1, 0:1]
    y = lane + (place % GY) * LANES
    hat_y = jnp.where(entry < width, hat(y, entry, width), 0.0)
    hat_y = 0.5 * hat_y + 0.25 * (pltpu.roll(hat_y, 1, 0) + pltpu.roll(hat_y, LANES - 1, 0))
    hat_y_ref[...] = jnp.where(entry < width, hat_y, 0.0).astype(BF16)
    x = sublane_index((side, LANES)) + (place // GY) * side
    for r in range(block_rows * coarse_rows):
        hat_x_ref[r] = 0.5 * hat(x, jnp.full((1, 1), r, jnp.int32), block_rows * coarse_rows)

    of = column_boxes(
        lambda i, h: fixed_ref[i + REACH * h],
        lambda i, h: moving_ref[i + REACH * h],
        side, single, double, box_ref,
    )
    clear_edges(sums, side)
    for f in range(5):
        boxed = [of(f, i, h) for h in range(2) for i in range(REACH)]
        up, down = running(boxed), running(boxed[::-1])[::-1]
        for z in range(planes):
            item = up[z + REACH] if z < REACH else down[z - REACH]
            sums[f, z, padded_rows(side)] = item
            own_ref[f, z] = row_box(item, sums.at[f, z], threes.at[f, z])


def first_kernel(
    image_ref, planes_ref, down_ref, across_ref, near_ref, far_ref, marks_ref,
    cells_ref, rows_ref, cols_ref, box_ref, own_ref,
    message_ref, mean_ref, variance_ref, halves,
    single, double, sums, threes, weight,
):
    planes, side, _ = image_ref.shape
    rows = padded_rows(side)
    below = lax.rem(lax.axis_index("gz") + 1, 2)
    halves[below] = near_ref[...]
    halves[1 - below] = far_ref[...]
    of = column_boxes(
        lambda i, h: halves[h, i],
        lambda i, h: halves[h, REACH + i + 1 - h],
        side, single, double, box_ref,
    )
    clear_edges(sums, side)
    outer = []
    for f in range(5):
        low = running([of(f, i, 0) for i in range(REACH)][::-1])[::-1]
        high = running([of(f, i, 1) for i in range(REACH)])
        outer.append(low + high)
        for z, item in enumerate(outer[f]):
            sums[f, z, rows] = item
    for z in range(planes):
        mean_i, mean_w, mean_ii, mean_ww, mean_iw = [
            (row_box(outer[f][z], sums.at[f, z], threes.at[f, z]) + own_ref[f, z]) * (1.0 / 729.0)
            for f in range(5)
        ]
        sii = mean_ii - mean_i * mean_i
        sww = mean_ww - mean_w * mean_w
        siw = mean_iw - mean_i * mean_w
        mean_ref[z] = mean_i
        variance_ref[z] = sii
        ratio = siw / (sii * sww + EPSILON)
        weight[z] = (2.0 * ratio) * (
            (image_ref[z] - mean_i) - siw / (sww + EPSILON) * (planes_ref[z, rows] - mean_w)
        )

    def plane(z):
        if z < 0:
            return halves[0, 2 * REACH + 1 + z].astype(F32)
        return planes_ref[z, rows] if z < planes else halves[1, REACH + z - planes].astype(F32)

    row = force_message(
        lambda z: weight[z],
        lambda z: (plane(z + 1) - plane(z - 1), down_ref[z], across_ref[z]),
        planes, cells_ref, rows_ref, cols_ref, marks_ref,
    )
    message_ref[...] = jnp.broadcast_to(row[None], message_ref.shape)


def second_kernel(
    received_ref, halves, image_ref, planes_ref, down_ref, across_ref, marks_ref,
    mean_ref, variance_ref, hats_ref, cells_ref, rows_ref, cols_ref, box_ref, slope_ref,
    spread_ref, hat_x_ref, hat_y_ref,
    message_ref, map_ref, velocity_ref,
    images, outer, outer_across, slopes, shift_ref, warped, sums, threes, parts, weight,
):
    planes, side, _ = mean_ref.shape
    wide = planes + 2 * REACH
    coarse_rows = rows_ref.shape[0]
    coarse_cols = LANES // SCALE
    block_rows = velocity_ref.shape[0] // 8 // coarse_rows
    coarse = hats_ref.shape[0] // wide
    rows = padded_rows(side)

    def image(z):
        if z < 0:
            return images.at[0, z + REACH]
        return image_ref.at[z] if z < planes else images.at[1, z - planes]

    def moving(z):
        if z < 0:
            return outer.at[0, z + REACH + 1]
        return planes_ref.at[z] if z < planes else outer.at[1, z - planes]

    before_columns, grids, factor = regular_grid(
        received_ref[...], spread_ref, coarse, block_rows, coarse_rows, coarse_cols
    )
    along = close_dot(jnp.concatenate(before_columns, axis=0), hat_y_ref[...]) * factor
    for r, grid in enumerate(grids):
        velocity_ref[8 * r : 8 * r + 8] = grid * factor
    shift = [[None] * coarse for _ in range(3)]
    for r in range(len(grids)):
        for c in range(3):
            for k in range(coarse):
                g = 8 * r + c * coarse + k
                term = hat_x_ref[r] * along[g : g + 1]
                shift[c][k] = term if r == 0 else shift[c][k] + term
    for c in range(3):
        for k in range(coarse):
            shift_ref[c, k] = shift[c][k] if k == 0 else shift[c][k] - shift[c][0]

    clear_edges(outer, side)
    for h in range(2):
        images[h] = halves[h, 0:REACH].astype(F32)
        outer[h, :, rows] = halves[h, REACH:].astype(F32)
        across = jnp.dot(
            halves[h, REACH + 1 - h : 2 * REACH + 1 - h].reshape(REACH * side, LANES),
            slope_ref[...],
            preferred_element_type=F32,
        )
        outer_across[h] = across.reshape(outer_across.shape[1:])
    for z in range(-REACH, planes + REACH):
        slope = moving(z + 1)[rows] - moving(z - 1)[rows]
        if not 0 <= z < planes:
            hats = [hats_ref[pl.ds(k * wide + z + REACH, 1), :] for k in range(coarse)]
            slope = slope * functools.reduce(lambda a, b: a + b, hats)
            slopes[1, z + REACH] = row_difference(moving(z), side)
        slopes[0, z + REACH] = slope

    @pl.when(lax.axis_index("gz") >= 0)
    def _():
        for z in range(-REACH, planes + REACH):
            hats = [hats_ref[pl.ds(k * wide + z + REACH, 1), :] for k in range(coarse)]
            if z < 0:
                down, across = slopes[1, z + REACH], outer_across[0, z + REACH]
            elif z < planes:
                down, across = down_ref[z], across_ref[z]
            else:
                down, across = slopes[1, z + REACH], outer_across[1, z - planes]
            plane = moving(z)[rows]
            for c, slope in enumerate((slopes[0, z + REACH], down, across)):
                u = shift_ref[c, 0]
                for k in range(1, coarse):
                    u = u + hats[k] * shift_ref[c, k]
                plane = plane + u * slope
            warped[z + REACH, rows] = plane
        clear_edges(warped, side)

        def fields(start):
            i = [image(z)[start : start + 8] for z in range(-REACH, planes + REACH)]
            w = [warped[z, PAD + start : PAD + start + 8] for z in range(wide)]
            return (w, [b * b for b in w], [a * b for a, b in zip(i, w)])

        of = box_sums(fields, planes, side, sums, threes, parts, box_ref)
        for z in range(planes):
            mean_w, mean_ww, mean_iw = [of(f, z) * (1.0 / 729.0) for f in range(3)]
            mean_i = mean_ref[z]
            sii = variance_ref[z]
            sww = mean_ww - mean_w * mean_w
            siw = mean_iw - mean_i * mean_w
            ratio = siw / (sii * sww + EPSILON)
            map_ref[z] = siw * ratio
            weight[z] = (2.0 * ratio) * (
                (image_ref[z] - mean_i)
                - siw / (sww + EPSILON) * (warped[z + REACH, rows] - mean_w)
            )
        row = force_message(
            lambda z: weight[z],
            lambda z: (
                warped[z + REACH + 1, rows] - warped[z + REACH - 1, rows],
                row_difference(warped.at[z + REACH], side),
                col_difference(warped[z + REACH, rows]),
            ),
            planes, cells_ref, rows_ref, cols_ref, marks_ref,
        )
        message_ref[...] = jnp.broadcast_to(row[None], message_ref.shape)


def last_kernel(
    received_ref, velocity_ref, spread_ref, map_ref, out_hbm, map_hbm, out_ref, sems
):
    map_copy = pltpu.make_async_copy(map_ref, map_hbm.at[0], sems.at[0])
    map_copy.start()
    _, coarse, rows, width = out_ref.shape
    coarse_cols = width // GY
    coarse_rows = spread_ref.shape[1] // (3 * coarse * LANES)
    block_rows = rows // coarse_rows
    _, grids, factor = regular_grid(
        received_ref[...], spread_ref, coarse, block_rows, coarse_rows, coarse_cols
    )
    for r, grid in enumerate(grids):
        velocity = velocity_ref[8 * r : 8 * r + 8] + grid * factor
        for c in range(3):
            for k in range(coarse):
                g = c * coarse + k
                out_ref[c, k, r : r + 1, :] = velocity[g : g + 1, :width]
    out_copy = pltpu.make_async_copy(out_ref, out_hbm, sems.at[1])
    out_copy.start()
    map_copy.wait()
    out_copy.wait()


def far_pairs(blocks, parts):
    pairs = []
    for block in range(blocks):
        for part in range(1, parts - 1, 2):
            low, high = block * parts + part, block * parts + part + 1
            pairs += [(low, high), (high, low)]
        for part in (0, parts - 1):
            pairs.append((block * parts + part, (block ^ 1) * parts + part))
    return pairs


VMEM = pl.BlockSpec(memory_space=pltpu.VMEM)
HBM = pl.BlockSpec(memory_space=pl.ANY)


def call(kernel, outs, scratch, *operands, in_specs=None, out_specs=None):
    return pl.pallas_call(
        kernel,
        out_shape=[jax.ShapeDtypeStruct(shape, dtype) for shape, dtype in outs],
        in_specs=in_specs or [VMEM] * len(operands),
        out_specs=out_specs or [VMEM] * len(outs),
        scratch_shapes=scratch,
        compiler_params=pltpu.CompilerParams(vmem_limit_bytes=24 << 20),
    )(*operands)


def per_device(fixed, moving, block_place, tissue):
    slots, planes, side, width = fixed.shape
    assert slots == 1 and width == LANES and planes == 2 * REACH
    depth_parts = lax.axis_size("gz")
    devices = lax.axis_size("blk") * depth_parts
    blocks = slots * lax.axis_size("blk")
    coarse = planes * depth_parts // SCALE
    coarse_rows, coarse_cols = side // SCALE, width // SCALE
    block_rows = blocks // GY
    wide = planes + 2 * REACH
    field = (planes, side, width)
    halo = ((2 * REACH + 1, side, width), BF16)

    near, far, fixed, moving = call(
        pack_kernel,
        [halo, halo, (field, BF16), (field, BF16)],
        [pltpu.SemaphoreType.DMA((2,))],
        pltpu.with_memory_space_constraint(fixed, pltpu.HBM),
        pltpu.with_memory_space_constraint(moving, pltpu.HBM),
        in_specs=[HBM] * 2,
    )
    far = lax.ppermute(far, ("blk", "gz"), far_pairs(lax.axis_size("blk"), depth_parts))
    pairs = [(i, i + 1) for i in range(0, depth_parts, 2)]
    near = lax.ppermute(near, "gz", pairs + [(b, a) for a, b in pairs])
    boxes = [
        pltpu.VMEM((2 * REACH * side, 2 * width), BF16),
        pltpu.VMEM((3 * REACH * side, 4 * width), BF16),
        pltpu.VMEM((5, planes, side + 2 * PAD, width), F32),
        pltpu.VMEM((5, planes, side + 2 * PAD, width), F32),
    ]
    (
        marks, hats, cells, rows, cols, box, slope, spread, hat_x, hat_y,
        own, image, padded, down, across,
    ) = call(
        functools.partial(table_kernel, block_rows=block_rows),
        [
            ((8, width), F32),
            ((coarse * wide, width), F32),
            ((coarse * planes, width), F32),
            ((coarse_rows, side, width), F32),
            ((width, 2 * width), BF16),
            ((6 * width, 2 * width), BF16),
            ((width, width), BF16),
            ((width, coarse_rows * 3 * coarse * width), BF16),
            ((block_rows * coarse_rows, side, width), F32),
            ((width, width), BF16),
            ((5,) + field, F32),
            (field, F32),
            ((planes, side + 2 * PAD, width), F32),
            (field, F32),
            (field, F32),
        ],
        boxes,
        jnp.stack([block_place, tissue]), fixed, moving,
    )

    message = ((devices, 1, LANES), F32)

    sent, mean, variance, halves = call(
        first_kernel,
        [message, (field, F32), (field, F32), ((2,) + halo[0], BF16)],
        boxes + [pltpu.VMEM(field, F32)],
        image, padded, down, across, near, far, marks, cells, rows, cols, box, own,
    )
    received = lax.all_to_all(sent, ("blk", "gz"), 0, 0).reshape(devices, LANES)
    sent, correlation, velocity = call(
        second_kernel,
        [message, (field, F32), ((8 * block_rows * coarse_rows, LANES), F32)],
        [
            pltpu.VMEM((2, REACH, side, width), F32),
            pltpu.VMEM((2, REACH + 1, side + 2 * PAD, width), F32),
            pltpu.VMEM((2, REACH, side, width), F32),
            pltpu.VMEM((2, wide, side, width), F32),
            pltpu.VMEM((3, coarse, side, width), F32),
            pltpu.VMEM((wide, side + 2 * PAD, width), F32),
            pltpu.VMEM((3, planes, side + 2 * PAD, width), F32),
            pltpu.VMEM((3, planes, side + 2 * PAD, width), F32),
            pltpu.VMEM((3 * planes * side // 2, 6 * width), BF16),
            pltpu.VMEM(field, F32),
        ],
        received, halves, image, padded, down, across, marks,
        mean, variance, hats, cells, rows, cols, box, slope,
        spread, hat_x, hat_y,
    )
    received = lax.all_to_all(sent, ("blk", "gz"), 0, 0).reshape(devices, LANES)
    grid = (3, coarse, block_rows * coarse_rows, GY * coarse_cols)
    return tuple(
        call(
            last_kernel,
            [(grid, F32), ((slots,) + field, F32)],
            [pltpu.VMEM(grid, F32), pltpu.SemaphoreType.DMA((2,))],
            received, velocity, spread, correlation,
            out_specs=[HBM, HBM],
        )
    )


def solution(mesh):
    return jax.shard_map(
        per_device,
        mesh=mesh,
        in_specs=(P("blk", "gz", None, None), P("blk", "gz", None, None), P("blk"), P("blk")),
        out_specs=(P(), P("blk", "gz", None, None)),
        check_vma=False,
    )
```

```python
import functools
import math

import jax
import jax.numpy as jnp
from jax import lax
from jax.experimental import pallas as pl
from jax.experimental.pallas import tpu as pltpu
from jax.sharding import PartitionSpec as P

SCALE = 16
GY = 8
EPSILON = 1e-05
STEP_LENGTH = 0.5
GAUSS_RAW = [math.exp(-((offset - 3) ** 2) / 4.5) for offset in range(7)]
GAUSS_TAPS = [value / sum(GAUSS_RAW) for value in GAUSS_RAW]
REACH = 4
PAD = 8
LANES = 128
F32 = jnp.float32
BF16 = jnp.bfloat16


def cell_weights(index, cell):
    total = jnp.zeros(index.shape, F32)
    for offset, weight in enumerate(GAUSS_TAPS):
        target = index + (offset - 3)
        inside = (target >= cell * SCALE) & (target < cell * SCALE + SCALE)
        total = total + jnp.where(inside, weight, 0.0)
    return total


def hat(index, cell, count):
    where = jnp.clip((index.astype(F32) + 0.5) * (1.0 / SCALE) - 0.5, 0.0, count - 1.0)
    return jnp.maximum(0.0, 1.0 - jnp.abs(where - cell.astype(F32)))


def lane_index(shape):
    return lax.broadcasted_iota(jnp.int32, shape, len(shape) - 1)


def sublane_index(shape):
    return lax.broadcasted_iota(jnp.int32, shape, len(shape) - 2)


def split(value, count):
    parts = []
    for _ in range(count):
        parts.append(value.astype(BF16))
        value = value - parts[-1].astype(F32)
    return parts


def close_dot(value, table):
    rows = value.shape[0]
    product = jnp.dot(
        jnp.concatenate(split(value, 2), axis=0), table, preferred_element_type=F32
    )
    return product[:rows] + product[rows:]


def window_of_nine(items):
    two = [a + b for a, b in zip(items[:-1], items[1:])]
    four = [a + b for a, b in zip(two[:-2], two[2:])]
    eight = [a + b for a, b in zip(four[:-4], four[4:])]
    return [a + b for a, b in zip(eight[:-1], items[8:])]


def padded_rows(side):
    return slice(PAD, PAD + side)


def clear_edges(ref, side):
    edge = jnp.zeros(ref.shape[:-2] + (PAD, LANES), F32)
    ref[..., 0:PAD, :] = edge
    ref[..., PAD + side :, :] = edge


def row_box(value, padded, three):
    side = value.shape[0]
    rows = padded_rows(side)
    middle = padded[PAD - 1 : PAD - 1 + side] + value + padded[PAD + 1 : PAD + 1 + side]
    three[0:PAD] = padded[1 : PAD + 1]
    three[rows] = middle
    three[PAD + side :] = padded[PAD + side - 1 : 2 * PAD + side - 1]
    return three[PAD - 3 : PAD - 3 + side] + middle + three[PAD + 3 : PAD + 3 + side]


def row_difference(padded, side):
    return padded[PAD + 1 : PAD + 1 + side] - padded[PAD - 1 : PAD - 1 + side]


def col_difference(plane):
    width = plane.shape[1]
    lane = lane_index(plane.shape)
    upper = jnp.where(lane < width - 1, pltpu.roll(plane, width - 1, 1), 0.0)
    lower = jnp.where(lane > 0, pltpu.roll(plane, 1, 1), 0.0)
    return upper - lower


def box_sums(fields, planes, side, sums, threes, parts, box_ref):
    half = planes // 2
    count = sums.shape[0]
    clear_edges(sums, side)
    for tile in range(side // 8):
        for f, items in enumerate(fields(8 * tile)):
            for z, item in enumerate(window_of_nine(items)):
                sums[f, z, PAD + 8 * tile : PAD + 8 * tile + 8] = item
    step = half // 4
    results = []
    for first in range(0, half, step):
        for i in range(first, first + step):
            for f in range(count):
                start = (i * count + f) * side
                for h in range(2):
                    z = i + h * half
                    total = row_box(sums[f, z, padded_rows(side)], sums.at[f, z], threes.at[f, z])
                    for part, rounded in enumerate(split(total, 3)):
                        lane = (2 * part + h) * LANES
                        parts[start : start + side, lane : lane + LANES] = rounded
        used = slice(first * count * side, (first + step) * count * side)
        results.append(jnp.dot(parts[used], box_ref[...], preferred_element_type=F32))

    def of(f, z):
        i, lane = z % half, (z // half) * LANES
        start = ((i % step) * count + f) * side
        return results[i // step][start : start + side, lane : lane + LANES]

    return of


def column_boxes(fixed, moving, side, pairs, single, double, box_ref):
    step = pairs
    results = []
    for first in range(0, pairs, step):
        for i in range(first, first + step):
            for h in range(2):
                lane = h * LANES
                planes = (fixed(i, h), moving(i, h))
                for f, plane in enumerate(planes):
                    start = (2 * i + f) * side
                    single[start : start + side, lane : lane + LANES] = plane
                a, b = (plane.astype(F32) for plane in planes)
                for f, product in enumerate((a * a, b * b, a * b)):
                    start = (3 * i + f) * side
                    high, low = split(product, 2)
                    double[start : start + side, lane : lane + LANES] = high
                    double[start : start + side, 2 * LANES + lane : 3 * LANES + lane] = low
        ones = single[2 * first * side : 2 * (first + step) * side]
        twos = double[3 * first * side : 3 * (first + step) * side]
        results.append(
            (
                jnp.dot(ones, box_ref[0 : 2 * LANES], preferred_element_type=F32),
                jnp.dot(twos, box_ref[0 : 4 * LANES], preferred_element_type=F32),
            )
        )

    def of(f, i, h):
        source, count, f = (0, 2, f) if f < 2 else (1, 3, f - 2)
        start = ((i % step) * count + f) * side
        return results[i // step][source][start : start + side, h * LANES : (h + 1) * LANES]

    return of


def running(items):
    total = [items[0]]
    for item in items[1:]:
        total.append(total[-1] + item)
    return total


def force_message(weights, slopes, planes, cells_ref, rows_ref, cols_ref, marks_ref):
    coarse = cells_ref.shape[0] // planes
    coarse_rows, side, _ = rows_ref.shape
    total = [[None] * coarse for _ in range(3)]
    for z in range(planes):
        directions = slopes(z)
        for k in range(coarse):
            index = k * planes + z
            share = weights(z) * cells_ref[index : index + 1, :]
            for c in range(3):
                term = share * directions[c]
                total[c][k] = term if z == 0 else total[c][k] + term
    tiles = []
    for c in range(3):
        for k in range(coarse):
            for a in range(coarse_rows):
                product = total[c][k] * rows_ref[a]
                tile = product[0:8]
                for start in range(8, side, 8):
                    tile = tile + product[start : start + 8]
                tiles.append(tile)
    sums = close_dot(jnp.concatenate(tiles, axis=0), cols_ref[...])
    sums = sums[:, :LANES] + sums[:, LANES:]
    coarse_cols = LANES // SCALE
    lane = lane_index((8, LANES))
    picked = jnp.zeros((8, LANES), F32)
    for g in range(len(tiles)):
        picked = jnp.where(lane // coarse_cols == g, sums[8 * g : 8 * g + 8], picked)
    row = jnp.sum(picked, axis=0, keepdims=True) * marks_ref[1:2]
    return jnp.where(lane[0:1] == len(tiles) * coarse_cols, marks_ref[0:1], row)


def regular_grid(received, spread_ref, coarse, block_rows, coarse_rows, coarse_cols):
    groups = 3 * coarse
    used = groups * coarse_rows * coarse_cols
    width = GY * coarse_cols
    place = received[:, used : used + 1].astype(jnp.int32)
    here = (place % GY) == lane_index(received.shape) // coarse_cols
    block_row = place // GY
    sub = sublane_index((8, LANES))
    entries = close_dot(received, spread_ref[...])
    grids = []
    for r in range(block_rows):
        chosen = here if block_rows == 1 else here & (block_row == r)
        for a in range(coarse_rows):
            grid = jnp.zeros((8, LANES), F32)
            for g in range(groups):
                start = (a * groups + g) * LANES
                entry = jnp.where(chosen, entries[:, start : start + LANES], 0.0)
                grid = jnp.where(sub == g, jnp.sum(entry, axis=0, keepdims=True), grid)
            grids.append(grid)
    none = [jnp.zeros((8, LANES), F32)]
    grids = [
        0.5 * g + 0.25 * (before + after)
        for g, before, after in zip(grids, none + grids[:-1], grids[1:] + none)
    ]
    before_columns = grids
    inside = lane_index((8, LANES)) < width
    grids = [
        jnp.where(
            inside, 0.5 * g + 0.25 * (pltpu.roll(g, 1, 1) + pltpu.roll(g, LANES - 1, 1)), 0.0
        )
        for g in grids
    ]
    square = functools.reduce(lambda a, b: a + b, [g * g for g in grids])
    square = jnp.sum(jnp.sum(square, axis=0, keepdims=True), axis=1, keepdims=True)
    mean = square * (1.0 / (groups * len(grids) * width))
    return before_columns, grids, STEP_LENGTH / jnp.sqrt(mean + EPSILON)


def pack_kernel(fixed_hbm, moving_hbm, near_ref, far_ref, fixed_ref, moving_ref, sems):
    copies = [
        pltpu.make_async_copy(source.at[0], target, sems.at[i])
        for i, (source, target) in enumerate(((fixed_hbm, fixed_ref), (moving_hbm, moving_ref)))
    ]
    for copy in copies:
        copy.start()
    planes = fixed_ref.shape[0]
    part = lax.axis_index("gz")
    odd = part % 2
    inner = (part > 0) & (part < lax.axis_size("gz") - 1)
    for copy in copies:
        copy.wait()
    for ref, low, keep in ((far_ref, odd == 0, inner), (near_ref, odd == 1, None)):
        i = fixed_ref[pl.ds(jnp.where(low, 0, planes - REACH), REACH)]
        j = moving_ref[pl.ds(jnp.where(low, 0, planes - REACH - 1), REACH + 1)]
        if keep is not None:
            i = jnp.where(keep, i.astype(F32), 0.0).astype(BF16)
            j = jnp.where(keep, j.astype(F32), 0.0).astype(BF16)
        ref[0:REACH] = i
        ref[REACH:] = j


def table_kernel(
    both_ref, fixed_ref, moving_ref,
    marks_ref, hats_ref, cells_ref, rows_ref, cols_ref, box_ref, slope_ref, spread_ref, hat_x_ref, hat_y_ref,
    own_ref, image_ref, planes_ref, down_ref, across_ref,
    single, double, sums, threes,
    *, block_rows,
):
    planes = fixed_ref.shape[0]
    part = lax.axis_index("gz")
    total = planes * lax.axis_size("gz")
    coarse_rows, side, _ = rows_ref.shape
    coarse_cols = LANES // SCALE
    width = GY * coarse_cols
    wide = planes + 2 * REACH
    row = sublane_index(hats_ref.shape)
    z = part * planes + row % wide - REACH
    hats_ref[...] = jnp.where((z >= 0) & (z < total), hat(z, row // wide, total // SCALE), 0.0)
    row = sublane_index(cells_ref.shape)
    cells_ref[...] = cell_weights(part * planes + row % planes, row // planes)
    for a in range(coarse_rows):
        rows_ref[a] = 0.5 * cell_weights(sublane_index((side, LANES)), a)
    square = (LANES, LANES)
    cols = cell_weights(sublane_index(square), lane_index(square) % coarse_cols)
    for i, value in enumerate(split(cols, 2)):
        cols_ref[:, i * LANES : (i + 1) * LANES] = value
    apart = sublane_index(square) - lane_index(square)
    band = jnp.where(jnp.abs(apart) <= 4, 1.0, 0.0).astype(BF16)
    box_ref[...] = jnp.zeros(box_ref.shape, BF16)
    for i in range(6):
        lane = (i % 2) * LANES
        box_ref[i * LANES : (i + 1) * LANES, lane : lane + LANES] = band
    slope = jnp.where(apart == 1, 1.0, jnp.where(apart == -1, -1.0, 0.0)).astype(BF16)
    slope_ref[...] = slope
    across = jnp.dot(
        moving_ref[...].reshape(planes * side, LANES), slope, preferred_element_type=F32
    )
    across_ref[...] = across.reshape(across_ref.shape)
    image_ref[...] = fixed_ref[...].astype(F32)
    clear_edges(planes_ref, side)
    planes_ref[:, padded_rows(side)] = moving_ref[...].astype(F32)
    for z in range(planes):
        down_ref[z] = row_difference(planes_ref.at[z], side)
    lane = lane_index(square)
    entry = sublane_index(square)
    coarse = total // SCALE
    group = coarse_rows * coarse_cols
    for a in range(coarse_rows):
        for c in range(3):
            for k in range(coarse):
                value = jnp.zeros(square, F32)
                for other, weight in ((k - 1, 0.25), (k, 0.5), (k + 1, 0.25)):
                    if 0 <= other < coarse:
                        start = (c * coarse + other) * group + a * coarse_cols
                        hit = (entry == start + lane % coarse_cols) & (lane < width)
                        value = jnp.where(hit, weight, value)
                start = ((a * 3 + c) * coarse + k) * LANES
                spread_ref[:, start : start + LANES] = value.astype(BF16)
    row = sublane_index(marks_ref.shape)
    marks_ref[...] = jnp.where(row == 0, both_ref[0:1, 0:1], both_ref[1:2, 0:1]).astype(F32)
    place = both_ref[0:1, 0:1]
    y = lane + (place % GY) * LANES
    hat_y = jnp.where(entry < width, hat(y, entry, width), 0.0)
    hat_y = 0.5 * hat_y + 0.25 * (pltpu.roll(hat_y, 1, 0) + pltpu.roll(hat_y, LANES - 1, 0))
    hat_y_ref[...] = jnp.where(entry < width, hat_y, 0.0).astype(BF16)
    x = sublane_index((side, LANES)) + (place // GY) * side
    for r in range(block_rows * coarse_rows):
        hat_x_ref[r] = 0.5 * hat(x, jnp.full((1, 1), r, jnp.int32), block_rows * coarse_rows)

    of = column_boxes(
        lambda i, h: fixed_ref[i + REACH * h],
        lambda i, h: moving_ref[i + REACH * h],
        side, REACH, single, double, box_ref,
    )
    clear_edges(sums, side)
    for f in range(5):
        boxed = [of(f, i, h) for h in range(2) for i in range(REACH)]
        up, down = running(boxed), running(boxed[::-1])[::-1]
        for z in range(planes):
            item = up[z + REACH] if z < REACH else down[z - REACH]
            sums[f, z, padded_rows(side)] = item
            own_ref[f, z] = row_box(item, sums.at[f, z], threes.at[f, z])


def add_side(planes_ref, below, box_ref, before_ref, after_ref, single, double, sums, threes):
    side = planes_ref.shape[1]

    def at(first, count, distance):
        return planes_ref[first + jnp.where(below, count - distance, distance - 1)]

    of = column_boxes(
        lambda i, h: at(0, REACH, 1 + i + 2 * h),
        lambda i, h: at(REACH, REACH + 1, 1 + i + 2 * h),
        side, REACH // 2, single, double, box_ref,
    )
    clear_edges(sums, side)
    for f in range(5):
        boxed = [of(f, d % 2, d // 2) for d in range(REACH)]
        for d, item in enumerate(running(boxed)):
            sums[f, d, padded_rows(side)] = item
            z = jnp.where(below, REACH - 1 - d, REACH + d)
            other = jnp.where(below, REACH + d, REACH - 1 - d)
            after_ref[f, z] = before_ref[f, z] + row_box(item, sums.at[f, d], threes.at[f, d])
            after_ref[f, other] = before_ref[f, other]


def near_kernel(near_ref, box_ref, own_ref, total_ref, *scratch):
    odd = lax.axis_index("gz") % 2 == 1
    add_side(near_ref, odd, box_ref, own_ref, total_ref, *scratch)


def first_kernel(
    image_ref, planes_ref, down_ref, across_ref, near_ref, far_ref, marks_ref,
    cells_ref, rows_ref, cols_ref, box_ref, near_total_ref,
    message_ref, mean_ref, variance_ref, halves,
    total_ref, weight, *scratch,
):
    planes, side, _ = image_ref.shape
    rows = padded_rows(side)
    odd = lax.axis_index("gz") % 2 == 1
    add_side(far_ref, ~odd, box_ref, near_total_ref, total_ref, *scratch)
    below = jnp.where(odd, 0, 1)
    halves[below] = near_ref[...]
    halves[1 - below] = far_ref[...]
    for z in range(planes):
        mean_i, mean_w, mean_ii, mean_ww, mean_iw = [
            total_ref[f, z] * (1.0 / 729.0) for f in range(5)
        ]
        sii = mean_ii - mean_i * mean_i
        sww = mean_ww - mean_w * mean_w
        siw = mean_iw - mean_i * mean_w
        mean_ref[z] = mean_i
        variance_ref[z] = sii
        ratio = siw / (sii * sww + EPSILON)
        weight[z] = (2.0 * ratio) * (
            (image_ref[z] - mean_i) - siw / (sww + EPSILON) * (planes_ref[z, rows] - mean_w)
        )

    def plane(z):
        if z < 0:
            return halves[0, 2 * REACH + 1 + z].astype(F32)
        return planes_ref[z, rows] if z < planes else halves[1, REACH + z - planes].astype(F32)

    row = force_message(
        lambda z: weight[z],
        lambda z: (plane(z + 1) - plane(z - 1), down_ref[z], across_ref[z]),
        planes, cells_ref, rows_ref, cols_ref, marks_ref,
    )
    message_ref[...] = jnp.broadcast_to(row[None], message_ref.shape)


def second_kernel(
    received_ref, halves, image_ref, planes_ref, down_ref, across_ref, marks_ref,
    mean_ref, variance_ref, hats_ref, cells_ref, rows_ref, cols_ref, box_ref, slope_ref,
    spread_ref, hat_x_ref, hat_y_ref,
    message_ref, map_ref, velocity_ref,
    images, outer, outer_across, slopes, shift_ref, warped, sums, threes, parts, weight,
):
    planes, side, _ = mean_ref.shape
    wide = planes + 2 * REACH
    coarse_rows = rows_ref.shape[0]
    coarse_cols = LANES // SCALE
    block_rows = velocity_ref.shape[0] // 8 // coarse_rows
    coarse = hats_ref.shape[0] // wide
    rows = padded_rows(side)

    def image(z):
        if z < 0:
            return images.at[0, z + REACH]
        return image_ref.at[z] if z < planes else images.at[1, z - planes]

    def moving(z):
        if z < 0:
            return outer.at[0, z + REACH + 1]
        return planes_ref.at[z] if z < planes else outer.at[1, z - planes]

    before_columns, grids, factor = regular_grid(
        received_ref[...], spread_ref, coarse, block_rows, coarse_rows, coarse_cols
    )
    along = close_dot(jnp.concatenate(before_columns, axis=0), hat_y_ref[...]) * factor
    for r, grid in enumerate(grids):
        velocity_ref[8 * r : 8 * r + 8] = grid * factor
    shift = [[None] * coarse for _ in range(3)]
    for r in range(len(grids)):
        for c in range(3):
            for k in range(coarse):
                g = 8 * r + c * coarse + k
                term = hat_x_ref[r] * along[g : g + 1]
                shift[c][k] = term if r == 0 else shift[c][k] + term
    for c in range(3):
        for k in range(coarse):
            shift_ref[c, k] = shift[c][k] if k == 0 else shift[c][k] - shift[c][0]

    clear_edges(outer, side)
    for h in range(2):
        images[h] = halves[h, 0:REACH].astype(F32)
        outer[h, :, rows] = halves[h, REACH:].astype(F32)
        across = jnp.dot(
            halves[h, REACH + 1 - h : 2 * REACH + 1 - h].reshape(REACH * side, LANES),
            slope_ref[...],
            preferred_element_type=F32,
        )
        outer_across[h] = across.reshape(outer_across.shape[1:])
    for z in range(-REACH, planes + REACH):
        slope = moving(z + 1)[rows] - moving(z - 1)[rows]
        if not 0 <= z < planes:
            hats = [hats_ref[pl.ds(k * wide + z + REACH, 1), :] for k in range(coarse)]
            slope = slope * functools.reduce(lambda a, b: a + b, hats)
            slopes[1, z + REACH] = row_difference(moving(z), side)
        slopes[0, z + REACH] = slope

    @pl.when(lax.axis_index("gz") >= 0)
    def _():
        for z in range(-REACH, planes + REACH):
            hats = [hats_ref[pl.ds(k * wide + z + REACH, 1), :] for k in range(coarse)]
            if z < 0:
                down, across = slopes[1, z + REACH], outer_across[0, z + REACH]
            elif z < planes:
                down, across = down_ref[z], across_ref[z]
            else:
                down, across = slopes[1, z + REACH], outer_across[1, z - planes]
            plane = moving(z)[rows]
            for c, slope in enumerate((slopes[0, z + REACH], down, across)):
                u = shift_ref[c, 0]
                for k in range(1, coarse):
                    u = u + hats[k] * shift_ref[c, k]
                plane = plane + u * slope
            warped[z + REACH, rows] = plane
        clear_edges(warped, side)

        def fields(start):
            i = [image(z)[start : start + 8] for z in range(-REACH, planes + REACH)]
            w = [warped[z, PAD + start : PAD + start + 8] for z in range(wide)]
            return (w, [b * b for b in w], [a * b for a, b in zip(i, w)])

        of = box_sums(fields, planes, side, sums, threes, parts, box_ref)
        for z in range(planes):
            mean_w, mean_ww, mean_iw = [of(f, z) * (1.0 / 729.0) for f in range(3)]
            mean_i = mean_ref[z]
            sii = variance_ref[z]
            sww = mean_ww - mean_w * mean_w
            siw = mean_iw - mean_i * mean_w
            ratio = siw / (sii * sww + EPSILON)
            map_ref[z] = siw * ratio
            weight[z] = (2.0 * ratio) * (
                (image_ref[z] - mean_i)
                - siw / (sww + EPSILON) * (warped[z + REACH, rows] - mean_w)
            )
        row = force_message(
            lambda z: weight[z],
            lambda z: (
                warped[z + REACH + 1, rows] - warped[z + REACH - 1, rows],
                row_difference(warped.at[z + REACH], side),
                col_difference(warped[z + REACH, rows]),
            ),
            planes, cells_ref, rows_ref, cols_ref, marks_ref,
        )
        message_ref[...] = jnp.broadcast_to(row[None], message_ref.shape)


def last_kernel(
    received_ref, velocity_ref, spread_ref, map_ref, out_hbm, map_hbm, out_ref, sems
):
    map_copy = pltpu.make_async_copy(map_ref, map_hbm.at[0], sems.at[0])
    map_copy.start()
    _, coarse, rows, width = out_ref.shape
    coarse_cols = width // GY
    coarse_rows = spread_ref.shape[1] // (3 * coarse * LANES)
    block_rows = rows // coarse_rows
    _, grids, factor = regular_grid(
        received_ref[...], spread_ref, coarse, block_rows, coarse_rows, coarse_cols
    )
    for r, grid in enumerate(grids):
        velocity = velocity_ref[8 * r : 8 * r + 8] + grid * factor
        for c in range(3):
            for k in range(coarse):
                g = c * coarse + k
                out_ref[c, k, r : r + 1, :] = velocity[g : g + 1, :width]
    out_copy = pltpu.make_async_copy(out_ref, out_hbm, sems.at[1])
    out_copy.start()
    map_copy.wait()
    out_copy.wait()


def far_pairs(blocks, parts):
    pairs = []
    for block in range(blocks):
        for part in range(1, parts - 1, 2):
            low, high = block * parts + part, block * parts + part + 1
            pairs += [(low, high), (high, low)]
        for part in (0, parts - 1):
            pairs.append((block * parts + part, (block ^ 1) * parts + part))
    return pairs


VMEM = pl.BlockSpec(memory_space=pltpu.VMEM)
HBM = pl.BlockSpec(memory_space=pl.ANY)


def call(kernel, outs, scratch, *operands, in_specs=None, out_specs=None):
    return pl.pallas_call(
        kernel,
        out_shape=[jax.ShapeDtypeStruct(shape, dtype) for shape, dtype in outs],
        in_specs=in_specs or [VMEM] * len(operands),
        out_specs=out_specs or [VMEM] * len(outs),
        scratch_shapes=scratch,
        compiler_params=pltpu.CompilerParams(vmem_limit_bytes=24 << 20),
    )(*operands)


def per_device(fixed, moving, block_place, tissue):
    slots, planes, side, width = fixed.shape
    assert slots == 1 and width == LANES and planes == 2 * REACH
    depth_parts = lax.axis_size("gz")
    devices = lax.axis_size("blk") * depth_parts
    blocks = slots * lax.axis_size("blk")
    coarse = planes * depth_parts // SCALE
    coarse_rows, coarse_cols = side // SCALE, width // SCALE
    block_rows = blocks // GY
    wide = planes + 2 * REACH
    field = (planes, side, width)
    halo = ((2 * REACH + 1, side, width), BF16)

    near, far, fixed, moving = call(
        pack_kernel,
        [halo, halo, (field, BF16), (field, BF16)],
        [pltpu.SemaphoreType.DMA((2,))],
        pltpu.with_memory_space_constraint(fixed, pltpu.HBM),
        pltpu.with_memory_space_constraint(moving, pltpu.HBM),
        in_specs=[HBM] * 2,
    )
    far = lax.ppermute(far, ("blk", "gz"), far_pairs(lax.axis_size("blk"), depth_parts))
    pairs = [(i, i + 1) for i in range(0, depth_parts, 2)]
    near = lax.ppermute(near, "gz", pairs + [(b, a) for a, b in pairs])
    boxes = [
        pltpu.VMEM((2 * REACH * side, 2 * width), BF16),
        pltpu.VMEM((3 * REACH * side, 4 * width), BF16),
        pltpu.VMEM((5, planes, side + 2 * PAD, width), F32),
        pltpu.VMEM((5, planes, side + 2 * PAD, width), F32),
    ]
    (
        marks, hats, cells, rows, cols, box, slope, spread, hat_x, hat_y,
        own, image, padded, down, across,
    ) = call(
        functools.partial(table_kernel, block_rows=block_rows),
        [
            ((8, width), F32),
            ((coarse * wide, width), F32),
            ((coarse * planes, width), F32),
            ((coarse_rows, side, width), F32),
            ((width, 2 * width), BF16),
            ((6 * width, 2 * width), BF16),
            ((width, width), BF16),
            ((width, coarse_rows * 3 * coarse * width), BF16),
            ((block_rows * coarse_rows, side, width), F32),
            ((width, width), BF16),
            ((5,) + field, F32),
            (field, F32),
            ((planes, side + 2 * PAD, width), F32),
            (field, F32),
            (field, F32),
        ],
        boxes,
        jnp.stack([block_place, tissue]), fixed, moving,
    )

    message = ((devices, 1, LANES), F32)

    half_boxes = [
        pltpu.VMEM((REACH * side, 2 * width), BF16),
        pltpu.VMEM((3 * REACH // 2 * side, 4 * width), BF16),
        pltpu.VMEM((5, REACH, side + 2 * PAD, width), F32),
        pltpu.VMEM((5, REACH, side + 2 * PAD, width), F32),
    ]
    (total,) = call(near_kernel, [((5,) + field, F32)], half_boxes, near, box, own)
    sent, mean, variance, halves = call(
        first_kernel,
        [message, (field, F32), (field, F32), ((2,) + halo[0], BF16)],
        [pltpu.VMEM((5,) + field, F32), pltpu.VMEM(field, F32)] + half_boxes,
        image, padded, down, across, near, far, marks, cells, rows, cols, box, total,
    )
    received = lax.all_to_all(sent, ("blk", "gz"), 0, 0).reshape(devices, LANES)
    sent, correlation, velocity = call(
        second_kernel,
        [message, (field, F32), ((8 * block_rows * coarse_rows, LANES), F32)],
        [
            pltpu.VMEM((2, REACH, side, width), F32),
            pltpu.VMEM((2, REACH + 1, side + 2 * PAD, width), F32),
            pltpu.VMEM((2, REACH, side, width), F32),
            pltpu.VMEM((2, wide, side, width), F32),
            pltpu.VMEM((3, coarse, side, width), F32),
            pltpu.VMEM((wide, side + 2 * PAD, width), F32),
            pltpu.VMEM((3, planes, side + 2 * PAD, width), F32),
            pltpu.VMEM((3, planes, side + 2 * PAD, width), F32),
            pltpu.VMEM((3 * planes * side // 2, 6 * width), BF16),
            pltpu.VMEM(field, F32),
        ],
        received, halves, image, padded, down, across, marks,
        mean, variance, hats, cells, rows, cols, box, slope,
        spread, hat_x, hat_y,
    )
    received = lax.all_to_all(sent, ("blk", "gz"), 0, 0).reshape(devices, LANES)
    grid = (3, coarse, block_rows * coarse_rows, GY * coarse_cols)
    return tuple(
        call(
            last_kernel,
            [(grid, F32), ((slots,) + field, F32)],
            [pltpu.VMEM(grid, F32), pltpu.SemaphoreType.DMA((2,))],
            received, velocity, spread, correlation,
            out_specs=[HBM, HBM],
        )
    )


def solution(mesh):
    return jax.shard_map(
        per_device,
        mesh=mesh,
        in_specs=(P("blk", "gz", None, None), P("blk", "gz", None, None), P("blk"), P("blk")),
        out_specs=(P(), P("blk", "gz", None, None)),
        check_vma=False,
    )
```

```python
import functools
import math

import jax
import jax.numpy as jnp
from jax import lax
from jax.experimental import pallas as pl
from jax.experimental.pallas import tpu as pltpu
from jax.sharding import PartitionSpec as P

SCALE = 16
GY = 8
EPSILON = 1e-05
STEP_LENGTH = 0.5
GAUSS_RAW = [math.exp(-((offset - 3) ** 2) / 4.5) for offset in range(7)]
GAUSS_TAPS = [value / sum(GAUSS_RAW) for value in GAUSS_RAW]
REACH = 4
PAD = 8
LANES = 128
F32 = jnp.float32
BF16 = jnp.bfloat16


def cell_weights(index, cell):
    total = jnp.zeros(index.shape, F32)
    for offset, weight in enumerate(GAUSS_TAPS):
        target = index + (offset - 3)
        inside = (target >= cell * SCALE) & (target < cell * SCALE + SCALE)
        total = total + jnp.where(inside, weight, 0.0)
    return total


def hat(index, cell, count):
    where = jnp.clip((index.astype(F32) + 0.5) * (1.0 / SCALE) - 0.5, 0.0, count - 1.0)
    return jnp.maximum(0.0, 1.0 - jnp.abs(where - cell.astype(F32)))


def lane_index(shape):
    return lax.broadcasted_iota(jnp.int32, shape, len(shape) - 1)


def sublane_index(shape):
    return lax.broadcasted_iota(jnp.int32, shape, len(shape) - 2)


def split(value, count):
    parts = []
    for _ in range(count):
        parts.append(value.astype(BF16))
        value = value - parts[-1].astype(F32)
    return parts


def close_dot(value, table):
    rows = value.shape[0]
    product = jnp.dot(
        jnp.concatenate(split(value, 2), axis=0), table, preferred_element_type=F32
    )
    return product[:rows] + product[rows:]


def window_of_nine(items):
    two = [a + b for a, b in zip(items[:-1], items[1:])]
    four = [a + b for a, b in zip(two[:-2], two[2:])]
    eight = [a + b for a, b in zip(four[:-4], four[4:])]
    return [a + b for a, b in zip(eight[:-1], items[8:])]


def padded_rows(side):
    return slice(PAD, PAD + side)


def clear_edges(ref, side):
    edge = jnp.zeros(ref.shape[:-2] + (PAD, LANES), F32)
    ref[..., 0:PAD, :] = edge
    ref[..., PAD + side :, :] = edge


def row_box(value, padded, three):
    side = value.shape[0]
    rows = padded_rows(side)
    middle = padded[PAD - 1 : PAD - 1 + side] + value + padded[PAD + 1 : PAD + 1 + side]
    three[0:PAD] = padded[1 : PAD + 1]
    three[rows] = middle
    three[PAD + side :] = padded[PAD + side - 1 : 2 * PAD + side - 1]
    return three[PAD - 3 : PAD - 3 + side] + middle + three[PAD + 3 : PAD + 3 + side]


def row_difference(padded, side):
    return padded[PAD + 1 : PAD + 1 + side] - padded[PAD - 1 : PAD - 1 + side]


def col_difference(plane):
    width = plane.shape[1]
    lane = lane_index(plane.shape)
    upper = jnp.where(lane < width - 1, pltpu.roll(plane, width - 1, 1), 0.0)
    lower = jnp.where(lane > 0, pltpu.roll(plane, 1, 1), 0.0)
    return upper - lower


def box_sums(fields, planes, side, sums, threes, parts, box_ref):
    half = planes // 2
    count = sums.shape[0]
    clear_edges(sums, side)
    for tile in range(side // 8):
        for f, items in enumerate(fields(8 * tile)):
            for z, item in enumerate(window_of_nine(items)):
                sums[f, z, PAD + 8 * tile : PAD + 8 * tile + 8] = item
    step = half // 4
    results = []
    for first in range(0, half, step):
        for i in range(first, first + step):
            for f in range(count):
                start = (i * count + f) * side
                for h in range(2):
                    z = i + h * half
                    total = row_box(sums[f, z, padded_rows(side)], sums.at[f, z], threes.at[f, z])
                    for part, rounded in enumerate(split(total, 3)):
                        lane = (2 * part + h) * LANES
                        parts[start : start + side, lane : lane + LANES] = rounded
        used = slice(first * count * side, (first + step) * count * side)
        results.append(jnp.dot(parts[used], box_ref[...], preferred_element_type=F32))

    def of(f, z):
        i, lane = z % half, (z // half) * LANES
        start = ((i % step) * count + f) * side
        return results[i // step][start : start + side, lane : lane + LANES]

    return of


def column_boxes(fixed, moving, side, pairs, single, double, box_ref):
    step = pairs
    results = []
    for first in range(0, pairs, step):
        for i in range(first, first + step):
            for h in range(2):
                lane = h * LANES
                planes = (fixed(i, h), moving(i, h))
                for f, plane in enumerate(planes):
                    start = (2 * i + f) * side
                    single[start : start + side, lane : lane + LANES] = plane
                a, b = (plane.astype(F32) for plane in planes)
                for f, product in enumerate((a * a, b * b, a * b)):
                    start = (3 * i + f) * side
                    high, low = split(product, 2)
                    double[start : start + side, lane : lane + LANES] = high
                    double[start : start + side, 2 * LANES + lane : 3 * LANES + lane] = low
        ones = single[2 * first * side : 2 * (first + step) * side]
        twos = double[3 * first * side : 3 * (first + step) * side]
        results.append(
            (
                jnp.dot(ones, box_ref[0 : 2 * LANES], preferred_element_type=F32),
                jnp.dot(twos, box_ref[0 : 4 * LANES], preferred_element_type=F32),
            )
        )

    def of(f, i, h):
        source, count, f = (0, 2, f) if f < 2 else (1, 3, f - 2)
        start = ((i % step) * count + f) * side
        return results[i // step][source][start : start + side, h * LANES : (h + 1) * LANES]

    return of


def running(items):
    total = [items[0]]
    for item in items[1:]:
        total.append(total[-1] + item)
    return total


def force_message(weights, slopes, planes, cells_ref, rows_ref, cols_ref, marks_ref):
    coarse = cells_ref.shape[0] // planes
    coarse_rows, side, _ = rows_ref.shape
    total = [[None] * coarse for _ in range(3)]
    for z in range(planes):
        directions = slopes(z)
        weight = weights(z)
        for k in range(coarse):
            index = k * planes + z
            share = weight * cells_ref[index : index + 1, :]
            for c in range(3):
                term = share * directions[c]
                total[c][k] = term if z == 0 else total[c][k] + term
    tiles = []
    for c in range(3):
        for k in range(coarse):
            for a in range(coarse_rows):
                product = total[c][k] * rows_ref[a]
                tile = product[0:8]
                for start in range(8, side, 8):
                    tile = tile + product[start : start + 8]
                tiles.append(tile)
    sums = close_dot(jnp.concatenate(tiles, axis=0), cols_ref[...])
    sums = sums[:, :LANES] + sums[:, LANES:]
    coarse_cols = LANES // SCALE
    lane = lane_index((8, LANES))
    picked = jnp.zeros((8, LANES), F32)
    for g in range(len(tiles)):
        picked = jnp.where(lane // coarse_cols == g, sums[8 * g : 8 * g + 8], picked)
    row = jnp.sum(picked, axis=0, keepdims=True) * marks_ref[1:2]
    return jnp.where(lane[0:1] == len(tiles) * coarse_cols, marks_ref[0:1], row)


def regular_grid(received, spread_ref, coarse, block_rows, coarse_rows, coarse_cols):
    groups = 3 * coarse
    used = groups * coarse_rows * coarse_cols
    width = GY * coarse_cols
    place = received[:, used : used + 1].astype(jnp.int32)
    here = (place % GY) == lane_index(received.shape) // coarse_cols
    block_row = place // GY
    sub = sublane_index((8, LANES))
    entries = close_dot(received, spread_ref[...])
    grids = []
    for r in range(block_rows):
        chosen = here if block_rows == 1 else here & (block_row == r)
        for a in range(coarse_rows):
            grid = jnp.zeros((8, LANES), F32)
            for g in range(groups):
                start = (a * groups + g) * LANES
                entry = jnp.where(chosen, entries[:, start : start + LANES], 0.0)
                grid = jnp.where(sub == g, jnp.sum(entry, axis=0, keepdims=True), grid)
            grids.append(grid)
    none = [jnp.zeros((8, LANES), F32)]
    grids = [
        0.5 * g + 0.25 * (before + after)
        for g, before, after in zip(grids, none + grids[:-1], grids[1:] + none)
    ]
    before_columns = grids
    inside = lane_index((8, LANES)) < width
    grids = [
        jnp.where(
            inside, 0.5 * g + 0.25 * (pltpu.roll(g, 1, 1) + pltpu.roll(g, LANES - 1, 1)), 0.0
        )
        for g in grids
    ]
    square = functools.reduce(lambda a, b: a + b, [g * g for g in grids])
    square = jnp.sum(jnp.sum(square, axis=0, keepdims=True), axis=1, keepdims=True)
    mean = square * (1.0 / (groups * len(grids) * width))
    return before_columns, grids, STEP_LENGTH / jnp.sqrt(mean + EPSILON)


def pack_kernel(fixed_hbm, moving_hbm, near_ref, far_ref, fixed_ref, moving_ref, sems):
    copies = [
        pltpu.make_async_copy(source.at[0], target, sems.at[i])
        for i, (source, target) in enumerate(((fixed_hbm, fixed_ref), (moving_hbm, moving_ref)))
    ]
    for copy in copies:
        copy.start()
    planes = fixed_ref.shape[0]
    part = lax.axis_index("gz")
    odd = part % 2
    inner = (part > 0) & (part < lax.axis_size("gz") - 1)
    for copy in copies:
        copy.wait()
    for ref, low, keep in ((far_ref, odd == 0, inner), (near_ref, odd == 1, None)):
        i = fixed_ref[pl.ds(jnp.where(low, 0, planes - REACH), REACH)]
        j = moving_ref[pl.ds(jnp.where(low, 0, planes - REACH - 1), REACH + 1)]
        if keep is not None:
            i = jnp.where(keep, i.astype(F32), 0.0).astype(BF16)
            j = jnp.where(keep, j.astype(F32), 0.0).astype(BF16)
        ref[0:REACH] = i
        ref[REACH:] = j


def table_kernel(
    both_ref, fixed_ref, moving_ref,
    marks_ref, hats_ref, cells_ref, rows_ref, cols_ref, box_ref, slope_ref, spread_ref, hat_x_ref, hat_y_ref,
    own_ref, image_ref, planes_ref, down_ref, across_ref,
    single, double, sums, threes,
    *, block_rows,
):
    planes = fixed_ref.shape[0]
    part = lax.axis_index("gz")
    total = planes * lax.axis_size("gz")
    coarse_rows, side, _ = rows_ref.shape
    coarse_cols = LANES // SCALE
    width = GY * coarse_cols
    wide = planes + 2 * REACH
    row = sublane_index(hats_ref.shape)
    z = part * planes + row % wide - REACH
    hats_ref[...] = jnp.where((z >= 0) & (z < total), hat(z, row // wide, total // SCALE), 0.0)
    row = sublane_index(cells_ref.shape)
    cells_ref[...] = cell_weights(part * planes + row % planes, row // planes)
    for a in range(coarse_rows):
        rows_ref[a] = cell_weights(sublane_index((side, LANES)), a)
    square = (LANES, LANES)
    cols = cell_weights(sublane_index(square), lane_index(square) % coarse_cols)
    for i, value in enumerate(split(cols, 2)):
        cols_ref[:, i * LANES : (i + 1) * LANES] = value
    apart = sublane_index(square) - lane_index(square)
    band = jnp.where(jnp.abs(apart) <= 4, 1.0, 0.0).astype(BF16)
    box_ref[...] = jnp.zeros(box_ref.shape, BF16)
    for i in range(6):
        lane = (i % 2) * LANES
        box_ref[i * LANES : (i + 1) * LANES, lane : lane + LANES] = band
    slope = jnp.where(apart == 1, 1.0, jnp.where(apart == -1, -1.0, 0.0)).astype(BF16)
    slope_ref[...] = slope
    across = jnp.dot(
        moving_ref[...].reshape(planes * side, LANES), slope, preferred_element_type=F32
    )
    across_ref[...] = across.reshape(across_ref.shape)
    image_ref[...] = fixed_ref[...].astype(F32)
    clear_edges(planes_ref, side)
    planes_ref[:, padded_rows(side)] = moving_ref[...].astype(F32)
    for z in range(planes):
        down_ref[z] = row_difference(planes_ref.at[z], side)
    lane = lane_index(square)
    entry = sublane_index(square)
    coarse = total // SCALE
    group = coarse_rows * coarse_cols
    for a in range(coarse_rows):
        for c in range(3):
            for k in range(coarse):
                value = jnp.zeros(square, F32)
                for other, weight in ((k - 1, 0.25), (k, 0.5), (k + 1, 0.25)):
                    if 0 <= other < coarse:
                        start = (c * coarse + other) * group + a * coarse_cols
                        hit = (entry == start + lane % coarse_cols) & (lane < width)
                        value = jnp.where(hit, weight, value)
                start = ((a * 3 + c) * coarse + k) * LANES
                spread_ref[:, start : start + LANES] = value.astype(BF16)
    row = sublane_index(marks_ref.shape)
    marks_ref[...] = jnp.where(row == 0, both_ref[0:1, 0:1], both_ref[1:2, 0:1]).astype(F32)
    place = both_ref[0:1, 0:1]
    y = lane + (place % GY) * LANES
    hat_y = jnp.where(entry < width, hat(y, entry, width), 0.0)
    hat_y = 0.5 * hat_y + 0.25 * (pltpu.roll(hat_y, 1, 0) + pltpu.roll(hat_y, LANES - 1, 0))
    hat_y_ref[...] = jnp.where(entry < width, hat_y, 0.0).astype(BF16)
    x = sublane_index((side, LANES)) + (place // GY) * side
    for r in range(block_rows * coarse_rows):
        hat_x_ref[r] = 0.5 * hat(x, jnp.full((1, 1), r, jnp.int32), block_rows * coarse_rows)

    of = column_boxes(
        lambda i, h: fixed_ref[i + REACH * h],
        lambda i, h: moving_ref[i + REACH * h],
        side, REACH, single, double, box_ref,
    )
    clear_edges(sums, side)
    for f in range(5):
        boxed = [of(f, i, h) for h in range(2) for i in range(REACH)]
        up, down = running(boxed), running(boxed[::-1])[::-1]
        for z in range(planes):
            item = up[z + REACH] if z < REACH else down[z - REACH]
            sums[f, z, padded_rows(side)] = item
            own_ref[f, z] = row_box(item, sums.at[f, z], threes.at[f, z])


def add_side(planes_ref, below, box_ref, before_ref, after_ref, single, double, sums, threes):
    side = planes_ref.shape[1]

    def at(first, count, distance):
        return planes_ref[first + jnp.where(below, count - distance, distance - 1)]

    of = column_boxes(
        lambda i, h: at(0, REACH, 1 + i + 2 * h),
        lambda i, h: at(REACH, REACH + 1, 1 + i + 2 * h),
        side, REACH // 2, single, double, box_ref,
    )
    clear_edges(sums, side)
    for f in range(5):
        boxed = [of(f, d % 2, d // 2) for d in range(REACH)]
        for d, item in enumerate(running(boxed)):
            sums[f, d, padded_rows(side)] = item
            z = jnp.where(below, REACH - 1 - d, REACH + d)
            other = jnp.where(below, REACH + d, REACH - 1 - d)
            after_ref[f, z] = before_ref[f, z] + row_box(item, sums.at[f, d], threes.at[f, d])
            after_ref[f, other] = before_ref[f, other]


def near_kernel(near_ref, box_ref, own_ref, total_ref, *scratch):
    odd = lax.axis_index("gz") % 2 == 1
    add_side(near_ref, odd, box_ref, own_ref, total_ref, *scratch)


def first_kernel(
    image_ref, planes_ref, down_ref, across_ref, near_ref, far_ref, marks_ref,
    cells_ref, rows_ref, cols_ref, box_ref, near_total_ref,
    message_ref, mean_ref, variance_ref, halves,
    total_ref, *scratch,
):
    planes, side, _ = image_ref.shape
    rows = padded_rows(side)
    odd = lax.axis_index("gz") % 2 == 1
    add_side(far_ref, ~odd, box_ref, near_total_ref, total_ref, *scratch)
    below = jnp.where(odd, 0, 1)
    halves[below] = near_ref[...]
    halves[1 - below] = far_ref[...]

    def weight(z):
        mean_i, mean_w, mean_ii, mean_ww, mean_iw = [
            total_ref[f, z] * (1.0 / 729.0) for f in range(5)
        ]
        sii = mean_ii - mean_i * mean_i
        sww = mean_ww - mean_w * mean_w
        siw = mean_iw - mean_i * mean_w
        mean_ref[z] = mean_i
        variance_ref[z] = sii
        ratio = siw / (sii * sww + EPSILON)
        return ratio * (
            (image_ref[z] - mean_i) - siw / (sww + EPSILON) * (planes_ref[z, rows] - mean_w)
        )

    def plane(z):
        if z < 0:
            return halves[0, 2 * REACH + 1 + z].astype(F32)
        return planes_ref[z, rows] if z < planes else halves[1, REACH + z - planes].astype(F32)

    row = force_message(
        weight,
        lambda z: (plane(z + 1) - plane(z - 1), down_ref[z], across_ref[z]),
        planes, cells_ref, rows_ref, cols_ref, marks_ref,
    )
    message_ref[...] = jnp.broadcast_to(row[None], message_ref.shape)


def second_kernel(
    received_ref, halves, image_ref, planes_ref, down_ref, across_ref, marks_ref,
    mean_ref, variance_ref, hats_ref, cells_ref, rows_ref, cols_ref, box_ref, slope_ref,
    spread_ref, hat_x_ref, hat_y_ref,
    message_ref, map_ref, velocity_ref,
    images, outer, outer_across, slopes, shift_ref, warped, sums, threes, parts,
):
    planes, side, _ = mean_ref.shape
    wide = planes + 2 * REACH
    coarse_rows = rows_ref.shape[0]
    coarse_cols = LANES // SCALE
    block_rows = velocity_ref.shape[0] // 8 // coarse_rows
    coarse = hats_ref.shape[0] // wide
    rows = padded_rows(side)

    def image(z):
        if z < 0:
            return images.at[0, z + REACH]
        return image_ref.at[z] if z < planes else images.at[1, z - planes]

    def moving(z):
        if z < 0:
            return outer.at[0, z + REACH + 1]
        return planes_ref.at[z] if z < planes else outer.at[1, z - planes]

    before_columns, grids, factor = regular_grid(
        received_ref[...], spread_ref, coarse, block_rows, coarse_rows, coarse_cols
    )
    along = close_dot(jnp.concatenate(before_columns, axis=0), hat_y_ref[...]) * factor
    for r, grid in enumerate(grids):
        velocity_ref[8 * r : 8 * r + 8] = grid * factor
    shift = [[None] * coarse for _ in range(3)]
    for r in range(len(grids)):
        for c in range(3):
            for k in range(coarse):
                g = 8 * r + c * coarse + k
                term = hat_x_ref[r] * along[g : g + 1]
                shift[c][k] = term if r == 0 else shift[c][k] + term
    for c in range(3):
        for k in range(coarse):
            shift_ref[c, k] = shift[c][k] if k == 0 else shift[c][k] - shift[c][0]

    clear_edges(outer, side)
    for h in range(2):
        images[h] = halves[h, 0:REACH].astype(F32)
        outer[h, :, rows] = halves[h, REACH:].astype(F32)
        across = jnp.dot(
            halves[h, REACH + 1 - h : 2 * REACH + 1 - h].reshape(REACH * side, LANES),
            slope_ref[...],
            preferred_element_type=F32,
        )
        outer_across[h] = across.reshape(outer_across.shape[1:])
    for z in range(-REACH, planes + REACH):
        slope = moving(z + 1)[rows] - moving(z - 1)[rows]
        if not 0 <= z < planes:
            hats = [hats_ref[pl.ds(k * wide + z + REACH, 1), :] for k in range(coarse)]
            slope = slope * functools.reduce(lambda a, b: a + b, hats)
            slopes[1, z + REACH] = row_difference(moving(z), side)
        slopes[0, z + REACH] = slope

    @pl.when(lax.axis_index("gz") >= 0)
    def _():
        for z in range(-REACH, planes + REACH):
            hats = [hats_ref[pl.ds(k * wide + z + REACH, 1), :] for k in range(coarse)]
            if z < 0:
                down, across = slopes[1, z + REACH], outer_across[0, z + REACH]
            elif z < planes:
                down, across = down_ref[z], across_ref[z]
            else:
                down, across = slopes[1, z + REACH], outer_across[1, z - planes]
            plane = moving(z)[rows]
            for c, slope in enumerate((slopes[0, z + REACH], down, across)):
                u = shift_ref[c, 0]
                for k in range(1, coarse):
                    u = u + hats[k] * shift_ref[c, k]
                plane = plane + u * slope
            warped[z + REACH, rows] = plane
        clear_edges(warped, side)

        def fields(start):
            i = [image(z)[start : start + 8] for z in range(-REACH, planes + REACH)]
            w = [warped[z, PAD + start : PAD + start + 8] for z in range(wide)]
            return (w, [b * b for b in w], [a * b for a, b in zip(i, w)])

        of = box_sums(fields, planes, side, sums, threes, parts, box_ref)

        def weight(z):
            mean_w, mean_ww, mean_iw = [of(f, z) * (1.0 / 729.0) for f in range(3)]
            mean_i = mean_ref[z]
            sii = variance_ref[z]
            sww = mean_ww - mean_w * mean_w
            siw = mean_iw - mean_i * mean_w
            ratio = siw / (sii * sww + EPSILON)
            map_ref[z] = siw * ratio
            return ratio * (
                (image_ref[z] - mean_i)
                - siw / (sww + EPSILON) * (warped[z + REACH, rows] - mean_w)
            )

        row = force_message(
            weight,
            lambda z: (
                warped[z + REACH + 1, rows] - warped[z + REACH - 1, rows],
                row_difference(warped.at[z + REACH], side),
                col_difference(warped[z + REACH, rows]),
            ),
            planes, cells_ref, rows_ref, cols_ref, marks_ref,
        )
        message_ref[...] = jnp.broadcast_to(row[None], message_ref.shape)


def last_kernel(
    received_ref, velocity_ref, spread_ref, map_ref, out_hbm, map_hbm, out_ref, sems
):
    map_copy = pltpu.make_async_copy(map_ref, map_hbm.at[0], sems.at[0])
    map_copy.start()
    _, coarse, rows, width = out_ref.shape
    coarse_cols = width // GY
    coarse_rows = spread_ref.shape[1] // (3 * coarse * LANES)
    block_rows = rows // coarse_rows
    _, grids, factor = regular_grid(
        received_ref[...], spread_ref, coarse, block_rows, coarse_rows, coarse_cols
    )
    for r, grid in enumerate(grids):
        velocity = velocity_ref[8 * r : 8 * r + 8] + grid * factor
        for c in range(3):
            for k in range(coarse):
                g = c * coarse + k
                out_ref[c, k, r : r + 1, :] = velocity[g : g + 1, :width]
    out_copy = pltpu.make_async_copy(out_ref, out_hbm, sems.at[1])
    out_copy.start()
    map_copy.wait()
    out_copy.wait()


def far_pairs(blocks, parts):
    pairs = []
    for block in range(blocks):
        for part in range(1, parts - 1, 2):
            low, high = block * parts + part, block * parts + part + 1
            pairs += [(low, high), (high, low)]
        for part in (0, parts - 1):
            pairs.append((block * parts + part, (block ^ 1) * parts + part))
    return pairs


VMEM = pl.BlockSpec(memory_space=pltpu.VMEM)
HBM = pl.BlockSpec(memory_space=pl.ANY)


def call(kernel, outs, scratch, *operands, in_specs=None, out_specs=None):
    return pl.pallas_call(
        kernel,
        out_shape=[jax.ShapeDtypeStruct(shape, dtype) for shape, dtype in outs],
        in_specs=in_specs or [VMEM] * len(operands),
        out_specs=out_specs or [VMEM] * len(outs),
        scratch_shapes=scratch,
        compiler_params=pltpu.CompilerParams(vmem_limit_bytes=24 << 20),
    )(*operands)


def per_device(fixed, moving, block_place, tissue):
    slots, planes, side, width = fixed.shape
    assert slots == 1 and width == LANES and planes == 2 * REACH
    depth_parts = lax.axis_size("gz")
    devices = lax.axis_size("blk") * depth_parts
    blocks = slots * lax.axis_size("blk")
    coarse = planes * depth_parts // SCALE
    coarse_rows, coarse_cols = side // SCALE, width // SCALE
    block_rows = blocks // GY
    wide = planes + 2 * REACH
    field = (planes, side, width)
    halo = ((2 * REACH + 1, side, width), BF16)

    near, far, fixed, moving = call(
        pack_kernel,
        [halo, halo, (field, BF16), (field, BF16)],
        [pltpu.SemaphoreType.DMA((2,))],
        pltpu.with_memory_space_constraint(fixed, pltpu.HBM),
        pltpu.with_memory_space_constraint(moving, pltpu.HBM),
        in_specs=[HBM] * 2,
    )
    far = lax.ppermute(far, ("blk", "gz"), far_pairs(lax.axis_size("blk"), depth_parts))
    pairs = [(i, i + 1) for i in range(0, depth_parts, 2)]
    near = lax.ppermute(near, "gz", pairs + [(b, a) for a, b in pairs])
    boxes = [
        pltpu.VMEM((2 * REACH * side, 2 * width), BF16),
        pltpu.VMEM((3 * REACH * side, 4 * width), BF16),
        pltpu.VMEM((5, planes, side + 2 * PAD, width), F32),
        pltpu.VMEM((5, planes, side + 2 * PAD, width), F32),
    ]
    (
        marks, hats, cells, rows, cols, box, slope, spread, hat_x, hat_y,
        own, image, padded, down, across,
    ) = call(
        functools.partial(table_kernel, block_rows=block_rows),
        [
            ((8, width), F32),
            ((coarse * wide, width), F32),
            ((coarse * planes, width), F32),
            ((coarse_rows, side, width), F32),
            ((width, 2 * width), BF16),
            ((6 * width, 2 * width), BF16),
            ((width, width), BF16),
            ((width, coarse_rows * 3 * coarse * width), BF16),
            ((block_rows * coarse_rows, side, width), F32),
            ((width, width), BF16),
            ((5,) + field, F32),
            (field, F32),
            ((planes, side + 2 * PAD, width), F32),
            (field, F32),
            (field, F32),
        ],
        boxes,
        jnp.stack([block_place, tissue]), fixed, moving,
    )

    message = ((devices, 1, LANES), F32)

    half_boxes = [
        pltpu.VMEM((REACH * side, 2 * width), BF16),
        pltpu.VMEM((3 * REACH // 2 * side, 4 * width), BF16),
        pltpu.VMEM((5, REACH, side + 2 * PAD, width), F32),
        pltpu.VMEM((5, REACH, side + 2 * PAD, width), F32),
    ]
    (total,) = call(near_kernel, [((5,) + field, F32)], half_boxes, near, box, own)
    sent, mean, variance, halves = call(
        first_kernel,
        [message, (field, F32), (field, F32), ((2,) + halo[0], BF16)],
        [pltpu.VMEM((5,) + field, F32)] + half_boxes,
        image, padded, down, across, near, far, marks, cells, rows, cols, box, total,
    )
    received = lax.all_to_all(sent, ("blk", "gz"), 0, 0).reshape(devices, LANES)
    sent, correlation, velocity = call(
        second_kernel,
        [message, (field, F32), ((8 * block_rows * coarse_rows, LANES), F32)],
        [
            pltpu.VMEM((2, REACH, side, width), F32),
            pltpu.VMEM((2, REACH + 1, side + 2 * PAD, width), F32),
            pltpu.VMEM((2, REACH, side, width), F32),
            pltpu.VMEM((2, wide, side, width), F32),
            pltpu.VMEM((3, coarse, side, width), F32),
            pltpu.VMEM((wide, side + 2 * PAD, width), F32),
            pltpu.VMEM((3, planes, side + 2 * PAD, width), F32),
            pltpu.VMEM((3, planes, side + 2 * PAD, width), F32),
            pltpu.VMEM((3 * planes * side // 2, 6 * width), BF16),
        ],
        received, halves, image, padded, down, across, marks,
        mean, variance, hats, cells, rows, cols, box, slope,
        spread, hat_x, hat_y,
    )
    received = lax.all_to_all(sent, ("blk", "gz"), 0, 0).reshape(devices, LANES)
    grid = (3, coarse, block_rows * coarse_rows, GY * coarse_cols)
    return tuple(
        call(
            last_kernel,
            [(grid, F32), ((slots,) + field, F32)],
            [pltpu.VMEM(grid, F32), pltpu.SemaphoreType.DMA((2,))],
            received, velocity, spread, correlation,
            out_specs=[HBM, HBM],
        )
    )


def solution(mesh):
    return jax.shard_map(
        per_device,
        mesh=mesh,
        in_specs=(P("blk", "gz", None, None), P("blk", "gz", None, None), P("blk"), P("blk")),
        out_specs=(P(), P("blk", "gz", None, None)),
        check_vma=False,
    )
```

```python
import functools
import math

import jax
import jax.numpy as jnp
from jax import lax
from jax.experimental import pallas as pl
from jax.experimental.pallas import tpu as pltpu
from jax.sharding import PartitionSpec as P

SCALE = 16
GY = 8
EPSILON = 1e-05
STEP_LENGTH = 0.5
GAUSS_RAW = [math.exp(-((offset - 3) ** 2) / 4.5) for offset in range(7)]
GAUSS_TAPS = [value / sum(GAUSS_RAW) for value in GAUSS_RAW]
REACH = 4
PAD = 8
LANES = 128
F32 = jnp.float32
BF16 = jnp.bfloat16


def cell_weights(index, cell):
    total = jnp.zeros(index.shape, F32)
    for offset, weight in enumerate(GAUSS_TAPS):
        target = index + (offset - 3)
        inside = (target >= cell * SCALE) & (target < cell * SCALE + SCALE)
        total = total + jnp.where(inside, weight, 0.0)
    return total


def hat(index, cell, count):
    where = jnp.clip((index.astype(F32) + 0.5) * (1.0 / SCALE) - 0.5, 0.0, count - 1.0)
    return jnp.maximum(0.0, 1.0 - jnp.abs(where - cell.astype(F32)))


def lane_index(shape):
    return lax.broadcasted_iota(jnp.int32, shape, len(shape) - 1)


def sublane_index(shape):
    return lax.broadcasted_iota(jnp.int32, shape, len(shape) - 2)


def split(value, count):
    parts = []
    for _ in range(count):
        parts.append(value.astype(BF16))
        value = value - parts[-1].astype(F32)
    return parts


def close_dot(value, table):
    rows = value.shape[0]
    product = jnp.dot(
        jnp.concatenate(split(value, 2), axis=0), table, preferred_element_type=F32
    )
    return product[:rows] + product[rows:]


def window_of_nine(items):
    two = [a + b for a, b in zip(items[:-1], items[1:])]
    four = [a + b for a, b in zip(two[:-2], two[2:])]
    eight = [a + b for a, b in zip(four[:-4], four[4:])]
    return [a + b for a, b in zip(eight[:-1], items[8:])]


def padded_rows(side):
    return slice(PAD, PAD + side)


def clear_edges(ref, side):
    edge = jnp.zeros(ref.shape[:-2] + (PAD, LANES), F32)
    ref[..., 0:PAD, :] = edge
    ref[..., PAD + side :, :] = edge


def row_box(value, padded, three):
    side = value.shape[0]
    rows = padded_rows(side)
    middle = padded[PAD - 1 : PAD - 1 + side] + value + padded[PAD + 1 : PAD + 1 + side]
    three[0:PAD] = padded[1 : PAD + 1]
    three[rows] = middle
    three[PAD + side :] = padded[PAD + side - 1 : 2 * PAD + side - 1]
    return three[PAD - 3 : PAD - 3 + side] + middle + three[PAD + 3 : PAD + 3 + side]


def row_difference(padded, side):
    return padded[PAD + 1 : PAD + 1 + side] - padded[PAD - 1 : PAD - 1 + side]


def col_difference(plane):
    width = plane.shape[1]
    lane = lane_index(plane.shape)
    upper = jnp.where(lane < width - 1, pltpu.roll(plane, width - 1, 1), 0.0)
    lower = jnp.where(lane > 0, pltpu.roll(plane, 1, 1), 0.0)
    return upper - lower


def box_sums(fields, planes, side, sums, threes, parts, box_ref):
    half = planes // 2
    count = sums.shape[0]
    clear_edges(sums, side)
    for tile in range(side // 8):
        for f, items in enumerate(fields(8 * tile)):
            for z, item in enumerate(window_of_nine(items)):
                sums[f, z, PAD + 8 * tile : PAD + 8 * tile + 8] = item
    step = half // 4
    results = []
    for first in range(0, half, step):
        for i in range(first, first + step):
            for f in range(count):
                start = (i * count + f) * side
                for h in range(2):
                    z = i + h * half
                    total = row_box(sums[f, z, padded_rows(side)], sums.at[f, z], threes.at[f, z])
                    for part, rounded in enumerate(split(total, 3)):
                        lane = (2 * part + h) * LANES
                        parts[start : start + side, lane : lane + LANES] = rounded
        used = slice(first * count * side, (first + step) * count * side)
        results.append(jnp.dot(parts[used], box_ref[...], preferred_element_type=F32))

    def of(f, z):
        i, lane = z % half, (z // half) * LANES
        start = ((i % step) * count + f) * side
        return results[i // step][start : start + side, lane : lane + LANES]

    return of


def column_boxes(fixed, moving, side, pairs, single, double, box_ref):
    step = pairs
    results = []
    for first in range(0, pairs, step):
        for i in range(first, first + step):
            for h in range(2):
                lane = h * LANES
                planes = (fixed(i, h), moving(i, h))
                for f, plane in enumerate(planes):
                    start = (2 * i + f) * side
                    single[start : start + side, lane : lane + LANES] = plane
                a, b = (plane.astype(F32) for plane in planes)
                for f, product in enumerate((a * a, b * b, a * b)):
                    start = (3 * i + f) * side
                    high, low = split(product, 2)
                    double[start : start + side, lane : lane + LANES] = high
                    double[start : start + side, 2 * LANES + lane : 3 * LANES + lane] = low
        ones = single[2 * first * side : 2 * (first + step) * side]
        twos = double[3 * first * side : 3 * (first + step) * side]
        results.append(
            (
                jnp.dot(ones, box_ref[0 : 2 * LANES], preferred_element_type=F32),
                jnp.dot(twos, box_ref[0 : 4 * LANES], preferred_element_type=F32),
            )
        )

    def of(f, i, h):
        source, count, f = (0, 2, f) if f < 2 else (1, 3, f - 2)
        start = ((i % step) * count + f) * side
        return results[i // step][source][start : start + side, h * LANES : (h + 1) * LANES]

    return of


def running(items):
    total = [items[0]]
    for item in items[1:]:
        total.append(total[-1] + item)
    return total


def force_message(weights, slopes, planes, cells_ref, rows_ref, cols_ref, marks_ref):
    coarse = cells_ref.shape[0] // planes
    coarse_rows, side, _ = rows_ref.shape
    total = [[None] * coarse for _ in range(3)]
    for z in range(planes):
        directions = slopes(z)
        weight = weights(z)
        for k in range(coarse):
            index = k * planes + z
            share = weight * cells_ref[index : index + 1, :]
            for c in range(3):
                term = share * directions[c]
                total[c][k] = term if z == 0 else total[c][k] + term
    tiles = []
    for c in range(3):
        for k in range(coarse):
            for a in range(coarse_rows):
                product = total[c][k] * rows_ref[a]
                tile = product[0:8]
                for start in range(8, side, 8):
                    tile = tile + product[start : start + 8]
                tiles.append(tile)
    sums = close_dot(jnp.concatenate(tiles, axis=0), cols_ref[...])
    sums = sums[:, :LANES] + sums[:, LANES:]
    coarse_cols = LANES // SCALE
    lane = lane_index((8, LANES))
    picked = jnp.zeros((8, LANES), F32)
    for g in range(len(tiles)):
        picked = jnp.where(lane // coarse_cols == g, sums[8 * g : 8 * g + 8], picked)
    row = jnp.sum(picked, axis=0, keepdims=True) * marks_ref[1:2]
    return jnp.where(lane[0:1] == len(tiles) * coarse_cols, marks_ref[0:1], row)


def regular_grid(received, spread_ref, coarse, block_rows, coarse_rows, coarse_cols):
    groups = 3 * coarse
    used = groups * coarse_rows * coarse_cols
    width = GY * coarse_cols
    place = received[:, used : used + 1].astype(jnp.int32)
    here = (place % GY) == lane_index(received.shape) // coarse_cols
    block_row = place // GY
    sub = sublane_index((8, LANES))
    entries = close_dot(received, spread_ref[...])
    grids = []
    for r in range(block_rows):
        chosen = here if block_rows == 1 else here & (block_row == r)
        for a in range(coarse_rows):
            grid = jnp.zeros((8, LANES), F32)
            for g in range(groups):
                start = (a * groups + g) * LANES
                entry = jnp.where(chosen, entries[:, start : start + LANES], 0.0)
                grid = jnp.where(sub == g, jnp.sum(entry, axis=0, keepdims=True), grid)
            grids.append(grid)
    none = [jnp.zeros((8, LANES), F32)]
    grids = [
        0.5 * g + 0.25 * (before + after)
        for g, before, after in zip(grids, none + grids[:-1], grids[1:] + none)
    ]
    before_columns = grids
    inside = lane_index((8, LANES)) < width
    grids = [
        jnp.where(
            inside, 0.5 * g + 0.25 * (pltpu.roll(g, 1, 1) + pltpu.roll(g, LANES - 1, 1)), 0.0
        )
        for g in grids
    ]
    square = functools.reduce(lambda a, b: a + b, [g * g for g in grids])
    square = jnp.sum(jnp.sum(square, axis=0, keepdims=True), axis=1, keepdims=True)
    mean = square * (1.0 / (groups * len(grids) * width))
    return before_columns, grids, STEP_LENGTH / jnp.sqrt(mean + EPSILON)


def pack_kernel(fixed_hbm, moving_hbm, near_ref, far_ref, fixed_ref, moving_ref, sems):
    copies = [
        pltpu.make_async_copy(source.at[0], target, sems.at[i])
        for i, (source, target) in enumerate(((fixed_hbm, fixed_ref), (moving_hbm, moving_ref)))
    ]
    for copy in copies:
        copy.start()
    planes = fixed_ref.shape[0]
    part = lax.axis_index("gz")
    odd = part % 2
    inner = (part > 0) & (part < lax.axis_size("gz") - 1)
    for copy in copies:
        copy.wait()
    for ref, low in ((far_ref, odd == 0), (near_ref, odd == 1)):
        ref[0:REACH] = fixed_ref[pl.ds(jnp.where(low, 0, planes - REACH), REACH)]
        ref[REACH:] = moving_ref[pl.ds(jnp.where(low, 0, planes - REACH - 1), REACH + 1)]

    @pl.when(~inner)
    def _():
        far_ref[...] = jnp.zeros(far_ref.shape, BF16)


def table_kernel(
    both_ref, fixed_ref, moving_ref,
    marks_ref, hats_ref, cells_ref, rows_ref, cols_ref, box_ref, slope_ref, spread_ref, hat_x_ref, hat_y_ref,
    own_ref, image_ref, planes_ref, down_ref, across_ref,
    single, double, sums, threes,
    *, block_rows,
):
    planes = fixed_ref.shape[0]
    part = lax.axis_index("gz")
    total = planes * lax.axis_size("gz")
    coarse_rows, side, _ = rows_ref.shape
    coarse_cols = LANES // SCALE
    width = GY * coarse_cols
    wide = planes + 2 * REACH
    row = sublane_index(hats_ref.shape)
    z = part * planes + row % wide - REACH
    hats_ref[...] = jnp.where((z >= 0) & (z < total), hat(z, row // wide, total // SCALE), 0.0)
    row = sublane_index(cells_ref.shape)
    cells_ref[...] = cell_weights(part * planes + row % planes, row // planes)
    for a in range(coarse_rows):
        rows_ref[a] = cell_weights(sublane_index((side, LANES)), a)
    square = (LANES, LANES)
    cols = cell_weights(sublane_index(square), lane_index(square) % coarse_cols)
    for i, value in enumerate(split(cols, 2)):
        cols_ref[:, i * LANES : (i + 1) * LANES] = value
    apart = sublane_index(square) - lane_index(square)
    band = jnp.where(jnp.abs(apart) <= 4, 1.0, 0.0).astype(BF16)
    box_ref[...] = jnp.zeros(box_ref.shape, BF16)
    for i in range(6):
        lane = (i % 2) * LANES
        box_ref[i * LANES : (i + 1) * LANES, lane : lane + LANES] = band
    slope = jnp.where(apart == 1, 1.0, jnp.where(apart == -1, -1.0, 0.0)).astype(BF16)
    slope_ref[...] = slope
    across = jnp.dot(
        moving_ref[...].reshape(planes * side, LANES), slope, preferred_element_type=F32
    )
    across_ref[...] = across.reshape(across_ref.shape)
    image_ref[...] = fixed_ref[...].astype(F32)
    clear_edges(planes_ref, side)
    planes_ref[:, padded_rows(side)] = moving_ref[...].astype(F32)
    for z in range(planes):
        down_ref[z] = row_difference(planes_ref.at[z], side)
    lane = lane_index(square)
    entry = sublane_index(square)
    coarse = total // SCALE
    group = coarse_rows * coarse_cols
    for a in range(coarse_rows):
        for c in range(3):
            for k in range(coarse):
                value = jnp.zeros(square, F32)
                for other, weight in ((k - 1, 0.25), (k, 0.5), (k + 1, 0.25)):
                    if 0 <= other < coarse:
                        start = (c * coarse + other) * group + a * coarse_cols
                        hit = (entry == start + lane % coarse_cols) & (lane < width)
                        value = jnp.where(hit, weight, value)
                start = ((a * 3 + c) * coarse + k) * LANES
                spread_ref[:, start : start + LANES] = value.astype(BF16)
    row = sublane_index(marks_ref.shape)
    marks_ref[...] = jnp.where(row == 0, both_ref[0:1, 0:1], both_ref[1:2, 0:1]).astype(F32)
    place = both_ref[0:1, 0:1]
    y = lane + (place % GY) * LANES
    hat_y = jnp.where(entry < width, hat(y, entry, width), 0.0)
    hat_y = 0.5 * hat_y + 0.25 * (pltpu.roll(hat_y, 1, 0) + pltpu.roll(hat_y, LANES - 1, 0))
    hat_y_ref[...] = jnp.where(entry < width, hat_y, 0.0).astype(BF16)
    x = sublane_index((side, LANES)) + (place // GY) * side
    for r in range(block_rows * coarse_rows):
        hat_x_ref[r] = 0.5 * hat(x, jnp.full((1, 1), r, jnp.int32), block_rows * coarse_rows)

    of = column_boxes(
        lambda i, h: fixed_ref[i + REACH * h],
        lambda i, h: moving_ref[i + REACH * h],
        side, REACH, single, double, box_ref,
    )
    clear_edges(sums, side)
    for f in range(5):
        boxed = [of(f, i, h) for h in range(2) for i in range(REACH)]
        up, down = running(boxed), running(boxed[::-1])[::-1]
        for z in range(planes):
            item = up[z + REACH] if z < REACH else down[z - REACH]
            sums[f, z, padded_rows(side)] = item
            own_ref[f, z] = row_box(item, sums.at[f, z], threes.at[f, z])


def add_side(planes_ref, below, box_ref, before_ref, after_ref, single, double, sums, threes):
    side = planes_ref.shape[1]

    def at(first, count, distance):
        return planes_ref[first + jnp.where(below, count - distance, distance - 1)]

    of = column_boxes(
        lambda i, h: at(0, REACH, 1 + i + 2 * h),
        lambda i, h: at(REACH, REACH + 1, 1 + i + 2 * h),
        side, REACH // 2, single, double, box_ref,
    )
    clear_edges(sums, side)
    for f in range(5):
        boxed = [of(f, d % 2, d // 2) for d in range(REACH)]
        for d, item in enumerate(running(boxed)):
            sums[f, d, padded_rows(side)] = item
            z = jnp.where(below, REACH - 1 - d, REACH + d)
            other = jnp.where(below, REACH + d, REACH - 1 - d)
            after_ref[f, z] = before_ref[f, z] + row_box(item, sums.at[f, d], threes.at[f, d])
            after_ref[f, other] = before_ref[f, other]


def near_kernel(near_ref, box_ref, own_ref, total_ref, *scratch):
    odd = lax.axis_index("gz") % 2 == 1
    add_side(near_ref, odd, box_ref, own_ref, total_ref, *scratch)


def first_kernel(
    image_ref, planes_ref, down_ref, across_ref, near_ref, far_ref, marks_ref,
    cells_ref, rows_ref, cols_ref, box_ref, near_total_ref,
    message_ref, mean_ref, variance_ref, halves,
    total_ref, *scratch,
):
    planes, side, _ = image_ref.shape
    rows = padded_rows(side)
    odd = lax.axis_index("gz") % 2 == 1
    add_side(far_ref, ~odd, box_ref, near_total_ref, total_ref, *scratch)
    below = jnp.where(odd, 0, 1)
    halves[below] = near_ref[...]
    halves[1 - below] = far_ref[...]

    def weight(z):
        mean_i, mean_w, mean_ii, mean_ww, mean_iw = [
            total_ref[f, z] * (1.0 / 729.0) for f in range(5)
        ]
        sii = mean_ii - mean_i * mean_i
        sww = mean_ww - mean_w * mean_w
        siw = mean_iw - mean_i * mean_w
        mean_ref[z] = mean_i
        variance_ref[z] = sii
        ratio = siw / (sii * sww + EPSILON)
        return ratio * (
            (image_ref[z] - mean_i) - siw / (sww + EPSILON) * (planes_ref[z, rows] - mean_w)
        )

    def plane(z):
        if z < 0:
            return halves[0, 2 * REACH + 1 + z].astype(F32)
        return planes_ref[z, rows] if z < planes else halves[1, REACH + z - planes].astype(F32)

    row = force_message(
        weight,
        lambda z: (plane(z + 1) - plane(z - 1), down_ref[z], across_ref[z]),
        planes, cells_ref, rows_ref, cols_ref, marks_ref,
    )
    message_ref[...] = jnp.broadcast_to(row[None], message_ref.shape)


def second_kernel(
    received_ref, halves, image_ref, planes_ref, down_ref, across_ref, marks_ref,
    mean_ref, variance_ref, hats_ref, cells_ref, rows_ref, cols_ref, box_ref, slope_ref,
    spread_ref, hat_x_ref, hat_y_ref,
    message_ref, map_ref, velocity_ref,
    images, outer, outer_across, slopes, shift_ref, warped, sums, threes, parts,
):
    planes, side, _ = mean_ref.shape
    wide = planes + 2 * REACH
    coarse_rows = rows_ref.shape[0]
    coarse_cols = LANES // SCALE
    block_rows = velocity_ref.shape[0] // 8 // coarse_rows
    coarse = hats_ref.shape[0] // wide
    rows = padded_rows(side)

    def image(z):
        if z < 0:
            return images.at[0, z + REACH]
        return image_ref.at[z] if z < planes else images.at[1, z - planes]

    def moving(z):
        if z < 0:
            return outer.at[0, z + REACH + 1]
        return planes_ref.at[z] if z < planes else outer.at[1, z - planes]

    before_columns, grids, factor = regular_grid(
        received_ref[...], spread_ref, coarse, block_rows, coarse_rows, coarse_cols
    )
    along = close_dot(jnp.concatenate(before_columns, axis=0), hat_y_ref[...]) * factor
    for r, grid in enumerate(grids):
        velocity_ref[8 * r : 8 * r + 8] = grid * factor
    shift = [[None] * coarse for _ in range(3)]
    for r in range(len(grids)):
        for c in range(3):
            for k in range(coarse):
                g = 8 * r + c * coarse + k
                term = hat_x_ref[r] * along[g : g + 1]
                shift[c][k] = term if r == 0 else shift[c][k] + term
    for c in range(3):
        for k in range(coarse):
            shift_ref[c, k] = shift[c][k] if k == 0 else shift[c][k] - shift[c][0]

    clear_edges(outer, side)
    for h in range(2):
        images[h] = halves[h, 0:REACH].astype(F32)
        outer[h, :, rows] = halves[h, REACH:].astype(F32)
        across = jnp.dot(
            halves[h, REACH + 1 - h : 2 * REACH + 1 - h].reshape(REACH * side, LANES),
            slope_ref[...],
            preferred_element_type=F32,
        )
        outer_across[h] = across.reshape(outer_across.shape[1:])
    for z in range(-REACH, planes + REACH):
        slope = moving(z + 1)[rows] - moving(z - 1)[rows]
        if not 0 <= z < planes:
            hats = [hats_ref[pl.ds(k * wide + z + REACH, 1), :] for k in range(coarse)]
            slope = slope * functools.reduce(lambda a, b: a + b, hats)
            slopes[1, z + REACH] = row_difference(moving(z), side)
        slopes[0, z + REACH] = slope

    @pl.when(lax.axis_index("gz") >= 0)
    def _():
        for z in range(-REACH, planes + REACH):
            hats = [hats_ref[pl.ds(k * wide + z + REACH, 1), :] for k in range(coarse)]
            if z < 0:
                down, across = slopes[1, z + REACH], outer_across[0, z + REACH]
            elif z < planes:
                down, across = down_ref[z], across_ref[z]
            else:
                down, across = slopes[1, z + REACH], outer_across[1, z - planes]
            plane = moving(z)[rows]
            for c, slope in enumerate((slopes[0, z + REACH], down, across)):
                u = shift_ref[c, 0]
                for k in range(1, coarse):
                    u = u + hats[k] * shift_ref[c, k]
                plane = plane + u * slope
            warped[z + REACH, rows] = plane
        clear_edges(warped, side)

        def fields(start):
            i = [image(z)[start : start + 8] for z in range(-REACH, planes + REACH)]
            w = [warped[z, PAD + start : PAD + start + 8] for z in range(wide)]
            return (w, [b * b for b in w], [a * b for a, b in zip(i, w)])

        of = box_sums(fields, planes, side, sums, threes, parts, box_ref)

        def weight(z):
            mean_w, mean_ww, mean_iw = [of(f, z) * (1.0 / 729.0) for f in range(3)]
            mean_i = mean_ref[z]
            sii = variance_ref[z]
            sww = mean_ww - mean_w * mean_w
            siw = mean_iw - mean_i * mean_w
            ratio = siw / (sii * sww + EPSILON)
            map_ref[z] = siw * ratio
            return ratio * (
                (image_ref[z] - mean_i)
                - siw / (sww + EPSILON) * (warped[z + REACH, rows] - mean_w)
            )

        row = force_message(
            weight,
            lambda z: (
                warped[z + REACH + 1, rows] - warped[z + REACH - 1, rows],
                row_difference(warped.at[z + REACH], side),
                col_difference(warped[z + REACH, rows]),
            ),
            planes, cells_ref, rows_ref, cols_ref, marks_ref,
        )
        message_ref[...] = jnp.broadcast_to(row[None], message_ref.shape)


def last_kernel(
    received_ref, velocity_ref, spread_ref, map_ref, out_hbm, map_hbm, out_ref, sems
):
    map_copy = pltpu.make_async_copy(map_ref, map_hbm.at[0], sems.at[0])
    map_copy.start()
    _, coarse, rows, width = out_ref.shape
    coarse_cols = width // GY
    coarse_rows = spread_ref.shape[1] // (3 * coarse * LANES)
    block_rows = rows // coarse_rows
    _, grids, factor = regular_grid(
        received_ref[...], spread_ref, coarse, block_rows, coarse_rows, coarse_cols
    )
    for r, grid in enumerate(grids):
        velocity = velocity_ref[8 * r : 8 * r + 8] + grid * factor
        for c in range(3):
            for k in range(coarse):
                g = c * coarse + k
                out_ref[c, k, r : r + 1, :] = velocity[g : g + 1, :width]
    out_copy = pltpu.make_async_copy(out_ref, out_hbm, sems.at[1])
    out_copy.start()
    map_copy.wait()
    out_copy.wait()


def far_pairs(blocks, parts):
    pairs = []
    for block in range(blocks):
        for part in range(1, parts - 1, 2):
            low, high = block * parts + part, block * parts + part + 1
            pairs += [(low, high), (high, low)]
        for part in (0, parts - 1):
            pairs.append((block * parts + part, (block ^ 1) * parts + part))
    return pairs


VMEM = pl.BlockSpec(memory_space=pltpu.VMEM)
HBM = pl.BlockSpec(memory_space=pl.ANY)


def call(kernel, outs, scratch, *operands, in_specs=None, out_specs=None):
    return pl.pallas_call(
        kernel,
        out_shape=[jax.ShapeDtypeStruct(shape, dtype) for shape, dtype in outs],
        in_specs=in_specs or [VMEM] * len(operands),
        out_specs=out_specs or [VMEM] * len(outs),
        scratch_shapes=scratch,
        compiler_params=pltpu.CompilerParams(vmem_limit_bytes=24 << 20),
    )(*operands)


def per_device(fixed, moving, block_place, tissue):
    slots, planes, side, width = fixed.shape
    assert slots == 1 and width == LANES and planes == 2 * REACH
    depth_parts = lax.axis_size("gz")
    devices = lax.axis_size("blk") * depth_parts
    blocks = slots * lax.axis_size("blk")
    coarse = planes * depth_parts // SCALE
    coarse_rows, coarse_cols = side // SCALE, width // SCALE
    block_rows = blocks // GY
    wide = planes + 2 * REACH
    field = (planes, side, width)
    halo = ((2 * REACH + 1, side, width), BF16)

    near, far, fixed, moving = call(
        pack_kernel,
        [halo, halo, (field, BF16), (field, BF16)],
        [pltpu.SemaphoreType.DMA((2,))],
        pltpu.with_memory_space_constraint(fixed, pltpu.HBM),
        pltpu.with_memory_space_constraint(moving, pltpu.HBM),
        in_specs=[HBM] * 2,
    )
    far = lax.ppermute(far, ("blk", "gz"), far_pairs(lax.axis_size("blk"), depth_parts))
    pairs = [(i, i + 1) for i in range(0, depth_parts, 2)]
    near = lax.ppermute(near, "gz", pairs + [(b, a) for a, b in pairs])
    boxes = [
        pltpu.VMEM((2 * REACH * side, 2 * width), BF16),
        pltpu.VMEM((3 * REACH * side, 4 * width), BF16),
        pltpu.VMEM((5, planes, side + 2 * PAD, width), F32),
        pltpu.VMEM((5, planes, side + 2 * PAD, width), F32),
    ]
    (
        marks, hats, cells, rows, cols, box, slope, spread, hat_x, hat_y,
        own, image, padded, down, across,
    ) = call(
        functools.partial(table_kernel, block_rows=block_rows),
        [
            ((8, width), F32),
            ((coarse * wide, width), F32),
            ((coarse * planes, width), F32),
            ((coarse_rows, side, width), F32),
            ((width, 2 * width), BF16),
            ((6 * width, 2 * width), BF16),
            ((width, width), BF16),
            ((width, coarse_rows * 3 * coarse * width), BF16),
            ((block_rows * coarse_rows, side, width), F32),
            ((width, width), BF16),
            ((5,) + field, F32),
            (field, F32),
            ((planes, side + 2 * PAD, width), F32),
            (field, F32),
            (field, F32),
        ],
        boxes,
        jnp.stack([block_place, tissue]), fixed, moving,
    )

    message = ((devices, 1, LANES), F32)

    half_boxes = [
        pltpu.VMEM((REACH * side, 2 * width), BF16),
        pltpu.VMEM((3 * REACH // 2 * side, 4 * width), BF16),
        pltpu.VMEM((5, REACH, side + 2 * PAD, width), F32),
        pltpu.VMEM((5, REACH, side + 2 * PAD, width), F32),
    ]
    (total,) = call(near_kernel, [((5,) + field, F32)], half_boxes, near, box, own)
    sent, mean, variance, halves = call(
        first_kernel,
        [message, (field, F32), (field, F32), ((2,) + halo[0], BF16)],
        [pltpu.VMEM((5,) + field, F32)] + half_boxes,
        image, padded, down, across, near, far, marks, cells, rows, cols, box, total,
    )
    received = lax.all_to_all(sent, ("blk", "gz"), 0, 0).reshape(devices, LANES)
    sent, correlation, velocity = call(
        second_kernel,
        [message, (field, F32), ((8 * block_rows * coarse_rows, LANES), F32)],
        [
            pltpu.VMEM((2, REACH, side, width), F32),
            pltpu.VMEM((2, REACH + 1, side + 2 * PAD, width), F32),
            pltpu.VMEM((2, REACH, side, width), F32),
            pltpu.VMEM((2, wide, side, width), F32),
            pltpu.VMEM((3, coarse, side, width), F32),
            pltpu.VMEM((wide, side + 2 * PAD, width), F32),
            pltpu.VMEM((3, planes, side + 2 * PAD, width), F32),
            pltpu.VMEM((3, planes, side + 2 * PAD, width), F32),
            pltpu.VMEM((3 * planes * side // 2, 6 * width), BF16),
        ],
        received, halves, image, padded, down, across, marks,
        mean, variance, hats, cells, rows, cols, box, slope,
        spread, hat_x, hat_y,
    )
    received = lax.all_to_all(sent, ("blk", "gz"), 0, 0).reshape(devices, LANES)
    grid = (3, coarse, block_rows * coarse_rows, GY * coarse_cols)
    return tuple(
        call(
            last_kernel,
            [(grid, F32), ((slots,) + field, F32)],
            [pltpu.VMEM(grid, F32), pltpu.SemaphoreType.DMA((2,))],
            received, velocity, spread, correlation,
            out_specs=[HBM, HBM],
        )
    )


def solution(mesh):
    return jax.shard_map(
        per_device,
        mesh=mesh,
        in_specs=(P("blk", "gz", None, None), P("blk", "gz", None, None), P("blk"), P("blk")),
        out_specs=(P(), P("blk", "gz", None, None)),
        check_vma=False,
    )
```
